32 devices in a mesh: dp: 4 (over y, x), row: 4 (over z), col: 2 (over core).
Axes of the slice: x: 2, y: 2, z: 4, core: 2. Of those that a mesh axis runs over, the one named last changes fastest.
Arguments:
- tokens: bfloat16 [16384, 768], P(('dp', 'row'), 'col'), may hold values from -6 to 6
- cotangent: bfloat16 [16384, 768], P(('dp', 'row'), 'col'), may hold values from -6 to 6
- qkv_weight: float32 [3, 768, 768], P(None, ('dp', 'row'), 'col'), may hold values from -0.3125 to 0.3125
- out_weight: float32 [768, 768], P('col', ('dp', 'row')), may hold values from -1.75 to 1.75
- up_weight: float32 [768, 3072], P(('dp', 'row'), 'col'), may hold values from -0.21875 to 0.21875
- down_weight: float32 [3072, 768], P('col', ('dp', 'row')), may hold values from -0.21875 to 0.21875
- query_bias: float32 [768], P('col'), may hold values from -3 to 3
- value_bias: float32 [768], P('col'), may hold values from -3 to 3
- out_bias: float32 [768], replicated, may hold values from -3 to 3
- up_bias: float32 [3072], P('col'), may hold values from -3 to 3
- down_bias: float32 [768], replicated, may hold values from -3 to 3
- first_gain: float32 [768], replicated, may hold values from 0.5 to 1.5
- first_shift: float32 [768], replicated, may hold values from -3 to 3
- second_gain: float32 [768], replicated, may hold values from 0.5 to 1.5
- second_shift: float32 [768], replicated, may hold values from -3 to 3
- head_gate: int32 [12], P('col'), may hold values from 0 to 1, as said below
- hidden_gate: int32 [768], replicated, may hold values 0 or 1
- intermediate_gate: int32 [3072], P('col'), may hold values 0 or 1
- attention_gate: int32 [16], P(('dp', 'row')), may hold values 0 or 1
- feedforward_gate: int32 [16], P(('dp', 'row')), may hold values 0 or 1
- prefix_length: int32 [16], P(('dp', 'row')), may hold values from 102 to 512
Outputs:
- layer_out: float32 [16384, 768], P(('dp', 'row'), 'col')
- grad_tokens: float32 [16384, 768], P(('dp', 'row'), 'col')
- grad_qkv: float32 [3, 768, 768], P(None, ('dp', 'row'), 'col')
- grad_out: float32 [768, 768], P('col', ('dp', 'row'))
- grad_up: float32 [768, 3072], P(('dp', 'row'), 'col')
- grad_down: float32 [3072, 768], P('col', ('dp', 'row'))
- grad_query_bias: float32 [768], P('col')
- grad_value_bias: float32 [768], P('col')
- grad_out_bias: float32 [768], replicated
- grad_up_bias: float32 [3072], P('col')
- grad_down_bias: float32 [768], replicated
- grad_first_gain: float32 [768], replicated
- grad_first_shift: float32 [768], replicated
- grad_second_gain: float32 [768], replicated
- grad_second_shift: float32 [768], replicated
- grad_head_gate: float32 [12], P('col')
- grad_hidden_gate: float32 [768], replicated
- grad_unit_gate: float32 [3072], P('col')
- grad_attention_gate: float32 [16], replicated
- grad_feedforward_gate: float32 [16], replicated
The draws below stay inside these ranges and needn't reach their ends.
Inputs may be any that keep to these rules, and one draw needn't show every extreme that they name: `head_gate`: 1 keeps a head, 0 removes it; exactly 3 heads are removed. `hidden_gate`: 1 keeps a feature on both branch outputs, 0 removes it. `intermediate_gate`: 1 keeps a hidden unit, 0 removes it. `attention_gate`: 1 keeps the sequence's attention sub-layer, 0 removes it. `feedforward_gate`: 1 keeps the sequence's feed-forward sub-layer, 0 removes it. `prefix_length`: positions below a sequence's prefix length see each other both ways.
All inputs are finite; a program needn't handle non-finite values. No bound on the sum of `intermediate_gate` or of `attention_gate` or of `feedforward_gate` on one device may be relied on, other than what follows from the above.
Results may differ from the reference program's by a relative error of at most 0.015.
The reference program's roundings to bfloat16 on the way count: a program that leaves them out, or rounds other values in their place, can miss the bound.
Values may be sent and summed in bfloat16 or wider, within the bound.
A program may use at most 128 MiB of HBM per device.

```python
import math
import jax
import jax.numpy as jnp
from jax import lax

D = 768
H = 12
DH = 64
FF = 3072
LEN = 1024
SEQS = 16
TOKENS = 16384


def draw_head_gate(key, part):
    order = jax.random.permutation(jax.random.fold_in(key, 17), H)
    return (order >= H // 4).astype(jnp.int32)


def plant(drawn, stream_key, low, largest):
    shape = drawn.shape
    place = [jax.random.randint(jax.random.fold_in(stream_key, axis), (), 0, shape[axis]) for axis in range(len(shape))]
    drawn = drawn.at[tuple(place)].set(low)
    longest = shape.index(max(shape))
    place[longest] = (place[longest] + 1) % shape[longest]
    return drawn.at[tuple(place)].set(largest)


def level_of(rng, shape, pieces, smallest, top_value):
    level, own = 1.0, jax.random.fold_in(rng, 6)
    for position, blocks in pieces:
        draws = jnp.exp(jax.random.uniform(jax.random.fold_in(own, position), (blocks,), jnp.float32, smallest / len(pieces), top_value / len(pieces)))
        level = level * jnp.repeat(draws, shape[position] // blocks).reshape([-1 if axis == position else 1 for axis in range(len(shape))])
    return level


def scatter_about(key, shape, scale, most, split=(), kind=jnp.bfloat16):
    entries = scale * jax.random.normal(key, shape, jnp.float32)
    if split:
        entries = entries * level_of(key, shape, split, -0.22, 0.18)
    return jnp.clip(entries, -most, most).astype(kind)


def setup_inputs(seed: int = 0) -> dict:
    splits = jax.random.split(jax.random.key(seed), 22)
    return {
        "tokens": scatter_about(splits[0], (TOKENS, D), 1.0, 6.0, ((0, 16), (1, 2))),
        "cotangent": scatter_about(splits[1], (TOKENS, D), 1.0, 6.0, ((0, 16), (1, 2))),
        "qkv_weight": scatter_about(splits[2], (3, D, D), (D // 2) ** -0.5, 0.3125, ((1, 16), (2, 2)), jnp.float32),
        "out_weight": scatter_about(splits[3], (D, D), (D // 64) ** -0.5, 1.75, ((0, 2), (1, 16)), jnp.float32),
        "up_weight": scatter_about(splits[4], (D, FF), D ** -0.5, 0.21875, ((0, 16), (1, 2)), jnp.float32),
        "down_weight": scatter_about(splits[5], (FF, D), (FF // 4) ** -0.5, 0.21875, ((0, 2), (1, 16)), jnp.float32),
        "query_bias": scatter_about(splits[6], (D,), 0.5, 3.0, ((0, 2),), jnp.float32),
        "value_bias": scatter_about(splits[7], (D,), 0.5, 3.0, ((0, 2),), jnp.float32),
        "out_bias": scatter_about(splits[8], (D,), 0.5, 3.0, (), jnp.float32),
        "up_bias": scatter_about(splits[9], (FF,), 0.5, 3.0, ((0, 2),), jnp.float32),
        "down_bias": scatter_about(splits[10], (D,), 0.5, 3.0, (), jnp.float32),
        "first_gain": jnp.clip(1.0 + 0.1 * jax.random.normal(splits[11], (D,), jnp.float32), 0.5, 1.5),
        "first_shift": scatter_about(splits[12], (D,), 0.5, 3.0, (), jnp.float32),
        "second_gain": jnp.clip(1.0 + 0.1 * jax.random.normal(splits[13], (D,), jnp.float32), 0.5, 1.5),
        "second_shift": scatter_about(splits[14], (D,), 0.5, 3.0, (), jnp.float32),
        "head_gate": draw_head_gate(jax.random.fold_in(splits[21], 71), 0),
        "hidden_gate": plant((jax.random.randint(splits[16], (D,), 0, 8) < 7).astype(jnp.int32), jax.random.fold_in(splits[16], 1), 0, 1),
        "intermediate_gate": plant((jax.random.randint(splits[17], (FF,), 0, 4) < 3).astype(jnp.int32), jax.random.fold_in(splits[17], 1), 0, 1),
        "attention_gate": plant((jax.random.randint(splits[18], (SEQS,), 0, 4) < 3).astype(jnp.int32), jax.random.fold_in(splits[18], 1), 0, 1),
        "feedforward_gate": plant((jax.random.randint(splits[19], (SEQS,), 0, 4) < 3).astype(jnp.int32), jax.random.fold_in(splits[19], 1), 0, 1),
        "prefix_length": plant(jax.random.randint(splits[20], (SEQS,), LEN // 10, LEN // 2 + 1), jax.random.fold_in(splits[20], 1), LEN // 10, (LEN // 2 + 1) - 1).astype(jnp.int32),
    }


@jax.custom_vjp
def low(v):
    return lax.optimization_barrier(v.astype(jnp.bfloat16)).astype(jnp.float32)

@jax.custom_vjp
def low_back(v):
    return v

def low_keep(v):
    return (low(v), None)

def low_pass(kept, grad):
    return (grad,)

def back_keep(v):
    return (v, None)

def back_low(kept, grad):
    return (low(grad),)
low.defvjp(low_keep, low_pass)
low_back.defvjp(back_keep, back_low)
masked_value = -1e+30
norm_eps = 1e-05

def matmul(left, right):
    return jnp.dot(left, right, precision=lax.Precision.HIGHEST, preferred_element_type=jnp.float32)

def layer_norm(values, scale_gain, shift_term):
    centre = lax.optimization_barrier(jnp.mean(values, axis=1, keepdims=True))
    centred = values - centre
    spread = lax.optimization_barrier(jnp.mean(centred * centred, axis=1, keepdims=True))
    return centred * lax.rsqrt(spread + norm_eps) * scale_gain + shift_term

def attend(element):
    query_seq, key_seq, value_seq, prefix_value = element
    positions = jnp.arange(LEN, dtype=jnp.int32)
    allowed = (positions[None, :] < prefix_value) | (positions[None, :] <= positions[:, None])
    scores = jnp.einsum('qhd,khd->hqk', query_seq, key_seq, precision=lax.Precision.HIGHEST) * DH ** (-0.5)
    scores = low_back(scores)
    scores = jnp.where(allowed[None], scores, masked_value)
    probs_low = low(jax.nn.softmax(scores, axis=2))
    return jnp.einsum('hqk,khd->qhd', probs_low, value_seq, precision=lax.Precision.HIGHEST)

def forward(weight_set, gate_set, seq_set, inputs, prefix_group):
    qkv_weight, out_weight, up_weight, down_weight, query_bias, value_bias, out_bias, up_bias, down_bias, first_gain, first_shift, second_gain, second_shift = weight_set
    head_mask, hidden_mask, unit_mask = gate_set
    attn_seq, dense_seq = seq_set
    seq_total = prefix_group.shape[0]
    qkv_low = low(qkv_weight)
    out_low = low(out_weight)
    up_low = low(up_weight)
    down_low = low(down_weight)
    query_rows = low(low_back(matmul(inputs, qkv_low[0]) + query_bias))
    key_rows = low(low_back(matmul(inputs, qkv_low[1])))
    value_rows = low(low_back(matmul(inputs, qkv_low[2]) + value_bias))
    head_shape = (seq_total, LEN, H, DH)
    context = lax.map(jax.checkpoint(attend), (query_rows.reshape(head_shape), key_rows.reshape(head_shape), value_rows.reshape(head_shape), prefix_group))
    gated_ctx = low(low_back(context * head_mask[None, None, :, None])).reshape(seq_total * LEN, D)
    attn_out = low_back(matmul(gated_ctx, out_low) + out_bias)
    attn_rows = jnp.repeat(attn_seq, LEN)[:, None]
    first_sum = inputs + attn_rows * hidden_mask * attn_out
    normed = layer_norm(first_sum, first_gain, first_shift)
    pre_act = low_back(matmul(low(normed), up_low) + up_bias)
    inner_act = low(low_back(jax.nn.gelu(pre_act, approximate=False) * unit_mask))
    dense_out = low_back(matmul(inner_act, down_low) + down_bias)
    dense_rows = jnp.repeat(dense_seq, LEN)[:, None]
    second_sum = normed + dense_rows * hidden_mask * dense_out
    return layer_norm(second_sum, second_gain, second_shift)

def reference(tokens, cotangent, qkv_weight, out_weight, up_weight, down_weight, query_bias, value_bias, out_bias, up_bias, down_bias, first_gain, first_shift, second_gain, second_shift, head_gate, hidden_gate, intermediate_gate, attention_gate, feedforward_gate, prefix_length):
    weights = (qkv_weight.astype(jnp.float32), out_weight.astype(jnp.float32), up_weight.astype(jnp.float32), down_weight.astype(jnp.float32), query_bias.astype(jnp.float32), value_bias.astype(jnp.float32), out_bias.astype(jnp.float32), up_bias.astype(jnp.float32), down_bias.astype(jnp.float32), first_gain.astype(jnp.float32), first_shift.astype(jnp.float32), second_gain.astype(jnp.float32), second_shift.astype(jnp.float32))
    shared_gates = (head_gate.astype(jnp.float32), hidden_gate.astype(jnp.float32), intermediate_gate.astype(jnp.float32))
    group_size = math.gcd(SEQS, max(1, 4096 // LEN))
    group_count = SEQS // group_size
    token_groups = tokens.astype(jnp.float32).reshape(group_count, group_size * LEN, D)
    grad_groups = cotangent.astype(jnp.float32).reshape(group_count, group_size * LEN, D)
    attn_groups = attention_gate.astype(jnp.float32).reshape(group_count, group_size)
    dense_groups = feedforward_gate.astype(jnp.float32).reshape(group_count, group_size)
    prefix_groups = prefix_length.astype(jnp.int32).reshape(group_count, group_size)

    def scan_step(running, element):
        token_group, grad_group, attn_group, dense_group, prefix_group = element

        def forward_group(weight_set, gate_set, seq_set, inputs):
            return forward(weight_set, gate_set, seq_set, inputs, prefix_group)
        result, pullback = jax.vjp(forward_group, weights, shared_gates, (attn_group, dense_group), token_group)
        grad_weights, grad_gates, grad_seq, grad_inputs = pullback(grad_group)
        running = jax.tree.map(jnp.add, running, (grad_weights, grad_gates))
        return (running, (result, grad_inputs, grad_seq[0], grad_seq[1]))
    initial = jax.tree.map(jnp.zeros_like, (weights, shared_gates))
    totals, stacked = lax.scan(scan_step, initial, (token_groups, grad_groups, attn_groups, dense_groups, prefix_groups))
    grad_weights, grad_gates = totals
    results, grad_inputs, grad_attn, grad_dense = stacked
    return (results.reshape(TOKENS, D), grad_inputs.reshape(TOKENS, D), grad_weights[0], grad_weights[1], grad_weights[2], grad_weights[3], grad_weights[4], grad_weights[5], grad_weights[6], grad_weights[7], grad_weights[8], grad_weights[9], grad_weights[10], grad_weights[11], grad_weights[12], grad_gates[0], grad_gates[1], grad_gates[2], grad_attn.reshape(SEQS), grad_dense.reshape(SEQS))
```

```python
from functools import partial
import math
from typing import NamedTuple

import jax
import jax.numpy as jnp
from jax import lax
from jax.experimental import pallas as pl
from jax.experimental.pallas import tpu as pltpu
from jax.sharding import PartitionSpec as P

masked_value = -1e30
norm_eps = 1e-05


def norm_forward(values, scale_gain, shift_term):
    centre = jnp.mean(values, axis=1, keepdims=True)
    centred = values - centre
    spread = jnp.mean(centred * centred, axis=1, keepdims=True)
    inverse = lax.rsqrt(spread + norm_eps)
    normed = centred * inverse
    return (normed * scale_gain + shift_term, normed, inverse)


def norm_backward(gradient, normed, inverse, scale_gain):
    scaled = gradient * scale_gain
    first_mean = jnp.mean(scaled, axis=1, keepdims=True)
    second_mean = jnp.mean(scaled * normed, axis=1, keepdims=True)
    return inverse * (scaled - first_mean - normed * second_mean)


def block_mask(start_row, block_rows, length, prefix_value):
    key_index = jnp.arange(length, dtype=jnp.int32)
    query_index = start_row + jnp.arange(block_rows, dtype=jnp.int32)
    return (key_index[None, :] < prefix_value) | (key_index[None, :] <= query_index[:, None])


def block_scores(query_block, key_seq, start_row, prefix_value, scale_factor):
    block_rows = query_block.shape[0]
    length = key_seq.shape[0]
    allowed = block_mask(start_row, block_rows, length, prefix_value)
    scores = (
        jnp.einsum("qhd,khd->hqk", query_block, key_seq, preferred_element_type=jnp.float32)
        * scale_factor
    )
    return jnp.where(allowed[None], scores, masked_value)


def attend_sequence(query_seq, key_seq, value_seq, prefix_value, block_rows, scale_factor):
    length = key_seq.shape[0]
    block_count = length // block_rows
    query_blocks = query_seq.reshape(
        block_count, block_rows, query_seq.shape[1], query_seq.shape[2]
    )
    starts = jnp.arange(block_count, dtype=jnp.int32) * block_rows

    def one_block(element):
        query_block, start_row = element
        scores = block_scores(query_block, key_seq, start_row, prefix_value, scale_factor)
        row_peak = jnp.max(scores, axis=2, keepdims=True)
        exponent = jnp.exp(scores - row_peak)
        row_total = jnp.sum(exponent, axis=2, keepdims=True)
        weights_low = (exponent / row_total).astype(jnp.bfloat16)
        context = jnp.einsum(
            "hqk,khd->qhd", weights_low, value_seq, preferred_element_type=jnp.float32
        )
        return (context, row_peak[..., 0] + jnp.log(row_total[..., 0]))

    contexts, log_totals = lax.map(one_block, (query_blocks, starts))
    return (contexts.reshape(length, query_seq.shape[1], query_seq.shape[2]), log_totals)


def attend_back(
    query_seq, key_seq, value_seq, grad_seq, log_seq, prefix_value, block_rows, scale_factor
):
    length = key_seq.shape[0]
    block_count = length // block_rows
    head_count = query_seq.shape[1]
    head_size = query_seq.shape[2]
    query_blocks = query_seq.reshape(block_count, block_rows, head_count, head_size)
    grad_blocks = grad_seq.reshape(block_count, block_rows, head_count, head_size)
    starts = jnp.arange(block_count, dtype=jnp.int32) * block_rows

    def one_block(running, element):
        grad_keys, grad_values = running
        query_block, grad_block, log_block, start_row = element
        scores = block_scores(query_block, key_seq, start_row, prefix_value, scale_factor)
        probs = jnp.exp(scores - log_block[..., None])
        grad_probs = jnp.einsum(
            "qhd,khd->hqk", grad_block, value_seq, preferred_element_type=jnp.float32
        )
        row_inner = jnp.sum(probs * grad_probs, axis=2, keepdims=True)
        grad_scores = (probs * (grad_probs - row_inner)).astype(jnp.bfloat16)
        grad_query = (
            jnp.einsum("hqk,khd->qhd", grad_scores, key_seq, preferred_element_type=jnp.float32)
            * scale_factor
        )
        grad_keys = (
            grad_keys
            + jnp.einsum(
                "hqk,qhd->khd", grad_scores, query_block, preferred_element_type=jnp.float32
            )
            * scale_factor
        )
        grad_values = grad_values + jnp.einsum(
            "hqk,qhd->khd",
            probs.astype(jnp.bfloat16),
            grad_block,
            preferred_element_type=jnp.float32,
        )
        return ((grad_keys, grad_values), grad_query)

    zeros_kv = jnp.zeros((length, head_count, head_size), jnp.float32)
    (grad_keys, grad_values), grad_query = lax.scan(
        one_block, (zeros_kv, zeros_kv), (query_blocks, grad_blocks, log_seq, starts)
    )
    return (grad_query.reshape(length, head_count, head_size), grad_keys, grad_values)


def per_device(
    tokens,
    cotangent,
    qkv_weight,
    out_weight,
    up_weight,
    down_weight,
    query_bias,
    value_bias,
    out_bias,
    up_bias,
    down_bias,
    first_gain,
    first_shift,
    second_gain,
    second_shift,
    head_gate,
    hidden_gate,
    intermediate_gate,
    attention_gate,
    feedforward_gate,
    prefix_length,
):
    row_count = tokens.shape[0]
    seq_count = prefix_length.shape[0]
    length = row_count // seq_count
    local_heads = head_gate.shape[0]
    head_width = qkv_weight.shape[2]
    head_size = head_width // local_heads
    model_width = first_gain.shape[0]
    part_width = model_width // lax.axis_size("col")
    block_rows = min(512, length)
    scale_factor = head_size ** (-0.5)
    col_index = lax.axis_index("col")
    qkv_low, out_low = (
        lax.all_gather(qkv_weight.astype(jnp.bfloat16), ("dp", "row"), axis=1, tiled=True),
        lax.all_gather(out_weight.astype(jnp.bfloat16), ("dp", "row"), axis=1, tiled=True),
    )
    up_low, down_low = (
        lax.all_gather(up_weight.astype(jnp.bfloat16), ("dp", "row"), axis=0, tiled=True),
        lax.all_gather(down_weight.astype(jnp.bfloat16), ("dp", "row"), axis=1, tiled=True),
    )
    token_full = lax.all_gather(tokens, "col", axis=1, tiled=True)
    projected = jnp.einsum("td,kdf->ktf", token_full, qkv_low, preferred_element_type=jnp.float32)
    query_low = (projected[0] + query_bias).astype(jnp.bfloat16)
    key_low = projected[1].astype(jnp.bfloat16)
    value_low = (projected[2] + value_bias).astype(jnp.bfloat16)

    def split_heads(array):
        return array.reshape(seq_count, length, local_heads, head_size)

    def forward_seq(element):
        query_seq, key_seq, value_seq, prefix_value = element
        return attend_sequence(
            query_seq, key_seq, value_seq, prefix_value, block_rows, scale_factor
        )

    contexts, log_totals = lax.map(
        forward_seq,
        (split_heads(query_low), split_heads(key_low), split_heads(value_low), prefix_length),
    )
    context = contexts.reshape(row_count, head_width)
    gate_columns = jnp.repeat(head_gate.astype(jnp.float32), head_size)
    gated_low = (context * gate_columns).astype(jnp.bfloat16)
    attn_terms = jnp.dot(gated_low, out_low, preferred_element_type=jnp.float32)
    attn_out = lax.psum(attn_terms, "col") + out_bias
    hidden_mask = hidden_gate.astype(jnp.float32)
    attn_rows = jnp.repeat(attention_gate.astype(jnp.float32), length)[:, None]
    dense_rows = jnp.repeat(feedforward_gate.astype(jnp.float32), length)[:, None]
    first_sum = token_full.astype(jnp.float32) + attn_rows * hidden_mask * attn_out
    normed_one, first_normed, first_inverse = norm_forward(first_sum, first_gain, first_shift)
    normed_low = normed_one.astype(jnp.bfloat16)
    pre_act = jnp.dot(normed_low, up_low, preferred_element_type=jnp.float32) + up_bias
    activated, gelu_pull = jax.vjp(partial(jax.nn.gelu, approximate=False), pre_act)
    unit_mask = intermediate_gate.astype(jnp.float32)
    inner_low = (activated * unit_mask).astype(jnp.bfloat16)
    dense_terms = jnp.dot(inner_low, down_low, preferred_element_type=jnp.float32)
    dense_out = lax.psum(dense_terms, "col") + down_bias
    second_sum = normed_one + dense_rows * hidden_mask * dense_out
    layer_full, second_normed, second_inverse = norm_forward(second_sum, second_gain, second_shift)
    layer_out = lax.dynamic_slice_in_dim(layer_full, col_index * part_width, part_width, 1)
    grad_full = lax.all_gather(cotangent, "col", axis=1, tiled=True).astype(jnp.float32)
    grad_gain_two = jnp.sum(grad_full * second_normed, axis=0)
    grad_shift_two = jnp.sum(grad_full, axis=0)
    grad_second = norm_backward(grad_full, second_normed, second_inverse, second_gain)
    grad_dense_low = (dense_rows * hidden_mask * grad_second).astype(jnp.bfloat16)
    dense_product = dense_out * grad_second
    grad_dense_gate = jnp.sum(
        dense_product.reshape(seq_count, length, model_width) * hidden_mask, axis=(1, 2)
    )
    hidden_from_dense = jnp.sum(dense_rows * dense_product, axis=0)
    grad_down_bias = jnp.sum(grad_dense_low.astype(jnp.float32), axis=0)
    up_low, down_low = (
        lax.all_gather(up_weight.astype(jnp.bfloat16), ("dp", "row"), axis=0, tiled=True),
        lax.all_gather(down_weight.astype(jnp.bfloat16), ("dp", "row"), axis=1, tiled=True),
    )
    grad_down = jnp.einsum(
        "tf,td->fd", inner_low, grad_dense_low, preferred_element_type=jnp.float32
    )
    grad_inner_low = jnp.einsum(
        "td,fd->tf", grad_dense_low, down_low, preferred_element_type=jnp.float32
    ).astype(jnp.bfloat16)
    grad_inner = grad_inner_low.astype(jnp.float32)
    grad_unit_gate = jnp.sum(activated * grad_inner, axis=0)
    (grad_pre,) = gelu_pull(unit_mask * grad_inner)
    grad_pre_low = grad_pre.astype(jnp.bfloat16)
    grad_up_bias = jnp.sum(grad_pre_low.astype(jnp.float32), axis=0)
    grad_up = jnp.einsum("td,tf->df", normed_low, grad_pre_low, preferred_element_type=jnp.float32)
    dense_parts = (
        lax.psum_scatter(grad_up, ("dp", "row"), scatter_dimension=0, tiled=True),
        lax.psum_scatter(grad_down, ("dp", "row"), scatter_dimension=1, tiled=True),
    )
    hidden_terms = jnp.einsum("tf,df->td", grad_pre_low, up_low, preferred_element_type=jnp.float32)
    grad_normed = grad_second + lax.psum(hidden_terms, "col")
    grad_gain_one = jnp.sum(grad_normed * first_normed, axis=0)
    grad_shift_one = jnp.sum(grad_normed, axis=0)
    grad_first = norm_backward(grad_normed, first_normed, first_inverse, first_gain)
    grad_attn_low = (attn_rows * hidden_mask * grad_first).astype(jnp.bfloat16)
    attn_product = attn_out * grad_first
    grad_attn_gate = jnp.sum(
        attn_product.reshape(seq_count, length, model_width) * hidden_mask, axis=(1, 2)
    )
    grad_hidden = hidden_from_dense + jnp.sum(attn_rows * attn_product, axis=0)
    grad_out_bias = jnp.sum(grad_attn_low.astype(jnp.float32), axis=0)
    qkv_low, out_low = (
        lax.all_gather(qkv_weight.astype(jnp.bfloat16), ("dp", "row"), axis=1, tiled=True),
        lax.all_gather(out_weight.astype(jnp.bfloat16), ("dp", "row"), axis=1, tiled=True),
    )
    grad_out = jnp.einsum("tc,td->cd", gated_low, grad_attn_low, preferred_element_type=jnp.float32)
    grad_gated_low = jnp.einsum(
        "td,cd->tc", grad_attn_low, out_low, preferred_element_type=jnp.float32
    ).astype(jnp.bfloat16)
    grad_head_cols = jnp.sum(context * grad_gated_low.astype(jnp.float32), axis=0)
    grad_head = jnp.sum(grad_head_cols.reshape(local_heads, head_size), axis=1)
    grad_context = grad_gated_low * gate_columns.astype(jnp.bfloat16)

    def backward_seq(element):
        query_seq, key_seq, value_seq, grad_seq, log_seq, prefix_value = element
        return attend_back(
            query_seq, key_seq, value_seq, grad_seq, log_seq, prefix_value, block_rows, scale_factor
        )

    grad_query, grad_keys, grad_values = lax.map(
        backward_seq,
        (
            split_heads(query_low),
            split_heads(key_low),
            split_heads(value_low),
            split_heads(grad_context),
            log_totals,
            prefix_length,
        ),
    )
    grad_qkv_low = jnp.stack([grad_query, grad_keys, grad_values]).reshape(3, row_count, head_width)
    grad_qkv_low = grad_qkv_low.astype(jnp.bfloat16)
    grad_query_bias = jnp.sum(grad_qkv_low[0].astype(jnp.float32), axis=0)
    grad_value_bias = jnp.sum(grad_qkv_low[2].astype(jnp.float32), axis=0)
    grad_qkv = jnp.einsum(
        "td,ktf->kdf", token_full, grad_qkv_low, preferred_element_type=jnp.float32
    )
    input_terms = jnp.einsum(
        "ktf,kdf->td", grad_qkv_low, qkv_low, preferred_element_type=jnp.float32
    )
    grad_tokens = lax.psum_scatter(
        input_terms.astype(jnp.bfloat16), "col", scatter_dimension=1, tiled=True
    ).astype(jnp.float32)
    grad_tokens = grad_tokens + lax.dynamic_slice_in_dim(
        grad_first, col_index * part_width, part_width, 1
    )
    grad_up_part, grad_down_part = dense_parts
    grad_qkv_part, grad_out_part = (
        lax.psum_scatter(grad_qkv, ("dp", "row"), scatter_dimension=1, tiled=True),
        lax.psum_scatter(grad_out, ("dp", "row"), scatter_dimension=1, tiled=True),
    )
    seq_total = seq_count * lax.axis_size(("dp", "row"))
    seq_start = lax.axis_index(("dp", "row")) * seq_count
    seq_stack = lax.dynamic_update_slice_in_dim(
        jnp.zeros((2, seq_total), jnp.float32),
        jnp.stack([grad_attn_gate, grad_dense_gate]),
        seq_start,
        1,
    )
    full_stack = jnp.stack(
        [
            grad_out_bias,
            grad_down_bias,
            grad_gain_one,
            grad_shift_one,
            grad_gain_two,
            grad_shift_two,
            grad_hidden,
        ]
    )
    half_stack = jnp.stack([grad_query_bias, grad_value_bias])
    unit_stack = jnp.stack([grad_up_bias, grad_unit_gate])
    full_sum, half_sum, unit_sum, head_sum, seq_sum = lax.psum(
        (full_stack, half_stack, unit_stack, grad_head, seq_stack), ("dp", "row")
    )
    return (
        layer_out,
        grad_tokens,
        grad_qkv_part,
        grad_out_part,
        grad_up_part,
        grad_down_part,
        half_sum[0],
        half_sum[1],
        full_sum[0],
        unit_sum[0],
        full_sum[1],
        full_sum[2],
        full_sum[3],
        full_sum[4],
        full_sum[5],
        head_sum,
        full_sum[6],
        unit_sum[1],
        seq_sum[0],
        seq_sum[1],
    )


low_type = jnp.bfloat16
wide = jnp.float32
mesh_ids = pl.DeviceIdType.MESH


def dot_nn(left, right):
    return jnp.dot(left, right, preferred_element_type=wide)


def dot_nt(left, right):
    return lax.dot_general(left, right, (((1,), (1,)), ((), ())), preferred_element_type=wide)


def rows_at(index, count):
    return pl.ds(pl.multiple_of(index * count, count), count)


def fold_rows(values):
    return jnp.sum(values.reshape(values.shape[0] // 8, 8, values.shape[1]), axis=0)


def norm_parts(values):
    centre = jnp.mean(values, axis=1, keepdims=True)
    centred = values - centre
    spread = jnp.mean(centred * centred, axis=1, keepdims=True)
    inverse = lax.rsqrt(spread + norm_eps)
    return centred * inverse, inverse


class Place:
    def __init__(self, row_size):
        self.dp, self.row, self.col = (lax.axis_index(name) for name in ("dp", "row", "col"))
        self.row_size = row_size
        self.x, self.y = lax.rem(self.dp, 2), self.dp // 2
        self.x_dp = self.y * 2 + (1 - self.x)
        self.y_dp = (1 - self.y) * 2 + self.x

    def x_mate(self):
        return {"dp": self.x_dp}

    def y_mate(self):
        return {"dp": self.y_dp}

    def row_mate(self, step):
        return {"row": lax.rem(self.row + step, self.row_size)}

    def col_mate(self):
        return {"col": 1 - self.col}

    def barrier(self):
        semaphore = pltpu.get_barrier_semaphore()
        mates = [self.x_mate(), self.y_mate(), self.col_mate()]
        mates += [self.row_mate(step) for step in range(1, self.row_size)]
        for mate in mates:
            pl.semaphore_signal(semaphore, inc=1, device_id=mate, device_id_type=mesh_ids)
        pl.semaphore_wait(semaphore, len(mates))


def send(source, target, semaphores, index, mate):
    sent, received = semaphores
    return pltpu.make_async_remote_copy(
        src_ref=source,
        dst_ref=target,
        send_sem=sent.at[index],
        recv_sem=received.at[index],
        device_id=mate,
        device_id_type=mesh_ids,
    )


class Gather:
    def __init__(self, place, shards, chunks, own_sem, z_sems, two_sems, three_sems):
        self.place, self.shards, self.chunks = place, shards, chunks
        self.own_sem, self.z_sems, self.two_sems, self.three_sems = own_sem, z_sems, two_sems, three_sems
        count = len(chunks)
        self.own, self.z, self.two, self.three = ([None] * count for _ in range(4))
        self.part = shards[0].shape[0]
        self.block = self.part * place.row_size
        self.half = self.block // 2
        self.steps, self.done = [], 0
        for t in range(count + 2):
            for stage in range(3):
                if 0 <= t - stage < count:
                    self.steps.append((stage, t - stage))

    def half_rows(self, dp, half):
        return pl.ds(pl.multiple_of(dp * self.block + half * self.half, 16), self.half)

    def start(self):
        place = self.place
        own = pl.ds(pl.multiple_of(place.dp * self.block + place.row * self.part, 16), self.part)
        for c, (shard, chunk) in enumerate(zip(self.shards, self.chunks)):
            self.own[c] = pltpu.make_async_copy(shard, chunk.at[own], self.own_sem.at[c])
            self.own[c].start()
            self.z[c] = [
                send(shard, chunk.at[own], self.z_sems, (c, step - 1), place.row_mate(step))
                for step in range(1, place.row_size)
            ]
            for copy in self.z[c]:
                copy.start()

    def step(self):
        stage, c = self.steps[self.done]
        self.done += 1
        place, chunk = self.place, self.chunks[c]

        def pass_on(dp, half, sems, index, mate):
            rows = self.half_rows(dp, half)
            copy = send(chunk.at[rows], chunk.at[rows], sems, (c, index), mate)
            copy.start()
            return copy

        if stage == 0:
            self.own[c].wait()
            for copy in self.z[c]:
                copy.wait_recv()
            self.two[c] = [
                pass_on(place.dp, 0, self.two_sems, 0, place.x_mate()),
                pass_on(place.dp, 1, self.two_sems, 1, place.y_mate()),
            ]
        elif stage == 1:
            for copy in self.two[c]:
                copy.wait_recv()
            self.three[c] = [
                pass_on(place.dp, 0, self.three_sems, 0, place.y_mate()),
                pass_on(place.x_dp, 0, self.three_sems, 1, place.y_mate()),
                pass_on(place.dp, 1, self.three_sems, 2, place.x_mate()),
                pass_on(place.y_dp, 1, self.three_sems, 3, place.x_mate()),
            ]
        else:
            for copy in self.three[c]:
                copy.wait_recv()

    def advance(self, count):
        for _ in range(count):
            if self.done < len(self.steps):
                self.step()

    def need(self, c):
        while self.done <= self.steps.index((2, c)):
            self.step()

    def finish(self):
        self.advance(len(self.steps))
        for c in range(len(self.chunks)):
            for copy in self.z[c] + self.two[c] + self.three[c]:
                copy.wait_send()


class Scatter:
    def __init__(self, place, chunks, outs, first, mid_send, mid, last_send, last, one_sems, two_sems, z_sems):
        self.place, self.chunks, self.outs = place, chunks, outs
        self.first, self.mid_send, self.mid, self.last_send, self.last = first, mid_send, mid, last_send, last
        self.one_sems, self.two_sems, self.z_sems = one_sems, two_sems, z_sems
        self.part = outs[0].shape[0]
        self.block = self.part * place.row_size
        self.half = self.block // 2
        self.count = len(chunks)
        self.one, self.two, self.z = ([None] * self.count for _ in range(3))
        self.steps, self.done, self.begun = [], 0, 0
        for t in range(self.count + 2):
            for stage in range(3):
                if 0 <= t - stage < self.count:
                    self.steps.append((stage, t - stage))

    def half_rows(self, dp, half):
        return pl.ds(pl.multiple_of(dp * self.block + half * self.half, 16), self.half)

    def begin(self):
        c = self.begun
        self.begun += 1
        place, chunk = self.place, self.chunks[c]
        self.one[c] = []
        for i in range(2):
            self.one[c].append(
                send(
                    chunk.at[self.half_rows((1 - place.y) * 2 + i, 0)],
                    self.first[c].at[0, i],
                    self.one_sems,
                    (c, i),
                    place.y_mate(),
                )
            )
            self.one[c].append(
                send(
                    chunk.at[self.half_rows(i * 2 + (1 - place.x), 1)],
                    self.first[c].at[1, i],
                    self.one_sems,
                    (c, 2 + i),
                    place.x_mate(),
                )
            )
        for copy in self.one[c]:
            copy.start()

    def step(self):
        stage, c = self.steps[self.done]
        self.done += 1
        place, chunk = self.place, self.chunks[c]
        first, mid_send, mid = self.first[c], self.mid_send[c], self.mid[c]
        last_send, last = self.last_send[c], self.last[c]
        if stage == 0:
            for copy in self.one[c]:
                copy.wait_recv()
            mid_send[0] = (
                chunk[self.half_rows(place.x_dp, 0), :].astype(wide) + first[0, 1 - place.x].astype(wide)
            ).astype(low_type)
            mid_send[1] = (
                chunk[self.half_rows(place.y_dp, 1), :].astype(wide) + first[1, 1 - place.y].astype(wide)
            ).astype(low_type)
            self.two[c] = [
                send(mid_send.at[0], mid.at[0], self.two_sems, (c, 0), place.x_mate()),
                send(mid_send.at[1], mid.at[1], self.two_sems, (c, 1), place.y_mate()),
            ]
            for copy in self.two[c]:
                copy.start()
        elif stage == 1:
            for copy in self.two[c]:
                copy.wait_recv()
            for half, slot in ((0, place.x), (1, place.y)):
                last_send[pl.ds(half * self.half, self.half), :] = (
                    chunk[self.half_rows(place.dp, half), :].astype(wide)
                    + first[half, slot].astype(wide)
                    + mid[half].astype(wide)
                ).astype(low_type)
            self.z[c] = []
            for step in range(1, place.row_size):
                mate = lax.rem(place.row + step, place.row_size)
                rows = pl.ds(pl.multiple_of(mate * self.part, 16), self.part)
                self.z[c].append(
                    send(last_send.at[rows], last.at[step - 1], self.z_sems, (c, step - 1), place.row_mate(step))
                )
            for copy in self.z[c]:
                copy.start()
        else:
            total = last_send[pl.ds(pl.multiple_of(place.row * self.part, 16), self.part), :].astype(wide)
            for step, copy in enumerate(self.z[c]):
                copy.wait_recv()
                total = total + last[step].astype(wide)
            self.outs[c][...] = total

    def advance(self, count):
        for _ in range(count):
            if self.done < len(self.steps) and self.steps[self.done][1] < self.begun:
                self.step()

    def finish(self):
        self.advance(len(self.steps))
        for c in range(self.count):
            for copy in self.one[c] + self.two[c] + self.z[c]:
                copy.wait_send()


def masked_tile(tile, query_start, key_start, prefix):
    key_index = key_start + lax.broadcasted_iota(jnp.int32, tile.shape, 0)
    query_index = query_start + lax.broadcasted_iota(jnp.int32, tile.shape, 1)
    return jnp.where((key_index < prefix) | (key_index <= query_index), tile, masked_value)


def key_tiles(block, rows, prefix_most):
    count = max((block + 1) * rows, prefix_most) // rows
    return [(tile, tile >= block) for tile in range(count)]


def forward_kernel(
    cut,
    token_part, cot_part, shards_a, shards_m, vec_d, vec_f, vec_h, scalars,
    wa_out, wm_out, token_out, token_t_out, qkv_out, lse_out, ctx_out, attn_out_out, normed_t_out,
    gelu_out, slope_out, layer_out, second_out, dense_out_low, dense_t_out, sums_out,
    wa, wm, token, token_t, qkv, lse, ctx, attn_out, normed_t, gelu, slope, layer, second, dense_low, dense_t,
    sums, cot, value_t, ctx_t, normed, normed_low, total, psend, precv, dsend, drecv,
    own_sem, z_s, z_r, two_s, two_r, three_s, three_r, col_s, col_r, half_sem, out_sem,
):
    length, width, heads, size = cut.length, cut.width, cut.heads, cut.size
    part, rows, fine = cut.part_width, cut.rows, cut.fine
    blocks = length // rows
    pair = 2 * size
    pairs = heads // 2
    place = Place(cut.row_size)
    place.barrier()
    prefix, attn_gate, dense_gate = scalars[0], scalars[1].astype(wide), scalars[2].astype(wide)
    mate = place.col_mate()
    own_cols = pl.ds(pl.multiple_of(place.col * part, 128), part)
    halves, crossed = [], []
    for i, (source, target) in enumerate(((token_part, token), (cot_part, cot))):
        halves.append(pltpu.make_async_copy(source, target.at[:, own_cols], half_sem.at[i]))
        crossed.append(send(source, target.at[:, own_cols], (col_s, col_r), i, mate))
        halves[i].start()
        crossed[i].start()
    chunks = [wa.at[i] for i in range(pairs + 1)] + [wm.at[i] for i in range(4)]
    shards = [shards_a.at[i] for i in range(pairs + 1)] + [shards_m.at[i] for i in range(4)]
    gather = Gather(place, shards, chunks, own_sem, (z_s, z_r), (two_s, two_r), (three_s, three_r))
    gather.start()
    outs = []

    def put(source, target):
        copy = pltpu.make_async_copy(source, target, out_sem.at[len(outs)])
        copy.start()
        outs.append(copy)

    sums[...] = jnp.zeros_like(sums)
    halves[0].wait()
    crossed[0].wait_recv()

    @pl.loop(0, blocks)
    def _(b):
        at = rows_at(b, rows)
        token_t[:, at] = token[at, :].T

    put(token, token_out)
    put(token_t, token_t_out)
    lane_head = lax.broadcasted_iota(jnp.int32, (1, pair), 1) // size
    for p in range(pairs):
        gather.need(p)
        query_bias = vec_d[7:8, p * pair : (p + 1) * pair]
        value_bias = vec_d[7:8, part + p * pair : part + (p + 1) * pair]
        bias = jnp.concatenate([query_bias, jnp.zeros_like(query_bias), value_bias], axis=1)

        @pl.loop(0, blocks)
        def _(b, p=p, bias=bias):
            at = rows_at(b, rows)
            made = dot_nn(token[at, :], wa[p]) + bias
            qkv[p, at, :] = made.astype(low_type)
            value_t[:, at] = made[:, 2 * pair :].T.astype(low_type)

        gather.advance(1)
        for h in range(2):
            own = jnp.where(lane_head == h, size ** (-0.5), 0.0).astype(low_type)
            for b in range(blocks):
                query = qkv[p, b * rows : (b + 1) * rows, :pair] * own
                tiles, masked = [], key_tiles(b, rows, cut.prefix_most)
                for tile, needs in masked:
                    score = dot_nt(qkv[p, tile * rows : (tile + 1) * rows, pair : 2 * pair], query)
                    tiles.append(masked_tile(score, b * rows, tile * rows, prefix) if needs else score)
                peak = tiles[0].max(axis=0, keepdims=True)
                for score in tiles[1:]:
                    peak = jnp.maximum(peak, score.max(axis=0, keepdims=True))
                row_total = jnp.zeros_like(peak)
                found = jnp.zeros((size, rows), wide)
                for (tile, _), score in zip(masked, tiles):
                    weight = jnp.exp(score - peak)
                    row_total = row_total + weight.sum(axis=0, keepdims=True)
                    found = found + dot_nn(
                        value_t[h * size : (h + 1) * size, tile * rows : (tile + 1) * rows],
                        weight.astype(low_type),
                    )
                ctx_t[h * size : (h + 1) * size, b * rows : (b + 1) * rows] = found / row_total
                lse[2 * p + h, :, b * rows : (b + 1) * rows] = peak + jnp.log(row_total)
                if b % 2:
                    gather.advance(1)

        @pl.loop(0, blocks)
        def _(b, p=p):
            at = rows_at(b, rows)
            ctx[at, p * pair : (p + 1) * pair] = ctx_t[:, at].T.astype(low_type)

    put(qkv, qkv_out)
    put(lse, lse_out)
    put(ctx, ctx_out)
    gather.need(pairs)
    put(wa, wa_out)
    gate_columns = vec_h[...].astype(low_type)

    def swap(source, target, start, b):
        at = pl.ds(b * rows, rows) if isinstance(b, int) else rows_at(b, rows)
        return send(source.at[at], target.at[at], (col_s, col_r), start + b, mate)

    @pl.loop(0, blocks)
    def _(b):
        at = rows_at(b, rows)
        psend[at, :] = dot_nt(ctx[at, :] * gate_columns, wa[pairs]).astype(low_type)
        swap(psend, precv, 2, b).start()

    gather.advance(1)
    hidden = vec_d[6:7, :]
    for b in range(blocks):
        swap(psend, precv, 2, b).wait_recv()

        @pl.loop(b * rows // fine, (b + 1) * rows // fine)
        def _(i):
            at = rows_at(i, fine)
            attn = psend[at, :].astype(wide) + precv[at, :].astype(wide) + vec_d[0:1, :]
            attn_out[at, :] = attn
            first, _ = norm_parts(token[at, :].astype(wide) + attn_gate * hidden * attn)
            out = first * vec_d[2:3, :] + vec_d[3:4, :]
            normed[at, :] = out
            normed_low[at, :] = out.astype(low_type)

    put(attn_out, attn_out_out)
    gather.advance(1)
    group = wm.shape[2]
    for j in range(2):
        gather.need(pairs + 1 + 2 * j)
        up_bias = vec_f[0:1, j * group : (j + 1) * group]
        unit_mask = vec_f[1:2, j * group : (j + 1) * group].astype(low_type)

        @pl.loop(0, blocks)
        def _(b, j=j, up_bias=up_bias):
            at = rows_at(b, rows)
            pre = dot_nn(normed_low[at, :], wm[2 * j]) + up_bias
            share = 0.5 * (1.0 + lax.erf(pre * (2.0 ** -0.5)))
            gelu[j, at, :] = (pre * share).astype(low_type)
            density = jnp.exp(-0.5 * pre * pre) * ((2.0 * math.pi) ** -0.5)
            slope[j, at, :] = (share + pre * density).astype(low_type)
            if j == 0:
                normed_t[:, at] = normed_low[at, :].T

        gather.need(pairs + 2 + 2 * j)

        @pl.loop(0, blocks)
        def _(b, j=j, unit_mask=unit_mask):
            at = rows_at(b, rows)
            made = dot_nt(gelu[j, at, :] * unit_mask, wm[2 * j + 1])
            if j == 0:
                total[at, :] = made
            else:
                dsend[at, :] = (total[at, :] + made).astype(low_type)
                swap(dsend, drecv, 2 + blocks, b).start()

    put(normed_t, normed_t_out)
    put(gelu, gelu_out)
    put(slope, slope_out)
    put(wm, wm_out)
    halves[1].wait()
    crossed[1].wait_recv()
    for b in range(blocks):
        swap(dsend, drecv, 2 + blocks, b).wait_recv()

        @pl.loop(b * rows // fine, (b + 1) * rows // fine)
        def _(i):
            at = rows_at(i, fine)
            dense = dsend[at, :].astype(wide) + drecv[at, :].astype(wide) + vec_d[1:2, :]
            last, inverse = norm_parts(normed[at, :] + dense_gate * hidden * dense)
            full = last * vec_d[4:5, :] + vec_d[5:6, :]
            layer[at, :] = jnp.where(place.col == 0, full[:, :part], full[:, part:])
            grad = cot[at, :].astype(wide)
            scaled = grad * vec_d[4:5, :]
            one = jnp.mean(scaled, axis=1, keepdims=True)
            two = jnp.mean(scaled * last, axis=1, keepdims=True)
            made = inverse * (scaled - one - last * two)
            second[at, :] = made
            gated = (dense_gate * hidden * made).astype(low_type)
            dense_low[at, :] = gated
            product = dense * made
            sums[0] += fold_rows(grad * last)
            sums[1] += fold_rows(grad)
            sums[2] += fold_rows(gated.astype(wide))
            sums[3] += fold_rows(product)

        at = pl.ds(b * rows, rows)
        dense_t[:, at] = dense_low[at, :].T

    put(layer, layer_out)
    put(second, second_out)
    put(dense_low, dense_out_low)
    put(dense_t, dense_t_out)
    put(sums, sums_out)
    gather.finish()
    for copy in crossed:
        copy.wait_send()
    for b in range(blocks):
        swap(psend, precv, 2, b).wait_send()
        swap(dsend, drecv, 2 + blocks, b).wait_send()
    for copy in outs:
        copy.wait()


def backward_kernel(
    cut,
    wa_in, wm_in, token_in, token_t_in, qkv_in, lse_in, ctx_in, attn_out_in, normed_t_in,
    gelu_in, slope_in, second_in, dense_low_in, dense_t_in, sums_in, vec_d, vec_f, vec_h, scalars,
    grad_token, small_out, *rest,
):
    length, width, heads, size = cut.length, cut.width, cut.heads, cut.size
    part, rows, fine = cut.part_width, cut.rows, cut.fine
    blocks = length // rows
    pair = 2 * size
    pairs = heads // 2
    count = pairs + 5
    rest = list(rest)

    def take(number):
        taken = rest[:number]
        del rest[:number]
        return taken

    grads = take(count)
    (wa, wm, token, token_t, qkv, lse, ctx, attn_out, normed_t, gelu, slope, second, dense_low, dense_t, sums) = take(15)
    (total, psend, precv, fsend, frecv, ctx_grad, triple, key_grad, value_grad, query_t, key_t) = take(11)
    (small, small_x, small_y, small_z, unit_sums, head_sums) = take(6)
    buffers, first, mid_send, mid, last_send, last = (take(count) for _ in range(6))
    (in_sem, one_s, one_r, two_s, two_r, z_s, z_r, col_s, col_r, small_s, small_r) = take(11)
    place = Place(cut.row_size)
    loads = {}
    for i, (name, source, target) in enumerate(
        (
            ("dense_low", dense_low_in, dense_low),
            ("wm", wm_in, wm),
            ("slope", slope_in, slope),
            ("gelu", gelu_in, gelu),
            ("dense_t", dense_t_in, dense_t),
            ("normed_t", normed_t_in, normed_t),
            ("sums", sums_in, sums),
            ("second", second_in, second),
            ("attn_out", attn_out_in, attn_out),
            ("token", token_in, token),
            ("wa", wa_in, wa),
            ("ctx", ctx_in, ctx),
            ("qkv", qkv_in, qkv),
            ("lse", lse_in, lse),
            ("token_t", token_t_in, token_t),
        )
    ):
        loads[name] = pltpu.make_async_copy(source, target, in_sem.at[i])
        loads[name].start()

    def load(*names):
        for name in names:
            loads[name].wait()

    place.barrier()
    prefix, attn_gate, dense_gate = scalars[0], scalars[1].astype(wide), scalars[2].astype(wide)
    mate = place.col_mate()
    scatter = Scatter(
        place, buffers, grads, first, mid_send, mid, last_send, last, (one_s, one_r), (two_s, two_r), (z_s, z_r)
    )
    unit_sums[...] = jnp.zeros_like(unit_sums)
    head_sums[...] = jnp.zeros_like(head_sums)
    group = wm.shape[2]

    def swap(source, target, start, b):
        at = pl.ds(b * rows, rows) if isinstance(b, int) else rows_at(b, rows)
        return send(source.at[at], target.at[at], (col_s, col_r), start + b, mate)

    def product(target, left, right, mask=None):
        @pl.loop(0, width // rows)
        def _(i):
            at = rows_at(i, rows)
            made = dot_nn(left[at, :], right[...])
            target[at, :] = (made if mask is None else made * mask).astype(low_type)

    load("dense_low", "wm", "slope", "gelu")
    for j in range(2):
        unit_mask = vec_f[1:2, j * group : (j + 1) * group]

        @pl.loop(0, blocks)
        def _(b, j=j, unit_mask=unit_mask):
            at = rows_at(b, rows)
            inner = dot_nn(dense_low[at, :], wm[2 * j + 1]).astype(low_type).astype(wide)
            unit_sums[2 + j] += fold_rows(gelu[j, at, :].astype(wide) * inner)
            pre = (unit_mask * inner * slope[j, at, :].astype(wide)).astype(low_type)
            slope[j, at, :] = pre
            unit_sums[j] += fold_rows(pre.astype(wide))
            made = dot_nt(pre, wm[2 * j])
            if j == 0:
                total[at, :] = made
            else:
                psend[at, :] = (total[at, :] + made).astype(low_type)
                swap(psend, precv, 0, b).start()

        if j == 0:
            load("dense_t")
        product(buffers[2 * j], dense_t, gelu.at[j], unit_mask)
        scatter.begin()
        if j == 0:
            load("normed_t")
        product(buffers[2 * j + 1], normed_t, slope.at[j])
        scatter.begin()

    load("sums", "second", "attn_out", "token")
    hidden = vec_d[6:7, :]
    scatter.advance(1)
    for b in range(blocks):
        swap(psend, precv, 0, b).wait_recv()

        @pl.loop(b * rows // fine, (b + 1) * rows // fine)
        def _(i):
            at = rows_at(i, fine)
            attn = attn_out[at, :]
            gate_row = attn_gate * hidden
            normed, inverse = norm_parts(token[at, :].astype(wide) + gate_row * attn)
            grad = second[at, :] + (psend[at, :].astype(wide) + precv[at, :].astype(wide))
            scaled = grad * vec_d[2:3, :]
            one = jnp.mean(scaled, axis=1, keepdims=True)
            two = jnp.mean(scaled * normed, axis=1, keepdims=True)
            made = inverse * (scaled - one - normed * two)
            second[at, :] = made
            gated = (gate_row * made).astype(low_type)
            dense_low[at, :] = gated
            sums[4] += fold_rows(grad * normed)
            sums[5] += fold_rows(grad)
            sums[6] += fold_rows(gated.astype(wide))
            sums[7] += fold_rows(attn * made)

        at = pl.ds(b * rows, rows)
        dense_t[:, at] = dense_low[at, :].T
        scatter.advance(1)

    load("wa", "ctx", "qkv", "lse", "token_t")
    gate_columns = vec_h[...]

    @pl.loop(0, blocks)
    def _(b):
        at = rows_at(b, rows)
        gated = dot_nn(dense_low[at, :], wa[pairs]).astype(low_type).astype(wide)
        seen = ctx[at, :].astype(wide)
        head_sums[...] += fold_rows(seen * gated)
        ctx_grad[at, :] = (gated * gate_columns).astype(low_type)
        ctx[at, :] = (seen * gate_columns).astype(low_type)

    product(buffers[4], dense_t, ctx)
    scatter.begin()
    lane_head = lax.broadcasted_iota(jnp.int32, (1, pair), 1) // size
    bias_sums = []
    for p in range(pairs):

        @pl.loop(0, blocks)
        def _(b, p=p):
            at = rows_at(b, rows)
            key_t[:, at] = qkv[p, at, pair : 2 * pair].astype(wide).T.astype(low_type)

        key_grad[...] = jnp.zeros_like(key_grad)
        value_grad[...] = jnp.zeros_like(value_grad)
        for h in range(2):
            own = jnp.where(lane_head == h, size ** (-0.5), 0.0).astype(low_type)
            one_head = jnp.where(lane_head == h, 1.0, 0.0).astype(low_type)
            for b in range(blocks):
                query = qkv[p, b * rows : (b + 1) * rows, :pair] * own
                context = ctx_grad[b * rows : (b + 1) * rows, p * pair : (p + 1) * pair] * one_head
                logs = lse[2 * p + h, :, b * rows : (b + 1) * rows]
                inner = jnp.zeros_like(logs)
                kept, masked = [], key_tiles(b, rows, cut.prefix_most)
                for tile, needs in masked:
                    score = dot_nt(qkv[p, tile * rows : (tile + 1) * rows, pair : 2 * pair], query)
                    score = masked_tile(score, b * rows, tile * rows, prefix) if needs else score
                    prob = jnp.exp(score - logs)
                    grad_prob = dot_nt(qkv[p, tile * rows : (tile + 1) * rows, 2 * pair :], context)
                    inner = inner + (prob * grad_prob).sum(axis=0, keepdims=True)
                    kept.append((prob, grad_prob))
                found = jnp.zeros((size, rows), wide)
                for (tile, _), (prob, grad_prob) in zip(masked, kept):
                    at = slice(tile * rows, (tile + 1) * rows)
                    grad_score = (prob * (grad_prob - inner)).astype(low_type)
                    value_grad[at, :] += dot_nn(prob.astype(low_type), context)
                    key_grad[at, :] += dot_nn(grad_score, query)
                    found = found + dot_nn(key_t[h * size : (h + 1) * size, at], grad_score)
                query_t[h * size : (h + 1) * size, b * rows : (b + 1) * rows] = found * size ** (-0.5)
                if b % 2:
                    scatter.advance(1)

        query_sum = jnp.zeros((8, pair), wide)
        value_sum = jnp.zeros((8, pair), wide)
        for b in range(blocks):
            at = pl.ds(b * rows, rows)
            query_low = query_t[:, at].T.astype(low_type)
            value_low = value_grad[at, :].astype(low_type)
            triple[at, :pair] = query_low
            triple[at, pair : 2 * pair] = key_grad[at, :].astype(low_type)
            triple[at, 2 * pair :] = value_low
            query_sum += fold_rows(query_low.astype(wide))
            value_sum += fold_rows(value_low.astype(wide))
        bias_sums.append((query_sum, value_sum))
        product(buffers[5 + p], token_t, triple)
        scatter.begin()
        scatter.advance(1)

        @pl.loop(0, blocks)
        def _(b, p=p):
            at = rows_at(b, rows)
            made = dot_nt(triple[at, :], wa[p])
            if p > 0:
                made = total[at, :] + made
            if p < pairs - 1:
                total[at, :] = made
            else:
                mine = jnp.where(place.col == 0, made[:, :part], made[:, part:])
                other = jnp.where(place.col == 0, made[:, part:], made[:, :part])
                kept = second[at, :]
                grad_token[at, :] = mine + jnp.where(place.col == 0, kept[:, :part], kept[:, part:])
                fsend[at, :] = other.astype(low_type)
                swap(fsend, frecv, blocks, b).start()

        if p < pairs - 1:
            scatter.advance(1)

    def whole(values):
        return jnp.sum(values, axis=0, keepdims=True)

    dense_col, attn_col = whole(sums[3]), whole(sums[7])
    seq_lane = lax.broadcasted_iota(jnp.int32, (1, width), 1)
    here = place.dp * place.row_size + place.row
    dense_all = jnp.sum(dense_col * hidden, axis=1, keepdims=True)
    attn_all = jnp.sum(attn_col * hidden, axis=1, keepdims=True)
    seq_row = jnp.where(seq_lane == here, attn_all, 0.0) + jnp.where(seq_lane == here + width // 2, dense_all, 0.0)
    small[0:1, :] = whole(sums[6])
    small[1:2, :] = whole(sums[2])
    small[2:3, :] = whole(sums[4])
    small[3:4, :] = whole(sums[5])
    small[4:5, :] = whole(sums[0])
    small[5:6, :] = whole(sums[1])
    small[6:7, :] = dense_gate * dense_col + attn_gate * attn_col
    small[7:8, :] = seq_row
    for j in range(4):
        small[8 + j : 9 + j, :] = whole(unit_sums[j])
    for p in range(pairs):
        small[12:13, p * pair : (p + 1) * pair] = whole(bias_sums[p][0])
        small[12:13, part + p * pair : part + (p + 1) * pair] = whole(bias_sums[p][1])
    small[13:14, :part] = whole(head_sums[...])
    small[13:14, part:] = jnp.zeros((1, part), wide)
    small[14:16, :] = jnp.zeros((2, width), wide)
    copy_x = send(small, small_x.at[0], (small_s, small_r), 0, place.x_mate())
    copy_x.start()
    scatter.advance(1)
    copy_x.wait_recv()
    small_x[1] = small[...] + small_x[0]
    copy_y = send(small_x.at[1], small_y.at[0], (small_s, small_r), 1, place.y_mate())
    copy_y.start()
    scatter.advance(1)
    copy_y.wait_recv()
    mine = small_x[1] + small_y[0]
    small_y[1] = mine
    small_z[place.row] = mine
    copies = [
        send(small_y.at[1], small_z.at[place.row], (small_s, small_r), 1 + step, place.row_mate(step))
        for step in range(1, cut.row_size)
    ]
    for copy in copies:
        copy.start()
    for b in range(blocks):
        swap(fsend, frecv, blocks, b).wait_recv()
        at = pl.ds(b * rows, rows)
        grad_token[at, :] += frecv[at, :].astype(wide)
    scatter.finish()
    for copy in copies:
        copy.wait_recv()
    result = small_z[0]
    for z in range(1, cut.row_size):
        result = result + small_z[z]
    small_out[...] = result
    for copy in [copy_x, copy_y] + copies:
        copy.wait_send()
    for b in range(blocks):
        swap(psend, precv, 0, b).wait_send()
        swap(fsend, frecv, blocks, b).wait_send()


class Cut(NamedTuple):
    length: int
    width: int
    part_width: int
    heads: int
    size: int
    units: int
    part: int
    row_size: int
    rows: int
    fine: int
    prefix_most: int


def any_spec():
    return pl.BlockSpec(memory_space=pl.ANY)


def vmem_spec():
    return pl.BlockSpec(memory_space=pltpu.VMEM)


def smem_spec():
    return pl.BlockSpec(memory_space=pltpu.SMEM)


def like(items):
    return [jax.ShapeDtypeStruct(shape, kind) for shape, kind in items]


def scratch(items):
    return [pltpu.VMEM(shape, kind) for shape, kind in items]


def dma(*shape):
    return pltpu.SemaphoreType.DMA(shape)


vmem_most = 67043328


def run_forward(cut, token_part, cot_part, shards_a, shards_m, vec_d, vec_f, vec_h, scalars):
    length, width, half = cut.length, cut.width, cut.part_width
    group = cut.units // 2
    chunks_a, chunks = cut.heads // 2 + 1, cut.heads // 2 + 5
    blocks = length // cut.rows
    kept = [
        ((chunks_a, width, half), low_type),
        ((4, width, group), low_type),
        ((length, width), low_type),
        ((width, length), low_type),
        ((cut.heads // 2, length, half), low_type),
        ((cut.heads, 1, length), wide),
        ((length, half), low_type),
        ((length, width), wide),
        ((width, length), low_type),
        ((2, length, group), low_type),
        ((2, length, group), low_type),
        ((length, half), wide),
        ((length, width), wide),
        ((length, width), low_type),
        ((width, length), low_type),
        ((8, 8, width), wide),
    ]
    own = [
        ((length, width), low_type),
        ((2 * cut.size, length), low_type),
        ((2 * cut.size, length), wide),
        ((length, width), wide),
        ((length, width), low_type),
        ((length, width), wide),
        ((length, width), low_type),
        ((length, width), low_type),
        ((length, width), low_type),
        ((length, width), low_type),
    ]
    z = cut.row_size - 1
    semaphores = [dma(chunks), dma(chunks, z), dma(chunks, z), dma(chunks, 2), dma(chunks, 2), dma(chunks, 4), dma(chunks, 4)]
    semaphores += [dma(2 + 2 * blocks), dma(2 + 2 * blocks), dma(2), dma(len(kept))]
    return pl.pallas_call(
        partial(forward_kernel, cut),
        out_shape=like(kept),
        in_specs=[any_spec()] * 2 + [vmem_spec()] * 5 + [smem_spec()],
        out_specs=[any_spec()] * len(kept),
        scratch_shapes=scratch(kept) + scratch(own) + semaphores,
        compiler_params=pltpu.CompilerParams(collective_id=0, has_side_effects=True, vmem_limit_bytes=vmem_most),
        name="layer_forward",
    )(token_part, cot_part, shards_a, shards_m, vec_d, vec_f, vec_h, scalars)


def run_backward(cut, kept, vec_d, vec_f, vec_h, scalars):
    length, width, half = cut.length, cut.width, cut.part_width
    group = cut.units // 2
    pairs = cut.heads // 2
    blocks = length // cut.rows
    columns = [group] * 4 + [half] * (pairs + 1)
    count = len(columns)
    outs = [((length, half), wide), ((16, width), wide)] + [((cut.part, n), wide) for n in columns]
    loaded = [(item.shape, item.dtype) for item in kept]
    own = [
        ((length, width), wide),
        ((length, width), low_type),
        ((length, width), low_type),
        ((length, half), low_type),
        ((length, half), low_type),
        ((length, half), low_type),
        ((length, half), low_type),
        ((length, 2 * cut.size), wide),
        ((length, 2 * cut.size), wide),
        ((2 * cut.size, length), wide),
        ((2 * cut.size, length), low_type),
        ((16, width), wide),
        ((2, 16, width), wide),
        ((2, 16, width), wide),
        ((cut.row_size, 16, width), wide),
        ((4, 8, width), wide),
        ((8, half), wide),
    ]
    quarter = cut.part * cut.row_size // 2
    own += [((width, n), low_type) for n in columns]
    own += [((2, 2, quarter, n), low_type) for n in columns]
    own += [((2, quarter, n), low_type) for n in columns]
    own += [((2, quarter, n), low_type) for n in columns]
    own += [((2 * quarter, n), low_type) for n in columns]
    own += [((cut.row_size - 1, cut.part, n), low_type) for n in columns]
    z = cut.row_size - 1
    semaphores = [dma(len(kept)), dma(count, 4), dma(count, 4), dma(count, 2), dma(count, 2), dma(count, z), dma(count, z)]
    semaphores += [dma(2 * blocks), dma(2 * blocks), dma(2 + z), dma(2 + z)]
    return pl.pallas_call(
        partial(backward_kernel, cut),
        out_shape=like(outs),
        in_specs=[any_spec()] * len(kept) + [vmem_spec()] * 3 + [smem_spec()],
        out_specs=[vmem_spec()] * len(outs),
        scratch_shapes=scratch(loaded) + scratch(own) + semaphores,
        compiler_params=pltpu.CompilerParams(collective_id=1, has_side_effects=True, vmem_limit_bytes=vmem_most),
        name="layer_backward",
    )(*kept, vec_d, vec_f, vec_h, scalars)


def fused_device(
    cut,
    tokens, cotangent, qkv_weight, out_weight, up_weight, down_weight, query_bias, value_bias, out_bias, up_bias,
    down_bias, first_gain, first_shift, second_gain, second_shift, head_gate, hidden_gate, intermediate_gate,
    attention_gate, feedforward_gate, prefix_length,
):
    pair, pairs, half = 2 * cut.size, cut.heads // 2, cut.part_width
    group = cut.units // 2
    qkv_low = qkv_weight.astype(low_type)
    out_low = out_weight.astype(low_type).T
    up_low = up_weight.astype(low_type)
    down_low = down_weight.astype(low_type).T
    shards_a = jnp.stack(
        [
            jnp.concatenate([qkv_low[k, :, p * pair : (p + 1) * pair] for k in range(3)], axis=1)
            for p in range(pairs)
        ]
        + [out_low]
    )
    shards_m = jnp.stack([up_low[:, :group], down_low[:, :group], up_low[:, group:], down_low[:, group:]])
    vec_d = jnp.stack(
        [
            out_bias, down_bias, first_gain, first_shift, second_gain, second_shift,
            hidden_gate.astype(wide), jnp.concatenate([query_bias, value_bias]),
        ]
    )
    vec_f = jnp.stack([up_bias, intermediate_gate.astype(wide)])
    vec_h = jnp.repeat(head_gate.astype(wide), cut.size)[None]
    scalars = jnp.concatenate([prefix_length, attention_gate, feedforward_gate])
    kept = list(run_forward(cut, tokens, cotangent, shards_a, shards_m, vec_d, vec_f, vec_h, scalars))
    layer_out = kept.pop(11)
    made = run_backward(cut, kept, vec_d, vec_f, vec_h, scalars)
    grad_tokens, small = made[0], made[1]
    down_0, up_0, down_1, up_1, grad_out = made[2:7]
    grad_qkv = jnp.stack(
        [jnp.concatenate([piece[:, k * pair : (k + 1) * pair] for piece in made[7:]], axis=1) for k in range(3)]
    )
    seq_total = lax.axis_size(("dp", "row"))
    return (
        layer_out,
        grad_tokens,
        grad_qkv,
        grad_out.T,
        jnp.concatenate([up_0, up_1], axis=1),
        jnp.concatenate([down_0, down_1], axis=1).T,
        small[12, :half],
        small[12, half:],
        small[0],
        small[8:10].reshape(-1),
        small[1],
        small[2],
        small[3],
        small[4],
        small[5],
        jnp.sum(small[13, :half].reshape(cut.heads, cut.size), axis=1),
        small[6],
        small[10:12].reshape(-1),
        small[7, :seq_total],
        small[7, cut.width // 2 : cut.width // 2 + seq_total],
    )


def cut_of(args):
    tokens, qkv_weight, up_weight, head_gate, prefix_length = args[0], args[2], args[4], args[15], args[20]
    length, part_width = tokens.shape
    part, width = qkv_weight.shape[1], args[11].shape[0]
    heads = head_gate.shape[0]
    row_size, dp_size = lax.axis_size("row"), lax.axis_size("dp")
    fits = (
        prefix_length.shape[0] == 1
        and lax.axis_size("col") == 2
        and dp_size == 4
        and row_size % 2 == 0
        and part % 16 == 0
        and heads % 2 == 0
        and part_width == qkv_weight.shape[2]
        and part_width == 3 * (2 * part_width // heads)
        and (2 * part_width // heads) % 128 == 0
        and width % 256 == 0
        and length % 512 == 0
        and up_weight.shape[1] == 2 * width
    )
    if not fits:
        return None
    return Cut(
        length, width, part_width, heads, part_width // heads, up_weight.shape[1], part, row_size, 256, 128, length // 2
    )


def any_device(*args):
    cut = cut_of(args)
    return per_device(*args) if cut is None else fused_device(cut, *args)


def solution(mesh):
    placed = (
        P(("dp", "row"), "col"),
        P(("dp", "row"), "col"),
        P(None, ("dp", "row"), "col"),
        P("col", ("dp", "row")),
        P(("dp", "row"), "col"),
        P("col", ("dp", "row")),
        P("col"),
        P("col"),
        P(),
        P("col"),
        P(),
        P(),
        P(),
        P(),
        P(),
        P("col"),
        P(),
        P("col"),
        P(("dp", "row")),
        P(("dp", "row")),
        P(("dp", "row")),
    )
    return jax.shard_map(
        any_device,
        mesh=mesh,
        in_specs=placed,
        out_specs=(
            P(("dp", "row"), "col"),
            P(("dp", "row"), "col"),
            P(None, ("dp", "row"), "col"),
            P("col", ("dp", "row")),
            P(("dp", "row"), "col"),
            P("col", ("dp", "row")),
            P("col"),
            P("col"),
            P(),
            P("col"),
            P(),
            P(),
            P(),
            P(),
            P(),
            P("col"),
            P(),
            P("col"),
            P(),
            P(),
        ),
        check_vma=False,
    )
```

```python
from functools import partial
import math
from typing import NamedTuple

import jax
import jax.numpy as jnp
from jax import lax
from jax.experimental import pallas as pl
from jax.experimental.pallas import tpu as pltpu
from jax.sharding import PartitionSpec as P

masked_value = -1e30
norm_eps = 1e-05


def norm_forward(values, scale_gain, shift_term):
    centre = jnp.mean(values, axis=1, keepdims=True)
    centred = values - centre
    spread = jnp.mean(centred * centred, axis=1, keepdims=True)
    inverse = lax.rsqrt(spread + norm_eps)
    normed = centred * inverse
    return (normed * scale_gain + shift_term, normed, inverse)


def norm_backward(gradient, normed, inverse, scale_gain):
    scaled = gradient * scale_gain
    first_mean = jnp.mean(scaled, axis=1, keepdims=True)
    second_mean = jnp.mean(scaled * normed, axis=1, keepdims=True)
    return inverse * (scaled - first_mean - normed * second_mean)


def block_mask(start_row, block_rows, length, prefix_value):
    key_index = jnp.arange(length, dtype=jnp.int32)
    query_index = start_row + jnp.arange(block_rows, dtype=jnp.int32)
    return (key_index[None, :] < prefix_value) | (key_index[None, :] <= query_index[:, None])


def block_scores(query_block, key_seq, start_row, prefix_value, scale_factor):
    block_rows = query_block.shape[0]
    length = key_seq.shape[0]
    allowed = block_mask(start_row, block_rows, length, prefix_value)
    scores = (
        jnp.einsum("qhd,khd->hqk", query_block, key_seq, preferred_element_type=jnp.float32)
        * scale_factor
    )
    return jnp.where(allowed[None], scores, masked_value)


def attend_sequence(query_seq, key_seq, value_seq, prefix_value, block_rows, scale_factor):
    length = key_seq.shape[0]
    block_count = length // block_rows
    query_blocks = query_seq.reshape(
        block_count, block_rows, query_seq.shape[1], query_seq.shape[2]
    )
    starts = jnp.arange(block_count, dtype=jnp.int32) * block_rows

    def one_block(element):
        query_block, start_row = element
        scores = block_scores(query_block, key_seq, start_row, prefix_value, scale_factor)
        row_peak = jnp.max(scores, axis=2, keepdims=True)
        exponent = jnp.exp(scores - row_peak)
        row_total = jnp.sum(exponent, axis=2, keepdims=True)
        weights_low = (exponent / row_total).astype(jnp.bfloat16)
        context = jnp.einsum(
            "hqk,khd->qhd", weights_low, value_seq, preferred_element_type=jnp.float32
        )
        return (context, row_peak[..., 0] + jnp.log(row_total[..., 0]))

    contexts, log_totals = lax.map(one_block, (query_blocks, starts))
    return (contexts.reshape(length, query_seq.shape[1], query_seq.shape[2]), log_totals)


def attend_back(
    query_seq, key_seq, value_seq, grad_seq, log_seq, prefix_value, block_rows, scale_factor
):
    length = key_seq.shape[0]
    block_count = length // block_rows
    head_count = query_seq.shape[1]
    head_size = query_seq.shape[2]
    query_blocks = query_seq.reshape(block_count, block_rows, head_count, head_size)
    grad_blocks = grad_seq.reshape(block_count, block_rows, head_count, head_size)
    starts = jnp.arange(block_count, dtype=jnp.int32) * block_rows

    def one_block(running, element):
        grad_keys, grad_values = running
        query_block, grad_block, log_block, start_row = element
        scores = block_scores(query_block, key_seq, start_row, prefix_value, scale_factor)
        probs = jnp.exp(scores - log_block[..., None])
        grad_probs = jnp.einsum(
            "qhd,khd->hqk", grad_block, value_seq, preferred_element_type=jnp.float32
        )
        row_inner = jnp.sum(probs * grad_probs, axis=2, keepdims=True)
        grad_scores = (probs * (grad_probs - row_inner)).astype(jnp.bfloat16)
        grad_query = (
            jnp.einsum("hqk,khd->qhd", grad_scores, key_seq, preferred_element_type=jnp.float32)
            * scale_factor
        )
        grad_keys = (
            grad_keys
            + jnp.einsum(
                "hqk,qhd->khd", grad_scores, query_block, preferred_element_type=jnp.float32
            )
            * scale_factor
        )
        grad_values = grad_values + jnp.einsum(
            "hqk,qhd->khd",
            probs.astype(jnp.bfloat16),
            grad_block,
            preferred_element_type=jnp.float32,
        )
        return ((grad_keys, grad_values), grad_query)

    zeros_kv = jnp.zeros((length, head_count, head_size), jnp.float32)
    (grad_keys, grad_values), grad_query = lax.scan(
        one_block, (zeros_kv, zeros_kv), (query_blocks, grad_blocks, log_seq, starts)
    )
    return (grad_query.reshape(length, head_count, head_size), grad_keys, grad_values)


def per_device(
    tokens,
    cotangent,
    qkv_weight,
    out_weight,
    up_weight,
    down_weight,
    query_bias,
    value_bias,
    out_bias,
    up_bias,
    down_bias,
    first_gain,
    first_shift,
    second_gain,
    second_shift,
    head_gate,
    hidden_gate,
    intermediate_gate,
    attention_gate,
    feedforward_gate,
    prefix_length,
):
    row_count = tokens.shape[0]
    seq_count = prefix_length.shape[0]
    length = row_count // seq_count
    local_heads = head_gate.shape[0]
    head_width = qkv_weight.shape[2]
    head_size = head_width // local_heads
    model_width = first_gain.shape[0]
    part_width = model_width // lax.axis_size("col")
    block_rows = min(512, length)
    scale_factor = head_size ** (-0.5)
    col_index = lax.axis_index("col")
    qkv_low, out_low = (
        lax.all_gather(qkv_weight.astype(jnp.bfloat16), ("dp", "row"), axis=1, tiled=True),
        lax.all_gather(out_weight.astype(jnp.bfloat16), ("dp", "row"), axis=1, tiled=True),
    )
    up_low, down_low = (
        lax.all_gather(up_weight.astype(jnp.bfloat16), ("dp", "row"), axis=0, tiled=True),
        lax.all_gather(down_weight.astype(jnp.bfloat16), ("dp", "row"), axis=1, tiled=True),
    )
    token_full = lax.all_gather(tokens, "col", axis=1, tiled=True)
    projected = jnp.einsum("td,kdf->ktf", token_full, qkv_low, preferred_element_type=jnp.float32)
    query_low = (projected[0] + query_bias).astype(jnp.bfloat16)
    key_low = projected[1].astype(jnp.bfloat16)
    value_low = (projected[2] + value_bias).astype(jnp.bfloat16)

    def split_heads(array):
        return array.reshape(seq_count, length, local_heads, head_size)

    def forward_seq(element):
        query_seq, key_seq, value_seq, prefix_value = element
        return attend_sequence(
            query_seq, key_seq, value_seq, prefix_value, block_rows, scale_factor
        )

    contexts, log_totals = lax.map(
        forward_seq,
        (split_heads(query_low), split_heads(key_low), split_heads(value_low), prefix_length),
    )
    context = contexts.reshape(row_count, head_width)
    gate_columns = jnp.repeat(head_gate.astype(jnp.float32), head_size)
    gated_low = (context * gate_columns).astype(jnp.bfloat16)
    attn_terms = jnp.dot(gated_low, out_low, preferred_element_type=jnp.float32)
    attn_out = lax.psum(attn_terms, "col") + out_bias
    hidden_mask = hidden_gate.astype(jnp.float32)
    attn_rows = jnp.repeat(attention_gate.astype(jnp.float32), length)[:, None]
    dense_rows = jnp.repeat(feedforward_gate.astype(jnp.float32), length)[:, None]
    first_sum = token_full.astype(jnp.float32) + attn_rows * hidden_mask * attn_out
    normed_one, first_normed, first_inverse = norm_forward(first_sum, first_gain, first_shift)
    normed_low = normed_one.astype(jnp.bfloat16)
    pre_act = jnp.dot(normed_low, up_low, preferred_element_type=jnp.float32) + up_bias
    activated, gelu_pull = jax.vjp(partial(jax.nn.gelu, approximate=False), pre_act)
    unit_mask = intermediate_gate.astype(jnp.float32)
    inner_low = (activated * unit_mask).astype(jnp.bfloat16)
    dense_terms = jnp.dot(inner_low, down_low, preferred_element_type=jnp.float32)
    dense_out = lax.psum(dense_terms, "col") + down_bias
    second_sum = normed_one + dense_rows * hidden_mask * dense_out
    layer_full, second_normed, second_inverse = norm_forward(second_sum, second_gain, second_shift)
    layer_out = lax.dynamic_slice_in_dim(layer_full, col_index * part_width, part_width, 1)
    grad_full = lax.all_gather(cotangent, "col", axis=1, tiled=True).astype(jnp.float32)
    grad_gain_two = jnp.sum(grad_full * second_normed, axis=0)
    grad_shift_two = jnp.sum(grad_full, axis=0)
    grad_second = norm_backward(grad_full, second_normed, second_inverse, second_gain)
    grad_dense_low = (dense_rows * hidden_mask * grad_second).astype(jnp.bfloat16)
    dense_product = dense_out * grad_second
    grad_dense_gate = jnp.sum(
        dense_product.reshape(seq_count, length, model_width) * hidden_mask, axis=(1, 2)
    )
    hidden_from_dense = jnp.sum(dense_rows * dense_product, axis=0)
    grad_down_bias = jnp.sum(grad_dense_low.astype(jnp.float32), axis=0)
    up_low, down_low = (
        lax.all_gather(up_weight.astype(jnp.bfloat16), ("dp", "row"), axis=0, tiled=True),
        lax.all_gather(down_weight.astype(jnp.bfloat16), ("dp", "row"), axis=1, tiled=True),
    )
    grad_down = jnp.einsum(
        "tf,td->fd", inner_low, grad_dense_low, preferred_element_type=jnp.float32
    )
    grad_inner_low = jnp.einsum(
        "td,fd->tf", grad_dense_low, down_low, preferred_element_type=jnp.float32
    ).astype(jnp.bfloat16)
    grad_inner = grad_inner_low.astype(jnp.float32)
    grad_unit_gate = jnp.sum(activated * grad_inner, axis=0)
    (grad_pre,) = gelu_pull(unit_mask * grad_inner)
    grad_pre_low = grad_pre.astype(jnp.bfloat16)
    grad_up_bias = jnp.sum(grad_pre_low.astype(jnp.float32), axis=0)
    grad_up = jnp.einsum("td,tf->df", normed_low, grad_pre_low, preferred_element_type=jnp.float32)
    dense_parts = (
        lax.psum_scatter(grad_up, ("dp", "row"), scatter_dimension=0, tiled=True),
        lax.psum_scatter(grad_down, ("dp", "row"), scatter_dimension=1, tiled=True),
    )
    hidden_terms = jnp.einsum("tf,df->td", grad_pre_low, up_low, preferred_element_type=jnp.float32)
    grad_normed = grad_second + lax.psum(hidden_terms, "col")
    grad_gain_one = jnp.sum(grad_normed * first_normed, axis=0)
    grad_shift_one = jnp.sum(grad_normed, axis=0)
    grad_first = norm_backward(grad_normed, first_normed, first_inverse, first_gain)
    grad_attn_low = (attn_rows * hidden_mask * grad_first).astype(jnp.bfloat16)
    attn_product = attn_out * grad_first
    grad_attn_gate = jnp.sum(
        attn_product.reshape(seq_count, length, model_width) * hidden_mask, axis=(1, 2)
    )
    grad_hidden = hidden_from_dense + jnp.sum(attn_rows * attn_product, axis=0)
    grad_out_bias = jnp.sum(grad_attn_low.astype(jnp.float32), axis=0)
    qkv_low, out_low = (
        lax.all_gather(qkv_weight.astype(jnp.bfloat16), ("dp", "row"), axis=1, tiled=True),
        lax.all_gather(out_weight.astype(jnp.bfloat16), ("dp", "row"), axis=1, tiled=True),
    )
    grad_out = jnp.einsum("tc,td->cd", gated_low, grad_attn_low, preferred_element_type=jnp.float32)
    grad_gated_low = jnp.einsum(
        "td,cd->tc", grad_attn_low, out_low, preferred_element_type=jnp.float32
    ).astype(jnp.bfloat16)
    grad_head_cols = jnp.sum(context * grad_gated_low.astype(jnp.float32), axis=0)
    grad_head = jnp.sum(grad_head_cols.reshape(local_heads, head_size), axis=1)
    grad_context = grad_gated_low * gate_columns.astype(jnp.bfloat16)

    def backward_seq(element):
        query_seq, key_seq, value_seq, grad_seq, log_seq, prefix_value = element
        return attend_back(
            query_seq, key_seq, value_seq, grad_seq, log_seq, prefix_value, block_rows, scale_factor
        )

    grad_query, grad_keys, grad_values = lax.map(
        backward_seq,
        (
            split_heads(query_low),
            split_heads(key_low),
            split_heads(value_low),
            split_heads(grad_context),
            log_totals,
            prefix_length,
        ),
    )
    grad_qkv_low = jnp.stack([grad_query, grad_keys, grad_values]).reshape(3, row_count, head_width)
    grad_qkv_low = grad_qkv_low.astype(jnp.bfloat16)
    grad_query_bias = jnp.sum(grad_qkv_low[0].astype(jnp.float32), axis=0)
    grad_value_bias = jnp.sum(grad_qkv_low[2].astype(jnp.float32), axis=0)
    grad_qkv = jnp.einsum(
        "td,ktf->kdf", token_full, grad_qkv_low, preferred_element_type=jnp.float32
    )
    input_terms = jnp.einsum(
        "ktf,kdf->td", grad_qkv_low, qkv_low, preferred_element_type=jnp.float32
    )
    grad_tokens = lax.psum_scatter(
        input_terms.astype(jnp.bfloat16), "col", scatter_dimension=1, tiled=True
    ).astype(jnp.float32)
    grad_tokens = grad_tokens + lax.dynamic_slice_in_dim(
        grad_first, col_index * part_width, part_width, 1
    )
    grad_up_part, grad_down_part = dense_parts
    grad_qkv_part, grad_out_part = (
        lax.psum_scatter(grad_qkv, ("dp", "row"), scatter_dimension=1, tiled=True),
        lax.psum_scatter(grad_out, ("dp", "row"), scatter_dimension=1, tiled=True),
    )
    seq_total = seq_count * lax.axis_size(("dp", "row"))
    seq_start = lax.axis_index(("dp", "row")) * seq_count
    seq_stack = lax.dynamic_update_slice_in_dim(
        jnp.zeros((2, seq_total), jnp.float32),
        jnp.stack([grad_attn_gate, grad_dense_gate]),
        seq_start,
        1,
    )
    full_stack = jnp.stack(
        [
            grad_out_bias,
            grad_down_bias,
            grad_gain_one,
            grad_shift_one,
            grad_gain_two,
            grad_shift_two,
            grad_hidden,
        ]
    )
    half_stack = jnp.stack([grad_query_bias, grad_value_bias])
    unit_stack = jnp.stack([grad_up_bias, grad_unit_gate])
    full_sum, half_sum, unit_sum, head_sum, seq_sum = lax.psum(
        (full_stack, half_stack, unit_stack, grad_head, seq_stack), ("dp", "row")
    )
    return (
        layer_out,
        grad_tokens,
        grad_qkv_part,
        grad_out_part,
        grad_up_part,
        grad_down_part,
        half_sum[0],
        half_sum[1],
        full_sum[0],
        unit_sum[0],
        full_sum[1],
        full_sum[2],
        full_sum[3],
        full_sum[4],
        full_sum[5],
        head_sum,
        full_sum[6],
        unit_sum[1],
        seq_sum[0],
        seq_sum[1],
    )


low_type = jnp.bfloat16
wide = jnp.float32
mesh_ids = pl.DeviceIdType.MESH


def dot_nn(left, right):
    return jnp.dot(left, right, preferred_element_type=wide)


def dot_nt(left, right):
    return lax.dot_general(left, right, (((1,), (1,)), ((), ())), preferred_element_type=wide)


def rows_at(index, count):
    return pl.ds(pl.multiple_of(index * count, count), count)


def fold_rows(values):
    return jnp.sum(values.reshape(values.shape[0] // 8, 8, values.shape[1]), axis=0)


def norm_parts(values):
    centre = jnp.mean(values, axis=1, keepdims=True)
    centred = values - centre
    spread = jnp.mean(centred * centred, axis=1, keepdims=True)
    inverse = lax.rsqrt(spread + norm_eps)
    return centred * inverse, inverse


class Place:
    def __init__(self, row_size):
        self.dp, self.row, self.col = (lax.axis_index(name) for name in ("dp", "row", "col"))
        self.row_size = row_size
        self.x, self.y = lax.rem(self.dp, 2), self.dp // 2
        self.x_dp = self.y * 2 + (1 - self.x)
        self.y_dp = (1 - self.y) * 2 + self.x

    def x_mate(self):
        return {"dp": self.x_dp}

    def y_mate(self):
        return {"dp": self.y_dp}

    def row_mate(self, step):
        return {"row": lax.rem(self.row + step, self.row_size)}

    def col_mate(self):
        return {"col": 1 - self.col}

    def barrier(self):
        semaphore = pltpu.get_barrier_semaphore()
        mates = [self.x_mate(), self.y_mate(), self.col_mate()]
        mates += [self.row_mate(step) for step in range(1, self.row_size)]
        for mate in mates:
            pl.semaphore_signal(semaphore, inc=1, device_id=mate, device_id_type=mesh_ids)
        pl.semaphore_wait(semaphore, len(mates))


def send(source, target, semaphores, index, mate):
    sent, received = semaphores
    return pltpu.make_async_remote_copy(
        src_ref=source,
        dst_ref=target,
        send_sem=sent.at[index],
        recv_sem=received.at[index],
        device_id=mate,
        device_id_type=mesh_ids,
    )


class Gather:
    def __init__(self, place, shards, chunks, order, own_sem, z_sems, two_sems, three_sems):
        self.place, self.shards, self.chunks = place, shards, chunks
        self.own_sem, self.z_sems, self.two_sems, self.three_sems = own_sem, z_sems, two_sems, three_sems
        self.part = shards[0].shape[0]
        self.block = self.part * place.row_size
        self.half = self.block // 2
        self.steps, self.done = order, 0

    def half_rows(self, dp, half):
        return pl.ds(pl.multiple_of(dp * self.block + half * self.half, 16), self.half)

    def own_rows(self):
        place = self.place
        return pl.ds(pl.multiple_of(place.dp * self.block + place.row * self.part, 16), self.part)

    def own(self, c):
        return pltpu.make_async_copy(self.shards[c], self.chunks[c].at[self.own_rows()], self.own_sem.at[c])

    def along_z(self, c):
        place = self.place
        return [
            send(
                self.shards[c], self.chunks[c].at[self.own_rows()], self.z_sems, (c, step - 1), place.row_mate(step)
            )
            for step in range(1, place.row_size)
        ]

    def pass_on(self, c, dp, half, sems, index, mate):
        at = self.chunks[c].at[self.half_rows(dp, half)]
        return send(at, at, sems, (c, index), mate)

    def second(self, c):
        place = self.place
        return [
            self.pass_on(c, place.dp, 0, self.two_sems, 0, place.x_mate()),
            self.pass_on(c, place.dp, 1, self.two_sems, 1, place.y_mate()),
        ]

    def third(self, c):
        place = self.place
        return [
            self.pass_on(c, place.dp, 0, self.three_sems, 0, place.y_mate()),
            self.pass_on(c, place.dp, 1, self.three_sems, 2, place.x_mate()),
            self.pass_on(c, place.x_dp, 0, self.three_sems, 1, place.y_mate()),
            self.pass_on(c, place.y_dp, 1, self.three_sems, 3, place.x_mate()),
        ]

    def start(self, c):
        self.own(c).start()
        for copy in self.along_z(c):
            copy.start()

    def step(self):
        stage, c = self.steps[self.done]
        self.done += 1
        if stage == 0:
            self.own(c).wait()
            for copy in self.along_z(c):
                copy.wait_recv()
            for copy in self.second(c):
                copy.start()
        elif stage == 1:
            for copy in self.second(c):
                copy.wait_recv()
            for copy in self.third(c):
                copy.start()
        else:
            for copy in self.third(c):
                copy.wait_recv()

    def advance(self, count):
        for _ in range(count):
            if self.done < len(self.steps):
                self.step()

    def need(self, c):
        while self.done <= self.steps.index((2, c)):
            self.step()

    def finish(self):
        self.advance(len(self.steps))
        for c in range(len(self.chunks)):
            for copy in self.along_z(c) + self.second(c) + self.third(c):
                copy.wait_send()


class Scatter:
    def __init__(self, place, chunks, outs, order, first, mid_send, mid, last_send, last, one_sems, two_sems, z_sems):
        self.place, self.chunks, self.outs = place, chunks, outs
        self.first, self.mid_send, self.mid, self.last_send, self.last = first, mid_send, mid, last_send, last
        self.one_sems, self.two_sems, self.z_sems = one_sems, two_sems, z_sems
        self.part = outs[0].shape[0]
        self.block = self.part * place.row_size
        self.half = self.block // 2
        self.count = len(chunks)
        self.steps, self.done, self.begun = order, 0, []

    def half_rows(self, dp, half):
        return pl.ds(pl.multiple_of(dp * self.block + half * self.half, 16), self.half)

    def one(self, c):
        place, chunk, first = self.place, self.chunks[c], self.first[c]
        found = []
        for i in range(2):
            rows = self.half_rows((1 - place.y) * 2 + i, 0)
            found.append(send(chunk.at[rows], first.at[0, i], self.one_sems, (c, i), place.y_mate()))
            rows = self.half_rows(i * 2 + (1 - place.x), 1)
            found.append(send(chunk.at[rows], first.at[1, i], self.one_sems, (c, 2 + i), place.x_mate()))
        return found

    def two(self, c):
        place, mid_send, mid = self.place, self.mid_send[c], self.mid[c]
        return [
            send(mid_send.at[0], mid.at[0], self.two_sems, (c, 0), place.x_mate()),
            send(mid_send.at[1], mid.at[1], self.two_sems, (c, 1), place.y_mate()),
        ]

    def along_z(self, c):
        place = self.place
        found = []
        for step in range(1, place.row_size):
            mate = lax.rem(place.row + step, place.row_size)
            rows = pl.ds(pl.multiple_of(mate * self.part, 16), self.part)
            found.append(
                send(
                    self.last_send[c].at[rows], self.last[c].at[step - 1], self.z_sems, (c, step - 1),
                    place.row_mate(step),
                )
            )
        return found

    def begin(self, c):
        self.begun.append(c)
        for copy in self.one(c):
            copy.start()

    def step(self):
        stage, c = self.steps[self.done]
        self.done += 1
        place, chunk = self.place, self.chunks[c]
        first, mid_send, mid = self.first[c], self.mid_send[c], self.mid[c]
        last_send, last = self.last_send[c], self.last[c]
        if stage == 0:
            for copy in self.one(c):
                copy.wait_recv()
            mid_send[0] = (
                chunk[self.half_rows(place.x_dp, 0), :].astype(wide) + first[0, 1 - place.x].astype(wide)
            ).astype(low_type)
            mid_send[1] = (
                chunk[self.half_rows(place.y_dp, 1), :].astype(wide) + first[1, 1 - place.y].astype(wide)
            ).astype(low_type)
            for copy in self.two(c):
                copy.start()
        elif stage == 1:
            for copy in self.two(c):
                copy.wait_recv()
            for half, slot in ((0, place.x), (1, place.y)):
                last_send[pl.ds(half * self.half, self.half), :] = (
                    chunk[self.half_rows(place.dp, half), :].astype(wide)
                    + first[half, slot].astype(wide)
                    + mid[half].astype(wide)
                ).astype(low_type)
            for copy in self.along_z(c):
                copy.start()
        else:
            total = last_send[pl.ds(pl.multiple_of(place.row * self.part, 16), self.part), :].astype(wide)
            for step, copy in enumerate(self.along_z(c)):
                copy.wait_recv()
                total = total + last[step].astype(wide)
            self.outs[c][...] = total

    def advance(self, count):
        for _ in range(count):
            if self.done < len(self.steps) and self.steps[self.done][1] in self.begun:
                self.step()

    def finish(self):
        self.advance(len(self.steps))
        for c in range(self.count):
            for copy in self.one(c) + self.two(c) + self.along_z(c):
                copy.wait_send()


def masked_tile(tile, query_start, key_start, prefix):
    key_index = key_start + lax.broadcasted_iota(jnp.int32, tile.shape, 0)
    query_index = query_start + lax.broadcasted_iota(jnp.int32, tile.shape, 1)
    return jnp.where((key_index < prefix) | (key_index <= query_index), tile, masked_value)


def key_tiles(block, rows, prefix_most):
    count = max((block + 1) * rows, prefix_most) // rows
    return [(tile, tile >= block) for tile in range(count)]


def flat_row(ref):
    return ref[...].reshape(1, ref.shape[0])


def gate_row(gates, heads, size):
    head = lax.broadcasted_iota(jnp.int32, (1, heads * size), 1) // size
    row = jnp.zeros((1, heads * size), wide)
    for h in range(heads):
        row = jnp.where(head == h, gates[h].astype(wide), row)
    return row


def forward_kernel(
    cut,
    token_part, cot_part, qkv_w, out_w, up_w, down_w, query_bias, value_bias, out_bias, up_bias, down_bias,
    first_gain, first_shift, second_gain, second_shift, hidden_gate, unit_gate,
    head_gate, attention_gate, feedforward_gate, prefix_length,
    wa_out, wm_out, token_out, token_t_out, qkv_out, lse_out, ctx_out, attn_out_out, normed_t_out,
    gelu_out, slope_out, layer_out, second_out, dense_out_low, dense_t_out, sums_out,
    wa, wm, token, token_t, qkv, lse, ctx, attn_out, normed_t, gelu, slope, layer, second, dense_low, dense_t, sums,
    cot, value_t, ctx_t, normed, normed_low, total, precv, drecv, shards_a, shards_m,
    own_sem, z_s, z_r, two_s, two_r, three_s, three_r, col_s, col_r, half_sem, out_sem,
):
    length, heads, size = cut.length, cut.heads, cut.size
    part, rows, fine = cut.part_width, cut.rows, cut.fine
    blocks = length // rows
    pair = 2 * size
    pairs = heads // 2
    group = wm.shape[2]
    place = Place(cut.row_size)
    for p in range(pairs):
        for k in range(3):
            shards_a[p, :, k * pair : (k + 1) * pair] = qkv_w[k, :, p * pair : (p + 1) * pair].astype(low_type)
    shards_a[pairs] = out_w[...].astype(low_type)
    for j in range(2):
        shards_m[2 * j] = up_w[:, j * group : (j + 1) * group].astype(low_type)
        shards_m[2 * j + 1] = down_w[:, j * group : (j + 1) * group].astype(low_type)
    place.barrier()
    prefix = prefix_length[0]
    attn_gate, dense_gate = attention_gate[0].astype(wide), feedforward_gate[0].astype(wide)
    hidden = flat_row(hidden_gate).astype(wide)
    query_bias, value_bias, up_bias, out_bias, down_bias, first_gain, first_shift, second_gain, second_shift = (
        flat_row(ref)
        for ref in (
            query_bias, value_bias, up_bias, out_bias, down_bias, first_gain, first_shift, second_gain, second_shift
        )
    )
    unit_row = flat_row(unit_gate).astype(wide)
    mate = place.col_mate()
    chunks = [wa.at[i] for i in range(pairs + 1)] + [wm.at[i] for i in range(4)]
    shards = [shards_a.at[i] for i in range(pairs + 1)] + [shards_m.at[i] for i in range(4)]
    order = gather_order(len(chunks))
    gather = Gather(place, shards, chunks, order, own_sem, (z_s, z_r), (two_s, two_r), (three_s, three_r))
    own_cols = pl.ds(pl.multiple_of(place.col * part, 128), part)
    halves, crossed = [], []
    for i, (source, target) in enumerate(((token_part, token), (cot_part, cot))):
        halves.append(pltpu.make_async_copy(source, target.at[:, own_cols], half_sem.at[i]))
        crossed.append(send(source, target.at[:, own_cols], (col_s, col_r), i, mate))
    gather.start(0)
    for i in range(2):
        halves[i].start()
        crossed[i].start()
    for c in range(1, len(chunks)):
        gather.start(c)
    outs = []

    def put(source, target):
        copy = pltpu.make_async_copy(source, target, out_sem.at[len(outs)])
        copy.start()
        outs.append(copy)

    sums[...] = jnp.zeros_like(sums)
    halves[0].wait()
    crossed[0].wait_recv()

    @pl.loop(0, blocks)
    def _(b):
        at = rows_at(b, rows)
        token_t[:, at] = token[at, :].T

    put(token, token_out)
    put(token_t, token_t_out)
    lane_head = lax.broadcasted_iota(jnp.int32, (1, pair), 1) // size
    for p in range(pairs):
        gather.need(p)
        query_row = query_bias[:, p * pair : (p + 1) * pair]
        bias = jnp.concatenate(
            [query_row, jnp.zeros_like(query_row), value_bias[:, p * pair : (p + 1) * pair]], axis=1
        )

        @pl.loop(0, blocks)
        def _(b, p=p, bias=bias):
            at = rows_at(b, rows)
            made = dot_nn(token[at, :], wa[p]) + bias
            qkv[p, at, :] = made.astype(low_type)
            value_t[:, at] = made[:, 2 * pair :].T.astype(low_type)

        gather.advance(1)

        @pl.loop(0, 2)
        def _(h, p=p):
            own = jnp.where(lane_head == h, size ** (-0.5), 0.0).astype(low_type)
            head_rows = rows_at(h, size)
            for b in range(blocks):
                query = qkv[p, b * rows : (b + 1) * rows, :pair] * own
                tiles, masked = [], key_tiles(b, rows, cut.prefix_most)
                for tile, needs in masked:
                    score = dot_nt(qkv[p, tile * rows : (tile + 1) * rows, pair : 2 * pair], query)
                    tiles.append(masked_tile(score, b * rows, tile * rows, prefix) if needs else score)
                peak = tiles[0].max(axis=0, keepdims=True)
                for score in tiles[1:]:
                    peak = jnp.maximum(peak, score.max(axis=0, keepdims=True))
                row_total = jnp.zeros_like(peak)
                weights = []
                for score in tiles:
                    weights.append(jnp.exp(score - peak))
                    row_total = row_total + weights[-1].sum(axis=0, keepdims=True)
                share = 1.0 / row_total
                found = jnp.zeros((size, rows), wide)
                for (tile, _), weight in zip(masked, weights):
                    found = found + dot_nn(
                        value_t[head_rows, tile * rows : (tile + 1) * rows], (weight * share).astype(low_type)
                    )
                ctx_t[head_rows, b * rows : (b + 1) * rows] = found
                lse[2 * p + h, :, b * rows : (b + 1) * rows] = peak + jnp.log(row_total)
                if b % 2:
                    for now in range(2):

                        @pl.when(h == now)
                        def _():
                            gather.advance(1)

        @pl.loop(0, blocks)
        def _(b, p=p):
            at = rows_at(b, rows)
            ctx[at, p * pair : (p + 1) * pair] = ctx_t[:, at].T.astype(low_type)

    put(qkv, qkv_out)
    put(lse, lse_out)
    put(ctx, ctx_out)
    gather.need(pairs)
    put(wa, wa_out)
    gate_columns = gate_row(head_gate, heads, size).astype(low_type)

    def swap(source, target, start, b):
        at = pl.ds(b * rows, rows) if isinstance(b, int) else rows_at(b, rows)
        return send(source.at[at], target.at[at], (col_s, col_r), start + b, mate)

    @pl.loop(0, blocks)
    def _(b):
        at = rows_at(b, rows)
        attn_out[at, :] = dot_nt(ctx[at, :] * gate_columns, wa[pairs])
        swap(attn_out, precv, 2, b).start()

    gather.advance(1)
    for b in range(blocks):
        swap(attn_out, precv, 2, b).wait()

        @pl.loop(b * rows // fine, (b + 1) * rows // fine)
        def _(i):
            at = rows_at(i, fine)
            attn = attn_out[at, :] + precv[at, :] + out_bias
            attn_out[at, :] = attn
            first, _ = norm_parts(token[at, :].astype(wide) + attn_gate * hidden * attn)
            out = first * first_gain + first_shift
            normed[at, :] = out
            normed_low[at, :] = out.astype(low_type)

    put(attn_out, attn_out_out)
    gather.advance(1)
    for j in range(2):
        gather.need(pairs + 1 + 2 * j)
        bias_row = up_bias[:, j * group : (j + 1) * group]
        unit_mask = unit_row[:, j * group : (j + 1) * group].astype(low_type)

        @pl.loop(0, blocks)
        def _(b, j=j, bias_row=bias_row):
            at = rows_at(b, rows)
            pre = dot_nn(normed_low[at, :], wm[2 * j]) + bias_row
            share = 0.5 * (1.0 + lax.erf(pre * (2.0 ** -0.5)))
            gelu[j, at, :] = (pre * share).astype(low_type)
            density = jnp.exp(-0.5 * pre * pre) * ((2.0 * math.pi) ** -0.5)
            slope[j, at, :] = (share + pre * density).astype(low_type)
            if j == 0:
                normed_t[:, at] = normed_low[at, :].T

        gather.need(pairs + 2 + 2 * j)

        @pl.loop(0, blocks)
        def _(b, j=j, unit_mask=unit_mask):
            at = rows_at(b, rows)
            made = dot_nt(gelu[j, at, :] * unit_mask, wm[2 * j + 1])
            if j == 0:
                total[at, :] = made
            else:
                total[at, :] += made
                swap(total, drecv, 2 + blocks, b).start()

    put(normed_t, normed_t_out)
    put(gelu, gelu_out)
    put(slope, slope_out)
    put(wm, wm_out)
    halves[1].wait()
    crossed[1].wait_recv()
    for b in range(blocks):
        swap(total, drecv, 2 + blocks, b).wait_recv()

        @pl.loop(b * rows // fine, (b + 1) * rows // fine)
        def _(i):
            at = rows_at(i, fine)
            dense = total[at, :] + drecv[at, :] + down_bias
            last, inverse = norm_parts(normed[at, :] + dense_gate * hidden * dense)
            full = last * second_gain + second_shift
            layer[at, :] = jnp.where(place.col == 0, full[:, :part], full[:, part:])
            grad = cot[at, :].astype(wide)
            scaled = grad * second_gain
            one = jnp.mean(scaled, axis=1, keepdims=True)
            two = jnp.mean(scaled * last, axis=1, keepdims=True)
            made = inverse * (scaled - one - last * two)
            second[at, :] = made
            gated = (dense_gate * hidden * made).astype(low_type)
            dense_low[at, :] = gated
            product = dense * made
            sums[0] += fold_rows(grad * last)
            sums[1] += fold_rows(grad)
            sums[2] += fold_rows(gated.astype(wide))
            sums[3] += fold_rows(product)

        at = pl.ds(b * rows, rows)
        dense_t[:, at] = dense_low[at, :].T

    put(layer, layer_out)
    put(second, second_out)
    put(dense_low, dense_out_low)
    put(dense_t, dense_t_out)
    put(sums, sums_out)
    gather.finish()
    for copy in crossed:
        copy.wait_send()
    for b in range(blocks):
        swap(total, drecv, 2 + blocks, b).wait_send()
    for copy in outs:
        copy.wait()


def backward_kernel(
    cut,
    wa_in, wm_in, token_in, token_t_in, qkv_in, lse_in, ctx_in, attn_out_in, normed_t_in,
    gelu_in, slope_in, second_in, dense_low_in, dense_t_in, sums_in,
    first_gain, hidden_gate, unit_gate, head_gate, attention_gate, feedforward_gate, prefix_length,
    grad_token, small_out, *rest,
):
    length, width, heads, size = cut.length, cut.width, cut.heads, cut.size
    part, rows, fine = cut.part_width, cut.rows, cut.fine
    blocks = length // rows
    pair = 2 * size
    pairs = heads // 2
    count = pairs + 5
    rest = list(rest)

    def take(number):
        taken = rest[:number]
        del rest[:number]
        return taken

    grads = take(count)
    (wa, wm, token, token_t, qkv, lse, ctx, attn_out, normed_t, gelu, slope, second, dense_low, dense_t, sums) = take(15)
    (total, precv, fsend, frecv, ctx_grad, triple, key_grad, value_grad, query_t, key_t) = take(10)
    (small, small_x, small_y, small_z, unit_sums, head_sums) = take(6)
    buffers, first, mid_send, mid, last_send, last = (take(count) for _ in range(6))
    (in_sem, one_s, one_r, two_s, two_r, z_s, z_r, col_s, col_r, small_s, small_r) = take(11)
    place = Place(cut.row_size)
    loads = {}
    for i, (name, source, target) in enumerate(
        (
            ("dense_t", dense_t_in, dense_t),
            ("gelu", gelu_in, gelu),
            ("dense_low", dense_low_in, dense_low),
            ("wm", wm_in, wm),
            ("slope", slope_in, slope),
            ("normed_t", normed_t_in, normed_t),
            ("sums", sums_in, sums),
            ("second", second_in, second),
            ("attn_out", attn_out_in, attn_out),
            ("token", token_in, token),
            ("wa", wa_in, wa),
            ("ctx", ctx_in, ctx),
            ("qkv", qkv_in, qkv),
            ("lse", lse_in, lse),
            ("token_t", token_t_in, token_t),
        )
    ):
        loads[name] = pltpu.make_async_copy(source, target, in_sem.at[i])
        loads[name].start()

    def load(*names):
        for name in names:
            loads[name].wait()

    place.barrier()
    prefix = prefix_length[0]
    attn_gate, dense_gate = attention_gate[0].astype(wide), feedforward_gate[0].astype(wide)
    hidden, unit_row = flat_row(hidden_gate).astype(wide), flat_row(unit_gate).astype(wide)
    first_gain = flat_row(first_gain)
    mate = place.col_mate()
    scatter = Scatter(
        place, buffers, grads, scatter_order(pairs), first, mid_send, mid, last_send, last,
        (one_s, one_r), (two_s, two_r), (z_s, z_r),
    )
    unit_sums[...] = jnp.zeros_like(unit_sums)
    head_sums[...] = jnp.zeros_like(head_sums)
    group = wm.shape[2]

    def swap(source, target, start, b):
        at = pl.ds(b * rows, rows) if isinstance(b, int) else rows_at(b, rows)
        return send(source.at[at], target.at[at], (col_s, col_r), start + b, mate)

    def product(target, left, right, mask=None):
        @pl.loop(0, width // rows)
        def _(i):
            at = rows_at(i, rows)
            made = dot_nn(left[at, :], right[...])
            target[at, :] = (made if mask is None else made * mask).astype(low_type)

    masks = [unit_row[:, j * group : (j + 1) * group] for j in range(2)]
    load("dense_t", "gelu")
    for j in range(2):
        product(buffers[j], dense_t, gelu.at[j], masks[j])
        scatter.begin(j)
    load("dense_low", "wm", "slope")
    for j in range(2):

        @pl.loop(0, blocks)
        def _(b, j=j):
            at = rows_at(b, rows)
            inner = dot_nn(dense_low[at, :], wm[2 * j + 1]).astype(low_type).astype(wide)
            unit_sums[2 + j] += fold_rows(gelu[j, at, :].astype(wide) * inner)
            pre = (masks[j] * inner * slope[j, at, :].astype(wide)).astype(low_type)
            slope[j, at, :] = pre
            unit_sums[j] += fold_rows(pre.astype(wide))
            made = dot_nt(pre, wm[2 * j])
            if j == 0:
                total[at, :] = made
            else:
                total[at, :] += made
                swap(total, precv, 0, b).start()

        scatter.advance(1)
        if j == 0:
            load("normed_t")
        product(buffers[2 + j], normed_t, slope.at[j])
        scatter.begin(2 + j)

    load("sums", "second", "attn_out", "token")
    for b in range(blocks):
        swap(total, precv, 0, b).wait_recv()

        @pl.loop(b * rows // fine, (b + 1) * rows // fine)
        def _(i):
            at = rows_at(i, fine)
            attn = attn_out[at, :]
            gate_cols = attn_gate * hidden
            normed, inverse = norm_parts(token[at, :].astype(wide) + gate_cols * attn)
            grad = second[at, :] + (total[at, :] + precv[at, :])
            scaled = grad * first_gain
            one = jnp.mean(scaled, axis=1, keepdims=True)
            two = jnp.mean(scaled * normed, axis=1, keepdims=True)
            made = inverse * (scaled - one - normed * two)
            second[at, :] = made
            gated = (gate_cols * made).astype(low_type)
            dense_low[at, :] = gated
            sums[4] += fold_rows(grad * normed)
            sums[5] += fold_rows(grad)
            sums[6] += fold_rows(gated.astype(wide))
            sums[7] += fold_rows(attn * made)

        at = pl.ds(b * rows, rows)
        dense_t[:, at] = dense_low[at, :].T
        if b % 2:
            scatter.advance(1)

    for b in range(blocks):
        swap(total, precv, 0, b).wait_send()
    load("wa", "ctx", "qkv", "lse", "token_t")
    gate_columns = gate_row(head_gate, heads, size)

    @pl.loop(0, blocks)
    def _(b):
        at = rows_at(b, rows)
        gated = dot_nn(dense_low[at, :], wa[pairs]).astype(low_type).astype(wide)
        seen = ctx[at, :].astype(wide)
        head_sums[...] += fold_rows(seen * gated)
        ctx_grad[at, :] = (gated * gate_columns).astype(low_type)
        ctx[at, :] = (seen * gate_columns).astype(low_type)

    product(buffers[4], dense_t, ctx)
    scatter.begin(4)
    scatter.advance(1)
    lane_head = lax.broadcasted_iota(jnp.int32, (1, pair), 1) // size
    bias_sums = []
    for p in range(pairs):

        @pl.loop(0, blocks)
        def _(b, p=p):
            at = rows_at(b, rows)
            key_t[:, at] = qkv[p, at, pair : 2 * pair].astype(wide).T.astype(low_type)

        key_grad[...] = jnp.zeros_like(key_grad)
        value_grad[...] = jnp.zeros_like(value_grad)

        @pl.loop(0, 2)
        def _(h, p=p):
            own = jnp.where(lane_head == h, size ** (-0.5), 0.0).astype(low_type)
            one_head = jnp.where(lane_head == h, 1.0, 0.0).astype(low_type)
            head_rows = rows_at(h, size)
            for b in range(blocks):
                query = qkv[p, b * rows : (b + 1) * rows, :pair] * own
                context = ctx_grad[b * rows : (b + 1) * rows, p * pair : (p + 1) * pair] * one_head
                logs = lse[2 * p + h, :, b * rows : (b + 1) * rows]
                inner = jnp.zeros_like(logs)
                kept, masked = [], key_tiles(b, rows, cut.prefix_most)
                for tile, needs in masked:
                    score = dot_nt(qkv[p, tile * rows : (tile + 1) * rows, pair : 2 * pair], query)
                    score = masked_tile(score, b * rows, tile * rows, prefix) if needs else score
                    prob = jnp.exp(score - logs)
                    grad_prob = dot_nt(qkv[p, tile * rows : (tile + 1) * rows, 2 * pair :], context)
                    inner = inner + (prob * grad_prob).sum(axis=0, keepdims=True)
                    kept.append((prob, grad_prob))
                found = jnp.zeros((size, rows), wide)
                for (tile, _), (prob, grad_prob) in zip(masked, kept):
                    at = slice(tile * rows, (tile + 1) * rows)
                    grad_score = (prob * (grad_prob - inner)).astype(low_type)
                    value_grad[at, :] += dot_nn(prob.astype(low_type), context)
                    key_grad[at, :] += dot_nn(grad_score, query)
                    found = found + dot_nn(key_t[head_rows, at], grad_score)
                query_t[head_rows, b * rows : (b + 1) * rows] = found * size ** (-0.5)
                if b % 2:
                    for now in range(2):

                        @pl.when(h == now)
                        def _():
                            scatter.advance(1)

        query_sum = jnp.zeros((8, pair), wide)
        value_sum = jnp.zeros((8, pair), wide)
        for b in range(blocks):
            at = pl.ds(b * rows, rows)
            query_low = query_t[:, at].T.astype(low_type)
            value_low = value_grad[at, :].astype(low_type)
            triple[at, :pair] = query_low
            triple[at, pair : 2 * pair] = key_grad[at, :].astype(low_type)
            triple[at, 2 * pair :] = value_low
            query_sum += fold_rows(query_low.astype(wide))
            value_sum += fold_rows(value_low.astype(wide))
        bias_sums.append((query_sum, value_sum))
        product(buffers[5 + p], token_t, triple)
        scatter.begin(5 + p)
        if p < pairs - 1:
            scatter.advance(1)

        @pl.loop(0, blocks)
        def _(b, p=p):
            at = rows_at(b, rows)
            made = dot_nt(triple[at, :], wa[p])
            if p > 0:
                made = total[at, :] + made
            if p < pairs - 1:
                total[at, :] = made
            else:
                mine = jnp.where(place.col == 0, made[:, :part], made[:, part:])
                other = jnp.where(place.col == 0, made[:, part:], made[:, :part])
                kept = second[at, :]
                grad_token[at, :] = mine + jnp.where(place.col == 0, kept[:, :part], kept[:, part:])
                fsend[at, :] = other.astype(low_type)
                swap(fsend, frecv, blocks, b).start()

    def whole(values):
        return jnp.sum(values, axis=0, keepdims=True)

    dense_col, attn_col = whole(sums[3]), whole(sums[7])
    seq_lane = lax.broadcasted_iota(jnp.int32, (1, width), 1)
    here = place.dp * place.row_size + place.row
    dense_all = jnp.sum(dense_col * hidden, axis=1, keepdims=True)
    attn_all = jnp.sum(attn_col * hidden, axis=1, keepdims=True)
    seq_row = jnp.where(seq_lane == here, attn_all, 0.0) + jnp.where(seq_lane == here + width // 2, dense_all, 0.0)
    small[0:1, :] = whole(sums[6])
    small[1:2, :] = whole(sums[2])
    small[2:3, :] = whole(sums[4])
    small[3:4, :] = whole(sums[5])
    small[4:5, :] = whole(sums[0])
    small[5:6, :] = whole(sums[1])
    small[6:7, :] = dense_gate * dense_col + attn_gate * attn_col
    small[7:8, :] = seq_row
    for j in range(4):
        small[8 + j : 9 + j, :] = whole(unit_sums[j])
    for p in range(pairs):
        small[12:13, p * pair : (p + 1) * pair] = whole(bias_sums[p][0])
        small[12:13, part + p * pair : part + (p + 1) * pair] = whole(bias_sums[p][1])
    small[13:14, :part] = whole(head_sums[...])
    small[13:14, part:] = jnp.zeros((1, part), wide)
    small[14:16, :] = jnp.zeros((2, width), wide)
    copy_x = send(small, small_x.at[0], (small_s, small_r), 0, place.x_mate())
    copy_x.start()
    scatter.advance(1)
    copy_x.wait_recv()
    small_x[1] = small[...] + small_x[0]
    copy_y = send(small_x.at[1], small_y.at[0], (small_s, small_r), 1, place.y_mate())
    copy_y.start()
    scatter.advance(1)
    copy_y.wait_recv()
    mine = small_x[1] + small_y[0]
    small_y[1] = mine
    small_z[place.row] = mine
    copies = [
        send(small_y.at[1], small_z.at[place.row], (small_s, small_r), 1 + step, place.row_mate(step))
        for step in range(1, cut.row_size)
    ]
    for copy in copies:
        copy.start()
    for b in range(blocks):
        swap(fsend, frecv, blocks, b).wait_recv()
        at = pl.ds(b * rows, rows)
        grad_token[at, :] += frecv[at, :].astype(wide)
    scatter.finish()
    for copy in copies:
        copy.wait_recv()
    result = small_z[0]
    for z in range(1, cut.row_size):
        result = result + small_z[z]
    small_out[...] = result
    for copy in [copy_x, copy_y] + copies:
        copy.wait_send()
    for b in range(blocks):
        swap(fsend, frecv, blocks, b).wait_send()


def place_kernel(
    cut,
    small, down_0, down_1, up_0, up_1, grad_out_t, *rest,
):
    pairs, pair, part, width = cut.heads // 2, 2 * cut.size, cut.part_width, cut.width
    pieces, rest = rest[:pairs], rest[pairs:]
    (
        grad_qkv, grad_out, grad_up, grad_down, query_bias, value_bias, out_bias, up_bias, down_bias, first_gain,
        first_shift, second_gain, second_shift, head, hidden, unit, attention, feedforward,
    ) = rest
    group = cut.units // 2
    for p, piece in enumerate(pieces):
        for k in range(3):
            grad_qkv[k, :, p * pair : (p + 1) * pair] = piece[:, k * pair : (k + 1) * pair]
    grad_out[...] = grad_out_t[...]
    for j, (up, down) in enumerate(((up_0, down_0), (up_1, down_1))):
        grad_up[:, j * group : (j + 1) * group] = up[...]
        grad_down[:, j * group : (j + 1) * group] = down[...]

    def flat(target, values):
        target[...] = values.reshape(target.shape)

    flat(up_bias, jnp.concatenate([small[8:9, :], small[9:10, :]], axis=1))
    flat(unit, jnp.concatenate([small[10:11, :], small[11:12, :]], axis=1))
    flat(query_bias, small[12:13, :part])
    flat(value_bias, small[12:13, part:])
    for row, target in enumerate((out_bias, down_bias, first_gain, first_shift, second_gain, second_shift, hidden)):
        flat(target, small[row : row + 1, :])
    lane = lax.broadcasted_iota(jnp.int32, (1, part), 1) // cut.size
    slot = lax.broadcasted_iota(jnp.int32, (1, cut.heads), 1)
    found = jnp.zeros((1, cut.heads), wide)
    for h in range(cut.heads):
        one = jnp.sum(jnp.where(lane == h, small[13:14, :part], 0.0), axis=1, keepdims=True)
        found = jnp.where(slot == h, one, found)
    flat(head, found)
    seq_total = attention.shape[0]
    flat(attention, small[7:8, :seq_total])
    flat(feedforward, small[7:8, width // 2 : width // 2 + seq_total])


def gather_order(count):
    return [(stage, t - stage) for t in range(count + 2) for stage in range(3) if 0 <= t - stage < count]


def scatter_order(pairs):
    out = [(0, 0), (0, 1), (0, 2), (1, 0), (1, 1), (0, 3), (2, 0), (1, 2), (2, 1), (1, 3), (0, 4), (2, 2), (1, 4), (2, 3)]
    before = 4
    for c in range(5, 5 + pairs):
        out += [(0, c), (2, before), (1, c)]
        before = c
    return out + [(2, before)]


class Cut(NamedTuple):
    length: int
    width: int
    part_width: int
    heads: int
    size: int
    units: int
    part: int
    row_size: int
    rows: int
    fine: int
    prefix_most: int


def any_spec():
    return pl.BlockSpec(memory_space=pl.ANY)


def vmem_spec():
    return pl.BlockSpec(memory_space=pltpu.VMEM)


def smem_spec():
    return pl.BlockSpec(memory_space=pltpu.SMEM)


def like(items):
    return [jax.ShapeDtypeStruct(shape, kind) for shape, kind in items]


def scratch(items):
    return [pltpu.VMEM(shape, kind) for shape, kind in items]


def dma(*shape):
    return pltpu.SemaphoreType.DMA(shape)


vmem_most = 67043328


def run_forward(cut, token_part, cot_part, *args):
    length, width, half = cut.length, cut.width, cut.part_width
    group = cut.units // 2
    chunks_a, chunks = cut.heads // 2 + 1, cut.heads // 2 + 5
    blocks = length // cut.rows
    kept = [
        ((chunks_a, width, half), low_type),
        ((4, width, group), low_type),
        ((length, width), low_type),
        ((width, length), low_type),
        ((cut.heads // 2, length, half), low_type),
        ((cut.heads, 1, length), wide),
        ((length, half), low_type),
        ((length, width), wide),
        ((width, length), low_type),
        ((2, length, group), low_type),
        ((2, length, group), low_type),
        ((length, half), wide),
        ((length, width), wide),
        ((length, width), low_type),
        ((width, length), low_type),
        ((8, 8, width), wide),
    ]
    own = [
        ((length, width), low_type),
        ((2 * cut.size, length), low_type),
        ((2 * cut.size, length), wide),
        ((length, width), wide),
        ((length, width), low_type),
        ((length, width), wide),
        ((length, width), wide),
        ((length, width), wide),
        ((chunks_a, cut.part, half), low_type),
        ((4, cut.part, group), low_type),
    ]
    z = cut.row_size - 1
    semaphores = [dma(chunks), dma(chunks, z), dma(chunks, z), dma(chunks, 2), dma(chunks, 2), dma(chunks, 4), dma(chunks, 4)]
    semaphores += [dma(2 + 2 * blocks), dma(2 + 2 * blocks), dma(2), dma(len(kept))]
    return pl.pallas_call(
        partial(forward_kernel, cut),
        out_shape=like(kept),
        in_specs=[any_spec()] * 2 + [vmem_spec()] * (len(args) - 4) + [smem_spec()] * 4,
        out_specs=[any_spec()] * len(kept),
        scratch_shapes=scratch(kept) + scratch(own) + semaphores,
        compiler_params=pltpu.CompilerParams(collective_id=0, has_side_effects=True, vmem_limit_bytes=vmem_most),
        name="layer_forward",
    )(token_part, cot_part, *args)


def run_backward(cut, kept, *args):
    length, width, half = cut.length, cut.width, cut.part_width
    group = cut.units // 2
    pairs = cut.heads // 2
    blocks = length // cut.rows
    columns = [group] * 4 + [half] * (pairs + 1)
    count = len(columns)
    outs = [((length, half), wide), ((16, width), wide)] + [((cut.part, n), wide) for n in columns]
    loaded = [(item.shape, item.dtype) for item in kept]
    own = [
        ((length, width), wide),
        ((length, width), wide),
        ((length, half), low_type),
        ((length, half), low_type),
        ((length, half), low_type),
        ((length, half), low_type),
        ((length, 2 * cut.size), wide),
        ((length, 2 * cut.size), wide),
        ((2 * cut.size, length), wide),
        ((2 * cut.size, length), low_type),
        ((16, width), wide),
        ((2, 16, width), wide),
        ((2, 16, width), wide),
        ((cut.row_size, 16, width), wide),
        ((4, 8, width), wide),
        ((8, half), wide),
    ]
    quarter = cut.part * cut.row_size // 2
    own += [((width, n), low_type) for n in columns]
    own += [((2, 2, quarter, n), low_type) for n in columns]
    own += [((2, quarter, n), low_type) for n in columns]
    own += [((2, quarter, n), low_type) for n in columns]
    own += [((2 * quarter, n), low_type) for n in columns]
    own += [((cut.row_size - 1, cut.part, n), low_type) for n in columns]
    z = cut.row_size - 1
    semaphores = [dma(len(kept)), dma(count, 4), dma(count, 4), dma(count, 2), dma(count, 2), dma(count, z), dma(count, z)]
    semaphores += [dma(2 * blocks), dma(2 * blocks), dma(2 + z), dma(2 + z)]
    return pl.pallas_call(
        partial(backward_kernel, cut),
        out_shape=like(outs),
        in_specs=[any_spec()] * len(kept) + [vmem_spec()] * 3 + [smem_spec()] * 4,
        out_specs=[vmem_spec()] * len(outs),
        scratch_shapes=scratch(loaded) + scratch(own) + semaphores,
        compiler_params=pltpu.CompilerParams(collective_id=1, has_side_effects=True, vmem_limit_bytes=vmem_most),
        name="layer_backward",
    )(*kept, *args)


def fused_device(
    cut,
    tokens, cotangent, qkv_weight, out_weight, up_weight, down_weight, query_bias, value_bias, out_bias, up_bias,
    down_bias, first_gain, first_shift, second_gain, second_shift, head_gate, hidden_gate, intermediate_gate,
    attention_gate, feedforward_gate, prefix_length,
):
    half, width, units, part = cut.part_width, cut.width, cut.units, cut.part
    rows = [
        query_bias, value_bias, out_bias, up_bias, down_bias, first_gain, first_shift, second_gain, second_shift,
        hidden_gate, intermediate_gate,
    ]
    scalars = [head_gate, attention_gate, feedforward_gate, prefix_length]
    weights = [qkv_weight, out_weight.T, up_weight, down_weight.T]
    kept = list(run_forward(cut, tokens, cotangent, *weights, *rows, *scalars))
    layer_out = kept.pop(11)
    made = run_backward(cut, kept, rows[5], rows[9], rows[10], *scalars)
    grad_tokens, small = made[0], made[1]
    seq_total = lax.axis_size(("dp", "row"))
    lanes = [half, half, width, units, width, width, width, width, width, cut.heads, width, units, seq_total, seq_total]
    shapes = [(3, part, half), (part, half), (part, units), (part, units)] + [(n,) for n in lanes]
    outs = pl.pallas_call(
        partial(place_kernel, cut),
        out_shape=like([(shape, wide) for shape in shapes]),
        in_specs=[vmem_spec()] * (len(made) - 1),
        out_specs=[vmem_spec()] * len(shapes),
        name="place_results",
    )(small, *made[2:])
    return (layer_out, grad_tokens, outs[0], outs[1].T, outs[2], outs[3].T, *outs[4:])


def cut_of(args):
    tokens, qkv_weight, up_weight, head_gate, prefix_length = args[0], args[2], args[4], args[15], args[20]
    length, part_width = tokens.shape
    part, width = qkv_weight.shape[1], args[11].shape[0]
    heads = head_gate.shape[0]
    row_size, dp_size = lax.axis_size("row"), lax.axis_size("dp")
    fits = (
        prefix_length.shape[0] == 1
        and lax.axis_size("col") == 2
        and dp_size == 4
        and row_size % 2 == 0
        and part % 16 == 0
        and heads % 2 == 0
        and part_width == qkv_weight.shape[2]
        and part_width == 3 * (2 * part_width // heads)
        and (2 * part_width // heads) % 128 == 0
        and width % 256 == 0
        and length % 512 == 0
        and up_weight.shape[1] == 2 * width
    )
    if not fits:
        return None
    return Cut(
        length, width, part_width, heads, part_width // heads, up_weight.shape[1], part, row_size, 256, 128, length // 2
    )


def any_device(*args):
    cut = cut_of(args)
    return per_device(*args) if cut is None else fused_device(cut, *args)


def solution(mesh):
    placed = (
        P(("dp", "row"), "col"),
        P(("dp", "row"), "col"),
        P(None, ("dp", "row"), "col"),
        P("col", ("dp", "row")),
        P(("dp", "row"), "col"),
        P("col", ("dp", "row")),
        P("col"),
        P("col"),
        P(),
        P("col"),
        P(),
        P(),
        P(),
        P(),
        P(),
        P("col"),
        P(),
        P("col"),
        P(("dp", "row")),
        P(("dp", "row")),
        P(("dp", "row")),
    )
    return jax.shard_map(
        any_device,
        mesh=mesh,
        in_specs=placed,
        out_specs=(
            P(("dp", "row"), "col"),
            P(("dp", "row"), "col"),
            P(None, ("dp", "row"), "col"),
            P("col", ("dp", "row")),
            P(("dp", "row"), "col"),
            P("col", ("dp", "row")),
            P("col"),
            P("col"),
            P(),
            P("col"),
            P(),
            P(),
            P(),
            P(),
            P(),
            P("col"),
            P(),
            P("col"),
            P(),
            P(),
        ),
        check_vma=False,
    )
```

```python
from functools import partial
import math
from typing import NamedTuple

import jax
import jax.numpy as jnp
from jax import lax
from jax.experimental import pallas as pl
from jax.experimental.pallas import tpu as pltpu
from jax.sharding import PartitionSpec as P

masked_value = -1e30
norm_eps = 1e-05


def norm_forward(values, scale_gain, shift_term):
    centre = jnp.mean(values, axis=1, keepdims=True)
    centred = values - centre
    spread = jnp.mean(centred * centred, axis=1, keepdims=True)
    inverse = lax.rsqrt(spread + norm_eps)
    normed = centred * inverse
    return (normed * scale_gain + shift_term, normed, inverse)


def norm_backward(gradient, normed, inverse, scale_gain):
    scaled = gradient * scale_gain
    first_mean = jnp.mean(scaled, axis=1, keepdims=True)
    second_mean = jnp.mean(scaled * normed, axis=1, keepdims=True)
    return inverse * (scaled - first_mean - normed * second_mean)


def block_mask(start_row, block_rows, length, prefix_value):
    key_index = jnp.arange(length, dtype=jnp.int32)
    query_index = start_row + jnp.arange(block_rows, dtype=jnp.int32)
    return (key_index[None, :] < prefix_value) | (key_index[None, :] <= query_index[:, None])


def block_scores(query_block, key_seq, start_row, prefix_value, scale_factor):
    block_rows = query_block.shape[0]
    length = key_seq.shape[0]
    allowed = block_mask(start_row, block_rows, length, prefix_value)
    scores = (
        jnp.einsum("qhd,khd->hqk", query_block, key_seq, preferred_element_type=jnp.float32)
        * scale_factor
    )
    return jnp.where(allowed[None], scores, masked_value)


def attend_sequence(query_seq, key_seq, value_seq, prefix_value, block_rows, scale_factor):
    length = key_seq.shape[0]
    block_count = length // block_rows
    query_blocks = query_seq.reshape(
        block_count, block_rows, query_seq.shape[1], query_seq.shape[2]
    )
    starts = jnp.arange(block_count, dtype=jnp.int32) * block_rows

    def one_block(element):
        query_block, start_row = element
        scores = block_scores(query_block, key_seq, start_row, prefix_value, scale_factor)
        row_peak = jnp.max(scores, axis=2, keepdims=True)
        exponent = jnp.exp(scores - row_peak)
        row_total = jnp.sum(exponent, axis=2, keepdims=True)
        weights_low = (exponent / row_total).astype(jnp.bfloat16)
        context = jnp.einsum(
            "hqk,khd->qhd", weights_low, value_seq, preferred_element_type=jnp.float32
        )
        return (context, row_peak[..., 0] + jnp.log(row_total[..., 0]))

    contexts, log_totals = lax.map(one_block, (query_blocks, starts))
    return (contexts.reshape(length, query_seq.shape[1], query_seq.shape[2]), log_totals)


def attend_back(
    query_seq, key_seq, value_seq, grad_seq, log_seq, prefix_value, block_rows, scale_factor
):
    length = key_seq.shape[0]
    block_count = length // block_rows
    head_count = query_seq.shape[1]
    head_size = query_seq.shape[2]
    query_blocks = query_seq.reshape(block_count, block_rows, head_count, head_size)
    grad_blocks = grad_seq.reshape(block_count, block_rows, head_count, head_size)
    starts = jnp.arange(block_count, dtype=jnp.int32) * block_rows

    def one_block(running, element):
        grad_keys, grad_values = running
        query_block, grad_block, log_block, start_row = element
        scores = block_scores(query_block, key_seq, start_row, prefix_value, scale_factor)
        probs = jnp.exp(scores - log_block[..., None])
        grad_probs = jnp.einsum(
            "qhd,khd->hqk", grad_block, value_seq, preferred_element_type=jnp.float32
        )
        row_inner = jnp.sum(probs * grad_probs, axis=2, keepdims=True)
        grad_scores = (probs * (grad_probs - row_inner)).astype(jnp.bfloat16)
        grad_query = (
            jnp.einsum("hqk,khd->qhd", grad_scores, key_seq, preferred_element_type=jnp.float32)
            * scale_factor
        )
        grad_keys = (
            grad_keys
            + jnp.einsum(
                "hqk,qhd->khd", grad_scores, query_block, preferred_element_type=jnp.float32
            )
            * scale_factor
        )
        grad_values = grad_values + jnp.einsum(
            "hqk,qhd->khd",
            probs.astype(jnp.bfloat16),
            grad_block,
            preferred_element_type=jnp.float32,
        )
        return ((grad_keys, grad_values), grad_query)

    zeros_kv = jnp.zeros((length, head_count, head_size), jnp.float32)
    (grad_keys, grad_values), grad_query = lax.scan(
        one_block, (zeros_kv, zeros_kv), (query_blocks, grad_blocks, log_seq, starts)
    )
    return (grad_query.reshape(length, head_count, head_size), grad_keys, grad_values)


def per_device(
    tokens,
    cotangent,
    qkv_weight,
    out_weight,
    up_weight,
    down_weight,
    query_bias,
    value_bias,
    out_bias,
    up_bias,
    down_bias,
    first_gain,
    first_shift,
    second_gain,
    second_shift,
    head_gate,
    hidden_gate,
    intermediate_gate,
    attention_gate,
    feedforward_gate,
    prefix_length,
):
    row_count = tokens.shape[0]
    seq_count = prefix_length.shape[0]
    length = row_count // seq_count
    local_heads = head_gate.shape[0]
    head_width = qkv_weight.shape[2]
    head_size = head_width // local_heads
    model_width = first_gain.shape[0]
    part_width = model_width // lax.axis_size("col")
    block_rows = min(512, length)
    scale_factor = head_size ** (-0.5)
    col_index = lax.axis_index("col")
    qkv_low, out_low = (
        lax.all_gather(qkv_weight.astype(jnp.bfloat16), ("dp", "row"), axis=1, tiled=True),
        lax.all_gather(out_weight.astype(jnp.bfloat16), ("dp", "row"), axis=1, tiled=True),
    )
    up_low, down_low = (
        lax.all_gather(up_weight.astype(jnp.bfloat16), ("dp", "row"), axis=0, tiled=True),
        lax.all_gather(down_weight.astype(jnp.bfloat16), ("dp", "row"), axis=1, tiled=True),
    )
    token_full = lax.all_gather(tokens, "col", axis=1, tiled=True)
    projected = jnp.einsum("td,kdf->ktf", token_full, qkv_low, preferred_element_type=jnp.float32)
    query_low = (projected[0] + query_bias).astype(jnp.bfloat16)
    key_low = projected[1].astype(jnp.bfloat16)
    value_low = (projected[2] + value_bias).astype(jnp.bfloat16)

    def split_heads(array):
        return array.reshape(seq_count, length, local_heads, head_size)

    def forward_seq(element):
        query_seq, key_seq, value_seq, prefix_value = element
        return attend_sequence(
            query_seq, key_seq, value_seq, prefix_value, block_rows, scale_factor
        )

    contexts, log_totals = lax.map(
        forward_seq,
        (split_heads(query_low), split_heads(key_low), split_heads(value_low), prefix_length),
    )
    context = contexts.reshape(row_count, head_width)
    gate_columns = jnp.repeat(head_gate.astype(jnp.float32), head_size)
    gated_low = (context * gate_columns).astype(jnp.bfloat16)
    attn_terms = jnp.dot(gated_low, out_low, preferred_element_type=jnp.float32)
    attn_out = lax.psum(attn_terms, "col") + out_bias
    hidden_mask = hidden_gate.astype(jnp.float32)
    attn_rows = jnp.repeat(attention_gate.astype(jnp.float32), length)[:, None]
    dense_rows = jnp.repeat(feedforward_gate.astype(jnp.float32), length)[:, None]
    first_sum = token_full.astype(jnp.float32) + attn_rows * hidden_mask * attn_out
    normed_one, first_normed, first_inverse = norm_forward(first_sum, first_gain, first_shift)
    normed_low = normed_one.astype(jnp.bfloat16)
    pre_act = jnp.dot(normed_low, up_low, preferred_element_type=jnp.float32) + up_bias
    activated, gelu_pull = jax.vjp(partial(jax.nn.gelu, approximate=False), pre_act)
    unit_mask = intermediate_gate.astype(jnp.float32)
    inner_low = (activated * unit_mask).astype(jnp.bfloat16)
    dense_terms = jnp.dot(inner_low, down_low, preferred_element_type=jnp.float32)
    dense_out = lax.psum(dense_terms, "col") + down_bias
    second_sum = normed_one + dense_rows * hidden_mask * dense_out
    layer_full, second_normed, second_inverse = norm_forward(second_sum, second_gain, second_shift)
    layer_out = lax.dynamic_slice_in_dim(layer_full, col_index * part_width, part_width, 1)
    grad_full = lax.all_gather(cotangent, "col", axis=1, tiled=True).astype(jnp.float32)
    grad_gain_two = jnp.sum(grad_full * second_normed, axis=0)
    grad_shift_two = jnp.sum(grad_full, axis=0)
    grad_second = norm_backward(grad_full, second_normed, second_inverse, second_gain)
    grad_dense_low = (dense_rows * hidden_mask * grad_second).astype(jnp.bfloat16)
    dense_product = dense_out * grad_second
    grad_dense_gate = jnp.sum(
        dense_product.reshape(seq_count, length, model_width) * hidden_mask, axis=(1, 2)
    )
    hidden_from_dense = jnp.sum(dense_rows * dense_product, axis=0)
    grad_down_bias = jnp.sum(grad_dense_low.astype(jnp.float32), axis=0)
    up_low, down_low = (
        lax.all_gather(up_weight.astype(jnp.bfloat16), ("dp", "row"), axis=0, tiled=True),
        lax.all_gather(down_weight.astype(jnp.bfloat16), ("dp", "row"), axis=1, tiled=True),
    )
    grad_down = jnp.einsum(
        "tf,td->fd", inner_low, grad_dense_low, preferred_element_type=jnp.float32
    )
    grad_inner_low = jnp.einsum(
        "td,fd->tf", grad_dense_low, down_low, preferred_element_type=jnp.float32
    ).astype(jnp.bfloat16)
    grad_inner = grad_inner_low.astype(jnp.float32)
    grad_unit_gate = jnp.sum(activated * grad_inner, axis=0)
    (grad_pre,) = gelu_pull(unit_mask * grad_inner)
    grad_pre_low = grad_pre.astype(jnp.bfloat16)
    grad_up_bias = jnp.sum(grad_pre_low.astype(jnp.float32), axis=0)
    grad_up = jnp.einsum("td,tf->df", normed_low, grad_pre_low, preferred_element_type=jnp.float32)
    dense_parts = (
        lax.psum_scatter(grad_up, ("dp", "row"), scatter_dimension=0, tiled=True),
        lax.psum_scatter(grad_down, ("dp", "row"), scatter_dimension=1, tiled=True),
    )
    hidden_terms = jnp.einsum("tf,df->td", grad_pre_low, up_low, preferred_element_type=jnp.float32)
    grad_normed = grad_second + lax.psum(hidden_terms, "col")
    grad_gain_one = jnp.sum(grad_normed * first_normed, axis=0)
    grad_shift_one = jnp.sum(grad_normed, axis=0)
    grad_first = norm_backward(grad_normed, first_normed, first_inverse, first_gain)
    grad_attn_low = (attn_rows * hidden_mask * grad_first).astype(jnp.bfloat16)
    attn_product = attn_out * grad_first
    grad_attn_gate = jnp.sum(
        attn_product.reshape(seq_count, length, model_width) * hidden_mask, axis=(1, 2)
    )
    grad_hidden = hidden_from_dense + jnp.sum(attn_rows * attn_product, axis=0)
    grad_out_bias = jnp.sum(grad_attn_low.astype(jnp.float32), axis=0)
    qkv_low, out_low = (
        lax.all_gather(qkv_weight.astype(jnp.bfloat16), ("dp", "row"), axis=1, tiled=True),
        lax.all_gather(out_weight.astype(jnp.bfloat16), ("dp", "row"), axis=1, tiled=True),
    )
    grad_out = jnp.einsum("tc,td->cd", gated_low, grad_attn_low, preferred_element_type=jnp.float32)
    grad_gated_low = jnp.einsum(
        "td,cd->tc", grad_attn_low, out_low, preferred_element_type=jnp.float32
    ).astype(jnp.bfloat16)
    grad_head_cols = jnp.sum(context * grad_gated_low.astype(jnp.float32), axis=0)
    grad_head = jnp.sum(grad_head_cols.reshape(local_heads, head_size), axis=1)
    grad_context = grad_gated_low * gate_columns.astype(jnp.bfloat16)

    def backward_seq(element):
        query_seq, key_seq, value_seq, grad_seq, log_seq, prefix_value = element
        return attend_back(
            query_seq, key_seq, value_seq, grad_seq, log_seq, prefix_value, block_rows, scale_factor
        )

    grad_query, grad_keys, grad_values = lax.map(
        backward_seq,
        (
            split_heads(query_low),
            split_heads(key_low),
            split_heads(value_low),
            split_heads(grad_context),
            log_totals,
            prefix_length,
        ),
    )
    grad_qkv_low = jnp.stack([grad_query, grad_keys, grad_values]).reshape(3, row_count, head_width)
    grad_qkv_low = grad_qkv_low.astype(jnp.bfloat16)
    grad_query_bias = jnp.sum(grad_qkv_low[0].astype(jnp.float32), axis=0)
    grad_value_bias = jnp.sum(grad_qkv_low[2].astype(jnp.float32), axis=0)
    grad_qkv = jnp.einsum(
        "td,ktf->kdf", token_full, grad_qkv_low, preferred_element_type=jnp.float32
    )
    input_terms = jnp.einsum(
        "ktf,kdf->td", grad_qkv_low, qkv_low, preferred_element_type=jnp.float32
    )
    grad_tokens = lax.psum_scatter(
        input_terms.astype(jnp.bfloat16), "col", scatter_dimension=1, tiled=True
    ).astype(jnp.float32)
    grad_tokens = grad_tokens + lax.dynamic_slice_in_dim(
        grad_first, col_index * part_width, part_width, 1
    )
    grad_up_part, grad_down_part = dense_parts
    grad_qkv_part, grad_out_part = (
        lax.psum_scatter(grad_qkv, ("dp", "row"), scatter_dimension=1, tiled=True),
        lax.psum_scatter(grad_out, ("dp", "row"), scatter_dimension=1, tiled=True),
    )
    seq_total = seq_count * lax.axis_size(("dp", "row"))
    seq_start = lax.axis_index(("dp", "row")) * seq_count
    seq_stack = lax.dynamic_update_slice_in_dim(
        jnp.zeros((2, seq_total), jnp.float32),
        jnp.stack([grad_attn_gate, grad_dense_gate]),
        seq_start,
        1,
    )
    full_stack = jnp.stack(
        [
            grad_out_bias,
            grad_down_bias,
            grad_gain_one,
            grad_shift_one,
            grad_gain_two,
            grad_shift_two,
            grad_hidden,
        ]
    )
    half_stack = jnp.stack([grad_query_bias, grad_value_bias])
    unit_stack = jnp.stack([grad_up_bias, grad_unit_gate])
    full_sum, half_sum, unit_sum, head_sum, seq_sum = lax.psum(
        (full_stack, half_stack, unit_stack, grad_head, seq_stack), ("dp", "row")
    )
    return (
        layer_out,
        grad_tokens,
        grad_qkv_part,
        grad_out_part,
        grad_up_part,
        grad_down_part,
        half_sum[0],
        half_sum[1],
        full_sum[0],
        unit_sum[0],
        full_sum[1],
        full_sum[2],
        full_sum[3],
        full_sum[4],
        full_sum[5],
        head_sum,
        full_sum[6],
        unit_sum[1],
        seq_sum[0],
        seq_sum[1],
    )


low_type = jnp.bfloat16
wide = jnp.float32
mesh_ids = pl.DeviceIdType.MESH


def dot_nn(left, right):
    return jnp.dot(left, right, preferred_element_type=wide)


def dot_nt(left, right):
    return lax.dot_general(left, right, (((1,), (1,)), ((), ())), preferred_element_type=wide)


def rows_at(index, count):
    return pl.ds(pl.multiple_of(index * count, count), count)


def fold_rows(values):
    return jnp.sum(values.reshape(values.shape[0] // 8, 8, values.shape[1]), axis=0)


def norm_parts(values):
    centre = jnp.mean(values, axis=1, keepdims=True)
    centred = values - centre
    spread = jnp.mean(centred * centred, axis=1, keepdims=True)
    inverse = lax.rsqrt(spread + norm_eps)
    return centred * inverse, inverse


class Place:
    def __init__(self, row_size):
        self.dp, self.row, self.col = (lax.axis_index(name) for name in ("dp", "row", "col"))
        self.row_size = row_size
        self.x, self.y = lax.rem(self.dp, 2), self.dp // 2
        self.x_dp = self.y * 2 + (1 - self.x)
        self.y_dp = (1 - self.y) * 2 + self.x

    def x_mate(self):
        return {"dp": self.x_dp}

    def y_mate(self):
        return {"dp": self.y_dp}

    def row_mate(self, step):
        return {"row": lax.rem(self.row + step, self.row_size)}

    def col_mate(self):
        return {"col": 1 - self.col}

    def barrier(self):
        semaphore = pltpu.get_barrier_semaphore()
        mates = [self.x_mate(), self.y_mate(), self.col_mate()]
        mates += [self.row_mate(step) for step in range(1, self.row_size)]
        for mate in mates:
            pl.semaphore_signal(semaphore, inc=1, device_id=mate, device_id_type=mesh_ids)
        pl.semaphore_wait(semaphore, len(mates))


def send(source, target, semaphores, index, mate):
    sent, received = semaphores
    return pltpu.make_async_remote_copy(
        src_ref=source,
        dst_ref=target,
        send_sem=sent.at[index],
        recv_sem=received.at[index],
        device_id=mate,
        device_id_type=mesh_ids,
    )


class Gather:
    def __init__(self, place, shards, chunks, order, own_sem, z_sems, two_sems, three_sems):
        self.place, self.shards, self.chunks = place, shards, chunks
        self.own_sem, self.z_sems, self.two_sems, self.three_sems = own_sem, z_sems, two_sems, three_sems
        self.part = shards[0].shape[0]
        self.block = self.part * place.row_size
        self.half = self.block // 2
        self.steps, self.done = order, 0

    def half_rows(self, dp, half):
        return pl.ds(pl.multiple_of(dp * self.block + half * self.half, 16), self.half)

    def own_rows(self):
        place = self.place
        return pl.ds(pl.multiple_of(place.dp * self.block + place.row * self.part, 16), self.part)

    def own(self, c):
        return pltpu.make_async_copy(self.shards[c], self.chunks[c].at[self.own_rows()], self.own_sem.at[c])

    def along_z(self, c):
        place = self.place
        return [
            send(
                self.shards[c], self.chunks[c].at[self.own_rows()], self.z_sems, (c, step - 1), place.row_mate(step)
            )
            for step in range(1, place.row_size)
        ]

    def pass_on(self, c, dp, half, sems, index, mate):
        at = self.chunks[c].at[self.half_rows(dp, half)]
        return send(at, at, sems, (c, index), mate)

    def second(self, c):
        place = self.place
        return [
            self.pass_on(c, place.dp, 0, self.two_sems, 0, place.x_mate()),
            self.pass_on(c, place.dp, 1, self.two_sems, 1, place.y_mate()),
        ]

    def third(self, c):
        place = self.place
        return [
            self.pass_on(c, place.dp, 0, self.three_sems, 0, place.y_mate()),
            self.pass_on(c, place.dp, 1, self.three_sems, 2, place.x_mate()),
            self.pass_on(c, place.x_dp, 0, self.three_sems, 1, place.y_mate()),
            self.pass_on(c, place.y_dp, 1, self.three_sems, 3, place.x_mate()),
        ]

    def start(self, c):
        self.own(c).start()
        for copy in self.along_z(c):
            copy.start()

    def step(self):
        stage, c = self.steps[self.done]
        self.done += 1
        if stage == 0:
            self.own(c).wait()
            for copy in self.along_z(c):
                copy.wait_recv()
            for copy in self.second(c):
                copy.start()
        elif stage == 1:
            for copy in self.second(c):
                copy.wait_recv()
            for copy in self.third(c):
                copy.start()
        else:
            for copy in self.third(c):
                copy.wait_recv()

    def advance(self, count):
        for _ in range(count):
            if self.done < len(self.steps):
                self.step()

    def need(self, c):
        while self.done <= self.steps.index((2, c)):
            self.step()

    def finish(self):
        self.advance(len(self.steps))
        for c in range(len(self.chunks)):
            for copy in self.along_z(c) + self.second(c) + self.third(c):
                copy.wait_send()


class Scatter:
    def __init__(self, place, chunks, outs, order, first, mid_send, mid, last_send, last, one_sems, two_sems, z_sems):
        self.place, self.chunks, self.outs = place, chunks, outs
        self.first, self.mid_send, self.mid, self.last_send, self.last = first, mid_send, mid, last_send, last
        self.one_sems, self.two_sems, self.z_sems = one_sems, two_sems, z_sems
        self.part = outs[0].shape[0]
        self.block = self.part * place.row_size
        self.half = self.block // 2
        self.count = len(chunks)
        self.steps, self.done, self.begun = order, 0, []

    def half_rows(self, dp, half):
        return pl.ds(pl.multiple_of(dp * self.block + half * self.half, 16), self.half)

    def one(self, c):
        place, chunk, first = self.place, self.chunks[c], self.first[c]
        found = []
        for i in range(2):
            rows = self.half_rows((1 - place.y) * 2 + i, 0)
            found.append(send(chunk.at[rows], first.at[0, i], self.one_sems, (c, i), place.y_mate()))
            rows = self.half_rows(i * 2 + (1 - place.x), 1)
            found.append(send(chunk.at[rows], first.at[1, i], self.one_sems, (c, 2 + i), place.x_mate()))
        return found

    def two(self, c):
        place, mid_send, mid = self.place, self.mid_send[c], self.mid[c]
        return [
            send(mid_send.at[0], mid.at[0], self.two_sems, (c, 0), place.x_mate()),
            send(mid_send.at[1], mid.at[1], self.two_sems, (c, 1), place.y_mate()),
        ]

    def along_z(self, c):
        place = self.place
        found = []
        for step in range(1, place.row_size):
            mate = lax.rem(place.row + step, place.row_size)
            rows = pl.ds(pl.multiple_of(mate * self.part, 16), self.part)
            found.append(
                send(
                    self.last_send[c].at[rows], self.last[c].at[step - 1], self.z_sems, (c, step - 1),
                    place.row_mate(step),
                )
            )
        return found

    def begin(self, c):
        self.begun.append(c)
        for copy in self.one(c):
            copy.start()

    def step(self):
        stage, c = self.steps[self.done]
        self.done += 1
        place, chunk = self.place, self.chunks[c]
        first, mid_send, mid = self.first[c], self.mid_send[c], self.mid[c]
        last_send, last = self.last_send[c], self.last[c]
        if stage == 0:
            for copy in self.one(c):
                copy.wait_recv()
            mid_send[0] = (
                chunk[self.half_rows(place.x_dp, 0), :].astype(wide) + first[0, 1 - place.x].astype(wide)
            ).astype(low_type)
            mid_send[1] = (
                chunk[self.half_rows(place.y_dp, 1), :].astype(wide) + first[1, 1 - place.y].astype(wide)
            ).astype(low_type)
            for copy in self.two(c):
                copy.start()
        elif stage == 1:
            for copy in self.two(c):
                copy.wait_recv()
            for half, slot in ((0, place.x), (1, place.y)):
                last_send[pl.ds(half * self.half, self.half), :] = (
                    chunk[self.half_rows(place.dp, half), :].astype(wide)
                    + first[half, slot].astype(wide)
                    + mid[half].astype(wide)
                ).astype(low_type)
            for copy in self.along_z(c):
                copy.start()
        else:
            total = last_send[pl.ds(pl.multiple_of(place.row * self.part, 16), self.part), :].astype(wide)
            for step, copy in enumerate(self.along_z(c)):
                copy.wait_recv()
                total = total + last[step].astype(wide)
            self.outs[c][...] = total

    def advance(self, count):
        for _ in range(count):
            if self.done < len(self.steps) and self.steps[self.done][1] in self.begun:
                self.step()

    def finish(self):
        self.advance(len(self.steps))
        for c in range(self.count):
            for copy in self.one(c) + self.two(c) + self.along_z(c):
                copy.wait_send()


def masked_tile(tile, query_start, key_start, prefix):
    key_index = key_start + lax.broadcasted_iota(jnp.int32, tile.shape, 0)
    query_index = query_start + lax.broadcasted_iota(jnp.int32, tile.shape, 1)
    return jnp.where((key_index < prefix) | (key_index <= query_index), tile, masked_value)


def key_tiles(block, rows, prefix_most):
    count = max((block + 1) * rows, prefix_most) // rows
    return [(tile, tile >= block) for tile in range(count)]


def flat_row(ref):
    return ref[...].reshape(1, ref.shape[0])


def gate_row(gates, heads, size):
    head = lax.broadcasted_iota(jnp.int32, (1, heads * size), 1) // size
    row = jnp.zeros((1, heads * size), wide)
    for h in range(heads):
        row = jnp.where(head == h, gates[h].astype(wide), row)
    return row


def layer_kernel(
    cut,
    token_part, cot_part, qkv_w, out_w, up_w, down_w, query_bias, value_bias, out_bias, up_bias, down_bias,
    first_gain, first_shift, second_gain, second_shift, hidden_gate, unit_gate,
    head_gate, attention_gate, feedforward_gate, prefix_length,
    layer_out, token_out, small_out, *rest,
):
    length, width, heads, size = cut.length, cut.width, cut.heads, cut.size
    part, rows, fine = cut.part_width, cut.rows, cut.fine
    blocks = length // rows
    own_count = blocks // 2
    pair = 2 * size
    pairs = heads // 2
    count = pairs + 5
    rest = list(rest)

    def take(number):
        taken = rest[:number]
        del rest[:number]
        return taken

    grads = take(count)
    (wa, wm, token, token_t, qkv, lse, ctx, attn_out, normed_t, gelu, slope, second, low, dense_t, sums) = take(15)
    (cot, total, arrive_a, arrive_b, stage, token_recv, ctx_grad, triple, key_grad, value_grad) = take(10)
    (pair_wide, pair_low, shards_a, shards_m) = take(4)
    (small, small_c, small_x, small_y, small_z, unit_sums, head_sums) = take(7)
    buffers, first, mid_send, mid, last_send, last = (take(count) for _ in range(6))
    (own_sem, gz_s, gz_r, g2_s, g2_r, g3_s, g3_r, half_sem, out_sem, s1_s, s1_r, s2_s, s2_r, sz_s, sz_r) = take(15)
    (col_s, col_r, small_s, small_r) = take(4)
    group = wm.shape[2]
    place = Place(cut.row_size)
    for p in range(pairs):
        for k in range(3):
            shards_a[p, :, k * pair : (k + 1) * pair] = qkv_w[k, :, p * pair : (p + 1) * pair].astype(low_type)
    shards_a[pairs] = out_w[...].astype(low_type)
    for j in range(2):
        shards_m[2 * j] = up_w[:, j * group : (j + 1) * group].astype(low_type)
        shards_m[2 * j + 1] = down_w[:, j * group : (j + 1) * group].astype(low_type)
    place.barrier()
    prefix = prefix_length[0]
    attn_gate, dense_gate = attention_gate[0].astype(wide), feedforward_gate[0].astype(wide)
    hidden, unit_row = flat_row(hidden_gate).astype(wide), flat_row(unit_gate).astype(wide)
    query_bias, value_bias, up_bias, out_bias, down_bias, first_gain, first_shift, second_gain, second_shift = (
        flat_row(ref)
        for ref in (
            query_bias, value_bias, up_bias, out_bias, down_bias, first_gain, first_shift, second_gain, second_shift
        )
    )
    chunks = [wa.at[i] for i in range(pairs + 1)] + [wm.at[i] for i in range(4)]
    shards = [shards_a.at[i] for i in range(pairs + 1)] + [shards_m.at[i] for i in range(4)]
    gather = Gather(
        place, shards, chunks, gather_order(count), own_sem, (gz_s, gz_r), (g2_s, g2_r), (g3_s, g3_r)
    )
    scatter = Scatter(
        place, buffers, grads, scatter_order(pairs), first, mid_send, mid, last_send, last,
        (s1_s, s1_r), (s2_s, s2_r), (sz_s, sz_r),
    )

    def to_mate(source, target, index):
        return send(source, target, (col_s, col_r), index, place.col_mate())

    def own_block(i):
        return rows_at(place.col * own_count + i, rows)

    def mate_block(i):
        return rows_at((1 - place.col) * own_count + i, rows)

    def near(i):
        return pl.ds(i * rows, rows) if isinstance(i, int) else rows_at(i, rows)

    def mate_first(t):
        return lax.rem((1 - place.col) * own_count + t, blocks)

    own_cols = pl.ds(pl.multiple_of(place.col * part, 128), part)
    own_half = pl.ds(pl.multiple_of(place.col * (length // 2), rows), length // 2)
    mate_half = pl.ds(pl.multiple_of((1 - place.col) * (length // 2), rows), length // 2)
    token_own = pltpu.make_async_copy(token_part, token.at[:, own_cols], half_sem.at[0])
    token_sent = to_mate(token_part, token.at[:, own_cols], 0)
    cot_own = pltpu.make_async_copy(cot_part.at[own_half], cot.at[:, own_cols], half_sem.at[1])
    cot_sent = to_mate(cot_part.at[mate_half], cot.at[:, own_cols], 1)

    def attn_swap(i):
        return to_mate(total.at[mate_block(i)], arrive_a.at[near(i)], 2 + i)

    def normed_swap(i):
        return to_mate(low.at[own_block(i)], low.at[own_block(i)], 2 + own_count + i)

    def dense_swap(i):
        return to_mate(total.at[mate_block(i)], arrive_b.at[near(i)], 2 + 2 * own_count + i)

    def grad_swap(i):
        return to_mate(low.at[own_block(i)], low.at[own_block(i)], 2 + 3 * own_count + i)

    def hidden_swap(i):
        return to_mate(total.at[mate_block(i)], arrive_a.at[near(i)], 2 + 4 * own_count + i)

    def attn_grad_swap(i):
        return to_mate(low.at[own_block(i)], low.at[own_block(i)], 2 + 5 * own_count + i)

    def layer_swap(i):
        return to_mate(stage.at[1, near(i)], layer_out.at[own_block(i)], 2 + 6 * own_count + i)

    def token_swap(b):
        return to_mate(total.at[near(b), pl.ds(0, part)], token_recv.at[near(b)], 2 + 7 * own_count + b)

    small_swap = 2 + 7 * own_count + blocks

    def layer_put(i):
        return pltpu.make_async_copy(stage.at[0, near(i)], layer_out.at[own_block(i)], out_sem.at[i])

    gather.start(0)
    for copy in (token_own, token_sent, cot_own, cot_sent):
        copy.start()
    for c in range(1, count):
        gather.start(c)
    sums[...] = jnp.zeros_like(sums)
    unit_sums[...] = jnp.zeros_like(unit_sums)
    head_sums[...] = jnp.zeros_like(head_sums)
    token_own.wait()
    token_sent.wait_recv()

    @pl.loop(0, blocks)
    def _(b):
        at = rows_at(b, rows)
        token_t[:, at] = token[at, :].T

    value_t, ctx_t = pair_low, pair_wide
    lane_head = lax.broadcasted_iota(jnp.int32, (1, pair), 1) // size
    for p in range(pairs):
        gather.need(p)
        query_row = query_bias[:, p * pair : (p + 1) * pair]
        bias = jnp.concatenate(
            [query_row, jnp.zeros_like(query_row), value_bias[:, p * pair : (p + 1) * pair]], axis=1
        )

        @pl.loop(0, blocks)
        def _(b, p=p, bias=bias):
            at = rows_at(b, rows)
            made = dot_nn(token[at, :], wa[p]) + bias
            qkv[p, at, :] = made.astype(low_type)
            value_t[:, at] = made[:, 2 * pair :].T.astype(low_type)

        pace = gather_pace[min(p, len(gather_pace) - 2)]
        gather.advance(pace[0])

        @pl.loop(0, 2)
        def _(h, p=p, pace=pace):
            own = jnp.where(lane_head == h, size ** (-0.5), 0.0).astype(low_type)
            head_rows = rows_at(h, size)
            for b in range(blocks):
                query = qkv[p, b * rows : (b + 1) * rows, :pair] * own
                tiles, masked = [], key_tiles(b, rows, cut.prefix_most)
                for tile, needs in masked:
                    score = dot_nt(qkv[p, tile * rows : (tile + 1) * rows, pair : 2 * pair], query)
                    tiles.append(masked_tile(score, b * rows, tile * rows, prefix) if needs else score)
                peak = tiles[0].max(axis=0, keepdims=True)
                for score in tiles[1:]:
                    peak = jnp.maximum(peak, score.max(axis=0, keepdims=True))
                row_total = jnp.zeros_like(peak)
                weights = []
                for score in tiles:
                    weights.append(jnp.exp(score - peak))
                    row_total = row_total + weights[-1].sum(axis=0, keepdims=True)
                share = 1.0 / row_total
                found = jnp.zeros((size, rows), wide)
                for (tile, _), weight in zip(masked, weights):
                    found = found + dot_nn(
                        value_t[head_rows, tile * rows : (tile + 1) * rows], (weight * share).astype(low_type)
                    )
                ctx_t[head_rows, b * rows : (b + 1) * rows] = found
                lse[2 * p + h, :, b * rows : (b + 1) * rows] = peak + jnp.log(row_total)
                for now in range(2):
                    if b % 2 and pace[1 + 2 * now + b // 2]:

                        @pl.when(h == now)
                        def _():
                            gather.advance(pace[1 + 2 * now + b // 2])

        @pl.loop(0, blocks)
        def _(b, p=p):
            at = rows_at(b, rows)
            ctx[at, p * pair : (p + 1) * pair] = ctx_t[:, at].T.astype(low_type)

    gather.need(pairs)
    gate_columns = gate_row(head_gate, heads, size)
    gate_low = gate_columns.astype(low_type)

    @pl.loop(0, blocks)
    def _(t):
        at = rows_at(mate_first(t), rows)
        total[at, :] = dot_nt(ctx[at, :] * gate_low, wa[pairs])

        @pl.when(t < own_count)
        def _():
            attn_swap(t).start()

    gather.advance(gather_pace[-1][0])
    gate_cols = attn_gate * hidden
    for i in range(own_count):
        attn_swap(i).wait_recv()

        @pl.loop(i * rows // fine, (i + 1) * rows // fine)
        def _(k):
            here = rows_at(k, fine)
            at = pl.ds(pl.multiple_of(place.col * (length // 2) + k * fine, fine), fine)
            attn = total[at, :] + arrive_a[here, :] + out_bias
            attn_out[here, :] = attn
            normed, _ = norm_parts(token[at, :].astype(wide) + gate_cols * attn)
            out = normed * first_gain + first_shift
            second[here, :] = out
            low[at, :] = out.astype(low_type)

        normed_swap(i).start()
    gather.advance(gather_pace[-1][1])

    masks = [unit_row[:, j * group : (j + 1) * group] for j in range(2)]
    for j in range(2):
        gather.need(pairs + 1 + 2 * j)
        bias_row = up_bias[:, j * group : (j + 1) * group]

        @pl.loop(0, blocks)
        def _(t, j=j, bias_row=bias_row):
            at = rows_at(lax.rem(place.col * own_count + t, blocks), rows)
            if j == 0:

                @pl.when(t == own_count)
                def _():
                    for i in range(own_count):
                        normed_swap(i).wait_recv()

            pre = dot_nn(low[at, :], wm[2 * j]) + bias_row
            share = 0.5 * (1.0 + lax.erf(pre * (2.0 ** -0.5)))
            gelu[j, at, :] = (pre * share).astype(low_type)
            density = jnp.exp(-0.5 * pre * pre) * ((2.0 * math.pi) ** -0.5)
            slope[j, at, :] = (share + pre * density).astype(low_type)
            if j == 0:
                normed_t[:, at] = low[at, :].T

        if j == 0:
            for i in range(own_count):
                attn_swap(i).wait_send()
                normed_swap(i).wait_send()
        gather.need(pairs + 2 + 2 * j)

        @pl.loop(0, blocks)
        def _(t, j=j):
            at = rows_at(mate_first(t), rows)
            made = dot_nt(gelu[j, at, :] * masks[j].astype(low_type), wm[2 * j + 1])
            if j == 0:
                total[at, :] = made
            else:
                total[at, :] += made

                @pl.when(t < own_count)
                def _():
                    dense_swap(t).start()

    cot_own.wait()
    cot_sent.wait_recv()
    for i in range(own_count):
        dense_swap(i).wait_recv()

        @pl.loop(i * rows // fine, (i + 1) * rows // fine)
        def _(k):
            here = rows_at(k, fine)
            at = pl.ds(pl.multiple_of(place.col * (length // 2) + k * fine, fine), fine)
            dense = total[at, :] + arrive_b[here, :] + down_bias
            normed, inverse = norm_parts(second[here, :] + dense_gate * hidden * dense)
            full = normed * second_gain + second_shift
            stage[0, here, :] = jnp.where(place.col == 0, full[:, :part], full[:, part:])
            stage[1, here, :] = jnp.where(place.col == 0, full[:, part:], full[:, :part])
            grad = cot[here, :].astype(wide)
            scaled = grad * second_gain
            one = jnp.mean(scaled, axis=1, keepdims=True)
            two = jnp.mean(scaled * normed, axis=1, keepdims=True)
            made = inverse * (scaled - one - normed * two)
            second[here, :] = made
            gated = (dense_gate * hidden * made).astype(low_type)
            low[at, :] = gated
            sums[0] += fold_rows(grad * normed)
            sums[1] += fold_rows(grad)
            sums[2] += fold_rows(gated.astype(wide))
            sums[3] += fold_rows(dense * made)

        grad_swap(i).start()
        dense_t[:, own_block(i)] = low[own_block(i), :].T
    for i in range(own_count):
        layer_swap(i).start()
        layer_put(i).start()
        grad_swap(i).wait_recv()
        dense_t[:, mate_block(i)] = low[mate_block(i), :].T

    def product(target, left, right, mask=None):
        @pl.loop(0, width // rows)
        def _(i):
            at = rows_at(i, rows)
            made = dot_nn(left[at, :], right[...])
            target[at, :] = (made if mask is None else made * mask).astype(low_type)

    for j in range(2):
        product(buffers[j], dense_t, gelu.at[j], masks[j])
        scatter.begin(j)
    for i in range(own_count):
        dense_swap(i).wait_send()
    for j in range(2):

        @pl.loop(0, blocks)
        def _(t, j=j):
            at = rows_at(mate_first(t), rows)
            inner = dot_nn(low[at, :], wm[2 * j + 1]).astype(low_type).astype(wide)
            unit_sums[2 + j] += fold_rows(gelu[j, at, :].astype(wide) * inner)
            pre = (masks[j] * inner * slope[j, at, :].astype(wide)).astype(low_type)
            slope[j, at, :] = pre
            unit_sums[j] += fold_rows(pre.astype(wide))
            made = dot_nt(pre, wm[2 * j])
            if j == 0:
                total[at, :] = made
            else:
                total[at, :] += made

                @pl.when(t < own_count)
                def _():
                    hidden_swap(t).start()

        scatter.advance(scatter_pace[0][j])
        product(buffers[2 + j], normed_t, slope.at[j])
        scatter.begin(2 + j)

    for i in range(own_count):
        grad_swap(i).wait_send()
    for i in range(own_count):
        hidden_swap(i).wait_recv()

        @pl.loop(i * rows // fine, (i + 1) * rows // fine)
        def _(k):
            here = rows_at(k, fine)
            at = pl.ds(pl.multiple_of(place.col * (length // 2) + k * fine, fine), fine)
            attn = attn_out[here, :]
            normed, inverse = norm_parts(token[at, :].astype(wide) + gate_cols * attn)
            grad = second[here, :] + (total[at, :] + arrive_a[here, :])
            scaled = grad * first_gain
            one = jnp.mean(scaled, axis=1, keepdims=True)
            two = jnp.mean(scaled * normed, axis=1, keepdims=True)
            made = inverse * (scaled - one - normed * two)
            second[here, :] = made
            gated = (gate_cols * made).astype(low_type)
            low[at, :] = gated
            sums[4] += fold_rows(grad * normed)
            sums[5] += fold_rows(grad)
            sums[6] += fold_rows(gated.astype(wide))
            sums[7] += fold_rows(attn * made)

        attn_grad_swap(i).start()
        dense_t[:, own_block(i)] = low[own_block(i), :].T
        scatter.advance(scatter_pace[1][i])
    for i in range(own_count):
        attn_grad_swap(i).wait_recv()
        dense_t[:, mate_block(i)] = low[mate_block(i), :].T

    @pl.loop(0, blocks)
    def _(b):
        at = rows_at(b, rows)
        gated = dot_nn(low[at, :], wa[pairs]).astype(low_type).astype(wide)
        seen = ctx[at, :].astype(wide)
        head_sums[...] += fold_rows(seen * gated)
        ctx_grad[at, :] = (gated * gate_columns).astype(low_type)
        ctx[at, :] = (seen * gate_columns).astype(low_type)

    product(buffers[4], dense_t, ctx)
    scatter.begin(4)
    scatter.advance(scatter_pace[2][0])
    for i in range(own_count):
        hidden_swap(i).wait_send()
        layer_put(i).wait()
        layer_swap(i).wait()
    key_t, query_t = pair_low, pair_wide
    bias_sums = []
    for p in range(pairs):

        @pl.loop(0, blocks)
        def _(b, p=p):
            at = rows_at(b, rows)
            key_t[:, at] = qkv[p, at, pair : 2 * pair].astype(wide).T.astype(low_type)

        key_grad[...] = jnp.zeros_like(key_grad)
        value_grad[...] = jnp.zeros_like(value_grad)
        pace = scatter_pace[3 + min(p, len(scatter_pace) - 4)]

        @pl.loop(0, 2)
        def _(h, p=p, pace=pace):
            own = jnp.where(lane_head == h, size ** (-0.5), 0.0).astype(low_type)
            one_head = jnp.where(lane_head == h, 1.0, 0.0).astype(low_type)
            head_rows = rows_at(h, size)
            for b in range(blocks):
                query = qkv[p, b * rows : (b + 1) * rows, :pair] * own
                context = ctx_grad[b * rows : (b + 1) * rows, p * pair : (p + 1) * pair] * one_head
                logs = lse[2 * p + h, :, b * rows : (b + 1) * rows]
                inner = jnp.zeros_like(logs)
                kept, masked = [], key_tiles(b, rows, cut.prefix_most)
                for tile, needs in masked:
                    score = dot_nt(qkv[p, tile * rows : (tile + 1) * rows, pair : 2 * pair], query)
                    score = masked_tile(score, b * rows, tile * rows, prefix) if needs else score
                    prob = jnp.exp(score - logs)
                    grad_prob = dot_nt(qkv[p, tile * rows : (tile + 1) * rows, 2 * pair :], context)
                    inner = inner + (prob * grad_prob).sum(axis=0, keepdims=True)
                    kept.append((prob, grad_prob))
                found = jnp.zeros((size, rows), wide)
                for (tile, _), (prob, grad_prob) in zip(masked, kept):
                    at = slice(tile * rows, (tile + 1) * rows)
                    grad_score = (prob * (grad_prob - inner)).astype(low_type)
                    value_grad[at, :] += dot_nn(prob.astype(low_type), context)
                    key_grad[at, :] += dot_nn(grad_score, query)
                    found = found + dot_nn(key_t[head_rows, at], grad_score)
                query_t[head_rows, b * rows : (b + 1) * rows] = found * size ** (-0.5)
                for now in range(2):
                    if b % 2 and pace[2 * now + b // 2]:

                        @pl.when(h == now)
                        def _():
                            scatter.advance(pace[2 * now + b // 2])

        query_sum = jnp.zeros((8, pair), wide)
        value_sum = jnp.zeros((8, pair), wide)
        for b in range(blocks):
            at = pl.ds(b * rows, rows)
            query_low = query_t[:, at].T.astype(low_type)
            value_low = value_grad[at, :].astype(low_type)
            triple[at, :pair] = query_low
            triple[at, pair : 2 * pair] = key_grad[at, :].astype(low_type)
            triple[at, 2 * pair :] = value_low
            query_sum += fold_rows(query_low.astype(wide))
            value_sum += fold_rows(value_low.astype(wide))
        bias_sums.append((query_sum, value_sum))
        product(buffers[5 + p], token_t, triple)
        scatter.begin(5 + p)
        scatter.advance(pace[4])

        @pl.loop(0, blocks)
        def _(t, p=p):
            b = mate_first(t)
            at = rows_at(b, rows)
            made = dot_nt(triple[at, :], wa[p])
            if p > 0:
                made = total[at, :] + made
            if p < pairs - 1:
                total[at, :] = made
            else:
                kept = second[rows_at(lax.rem(t, own_count), rows), :]
                made = made + jnp.where(t >= own_count, kept, 0.0)
                total[at, :part] = jnp.where(place.col == 0, made[:, part:], made[:, :part])
                total[at, part:] = jnp.where(place.col == 0, made[:, :part], made[:, part:])
                token_swap(b).start()

    def whole(values):
        return jnp.sum(values, axis=0, keepdims=True)

    dense_col, attn_col = whole(sums[3]), whole(sums[7])
    seq_lane = lax.broadcasted_iota(jnp.int32, (1, width), 1)
    here = place.dp * place.row_size + place.row
    dense_all = jnp.sum(dense_col * hidden, axis=1, keepdims=True)
    attn_all = jnp.sum(attn_col * hidden, axis=1, keepdims=True)
    seq_row = jnp.where(seq_lane == here, attn_all, 0.0) + jnp.where(seq_lane == here + width // 2, dense_all, 0.0)
    small[0:1, :] = whole(sums[6])
    small[1:2, :] = whole(sums[2])
    small[2:3, :] = whole(sums[4])
    small[3:4, :] = whole(sums[5])
    small[4:5, :] = whole(sums[0])
    small[5:6, :] = whole(sums[1])
    small[6:7, :] = dense_gate * dense_col + attn_gate * attn_col
    small[7:8, :] = seq_row
    for j in range(4):
        small[8 + j : 9 + j, :] = whole(unit_sums[j])
    for p in range(pairs):
        small[12:13, p * pair : (p + 1) * pair] = whole(bias_sums[p][0])
        small[12:13, part + p * pair : part + (p + 1) * pair] = whole(bias_sums[p][1])
    small[13:14, :part] = whole(head_sums[...])
    small[13:14, part:] = jnp.zeros((1, part), wide)
    small[14:16, :] = jnp.zeros((2, width), wide)
    copy_c = to_mate(small.at[pl.ds(0, 8)], small_c.at[0, pl.ds(0, 8)], small_swap)
    copy_c.start()
    copy_c.wait_recv()
    small_c[1, 0:8, :] = small[0:8, :] + small_c[0, 0:8, :]
    small_c[1, 8:16, :] = small[8:16, :]
    copy_x = send(small_c.at[1], small_x.at[0], (small_s, small_r), 0, place.x_mate())
    copy_x.start()
    scatter.advance(1)
    copy_x.wait_recv()
    small_x[1] = small_c[1] + small_x[0]
    copy_y = send(small_x.at[1], small_y.at[0], (small_s, small_r), 1, place.y_mate())
    copy_y.start()
    scatter.advance(1)
    copy_y.wait_recv()
    mine = small_x[1] + small_y[0]
    small_y[1] = mine
    small_z[place.row] = mine
    copies = [
        send(small_y.at[1], small_z.at[place.row], (small_s, small_r), 1 + step, place.row_mate(step))
        for step in range(1, cut.row_size)
    ]
    for copy in copies:
        copy.start()
    for b in range(blocks):
        token_swap(b).wait_recv()
        found = total[near(b), part:] + token_recv[near(b), :]
        stage[b // own_count, near(b % own_count), :] = found
        pltpu.make_async_copy(
            stage.at[b // own_count, near(b % own_count)], token_out.at[near(b)], out_sem.at[own_count + b]
        ).start()
    scatter.finish()
    for copy in copies:
        copy.wait_recv()
    result = small_z[0]
    for z in range(1, cut.row_size):
        result = result + small_z[z]
    small_out[...] = result
    gather.finish()
    for copy in [token_sent, cot_sent, copy_c, copy_x, copy_y] + copies:
        copy.wait_send()
    for i in range(own_count):
        attn_grad_swap(i).wait_send()
    for b in range(blocks):
        token_swap(b).wait_send()
        pltpu.make_async_copy(
            stage.at[b // own_count, near(b % own_count)], token_out.at[near(b)], out_sem.at[own_count + b]
        ).wait()


def place_kernel(
    cut,
    small, down_0, down_1, up_0, up_1, grad_out_t, *rest,
):
    pairs, pair, part, width = cut.heads // 2, 2 * cut.size, cut.part_width, cut.width
    pieces, rest = rest[:pairs], rest[pairs:]
    (
        grad_qkv, grad_out, grad_up, grad_down, query_bias, value_bias, out_bias, up_bias, down_bias, first_gain,
        first_shift, second_gain, second_shift, head, hidden, unit, attention, feedforward,
    ) = rest
    group = cut.units // 2
    for p, piece in enumerate(pieces):
        for k in range(3):
            grad_qkv[k, :, p * pair : (p + 1) * pair] = piece[:, k * pair : (k + 1) * pair]
    grad_out[...] = grad_out_t[...]
    for j, (up, down) in enumerate(((up_0, down_0), (up_1, down_1))):
        grad_up[:, j * group : (j + 1) * group] = up[...]
        grad_down[:, j * group : (j + 1) * group] = down[...]

    def flat(target, values):
        target[...] = values.reshape(target.shape)

    flat(up_bias, jnp.concatenate([small[8:9, :], small[9:10, :]], axis=1))
    flat(unit, jnp.concatenate([small[10:11, :], small[11:12, :]], axis=1))
    flat(query_bias, small[12:13, :part])
    flat(value_bias, small[12:13, part:])
    for row, target in enumerate((out_bias, down_bias, first_gain, first_shift, second_gain, second_shift, hidden)):
        flat(target, small[row : row + 1, :])
    lane = lax.broadcasted_iota(jnp.int32, (1, part), 1) // cut.size
    slot = lax.broadcasted_iota(jnp.int32, (1, cut.heads), 1)
    found = jnp.zeros((1, cut.heads), wide)
    for h in range(cut.heads):
        one = jnp.sum(jnp.where(lane == h, small[13:14, :part], 0.0), axis=1, keepdims=True)
        found = jnp.where(slot == h, one, found)
    flat(head, found)
    seq_total = attention.shape[0]
    flat(attention, small[7:8, :seq_total])
    flat(feedforward, small[7:8, width // 2 : width // 2 + seq_total])


def gather_order(count):
    return [(stage, t - stage) for t in range(count + 2) for stage in range(3) if 0 <= t - stage < count]


def scatter_order(pairs):
    return [(0, 0), (0, 1), (1, 0), (0, 2), (1, 1), (2, 0), (0, 3), (0, 4), (1, 2), (2, 1), (0, 5), (1, 3), (1, 5), (0, 6), (1, 4), (0, 7), (2, 2), (1, 6), (2, 3), (1, 7), (2, 5), (2, 4), (2, 6), (2, 7)]


gather_pace = ((1, 1, 0, 1, 0), (1, 1, 1, 1, 1), (1, 0, 1, 0, 1), (1, 1))
scatter_pace = ((1, 1), (0, 0), (0,), (1, 0, 0, 1, 0), (2, 1, 1, 1, 0), (1, 2, 0, 0, 1))


class Cut(NamedTuple):
    length: int
    width: int
    part_width: int
    heads: int
    size: int
    units: int
    part: int
    row_size: int
    rows: int
    fine: int
    prefix_most: int


def any_spec():
    return pl.BlockSpec(memory_space=pl.ANY)


def vmem_spec():
    return pl.BlockSpec(memory_space=pltpu.VMEM)


def smem_spec():
    return pl.BlockSpec(memory_space=pltpu.SMEM)


def like(items):
    return [jax.ShapeDtypeStruct(shape, kind) for shape, kind in items]


def scratch(items):
    return [pltpu.VMEM(shape, kind) for shape, kind in items]


def dma(*shape):
    return pltpu.SemaphoreType.DMA(shape)


vmem_most = 67043328


def run_layer(cut, *args):
    length, width, half = cut.length, cut.width, cut.part_width
    group = cut.units // 2
    pairs = cut.heads // 2
    blocks = length // cut.rows
    columns = [group] * 4 + [half] * (pairs + 1)
    count = len(columns)
    outs = [((length, half), wide), ((length, half), wide), ((16, width), wide)]
    outs += [((cut.part, n), wide) for n in columns]
    own = [
        ((pairs + 1, width, half), low_type),
        ((4, width, group), low_type),
        ((length, width), low_type),
        ((width, length), low_type),
        ((pairs, length, half), low_type),
        ((cut.heads, 1, length), wide),
        ((length, half), low_type),
        ((length // 2, width), wide),
        ((width, length), low_type),
        ((2, length, group), low_type),
        ((2, length, group), low_type),
        ((length // 2, width), wide),
        ((length, width), low_type),
        ((width, length), low_type),
        ((8, 8, width), wide),
        ((length // 2, width), low_type),
        ((length, width), wide),
        ((length // 2, width), wide),
        ((length // 2, width), wide),
        ((2, length // 2, half), wide),
        ((length, half), wide),
        ((length, half), low_type),
        ((length, half), low_type),
        ((length, 2 * cut.size), wide),
        ((length, 2 * cut.size), wide),
        ((2 * cut.size, length), wide),
        ((2 * cut.size, length), low_type),
        ((pairs + 1, cut.part, half), low_type),
        ((4, cut.part, group), low_type),
        ((16, width), wide),
        ((2, 16, width), wide),
        ((2, 16, width), wide),
        ((2, 16, width), wide),
        ((cut.row_size, 16, width), wide),
        ((4, 8, width), wide),
        ((8, half), wide),
    ]
    quarter = cut.part * cut.row_size // 2
    own += [((width, n), low_type) for n in columns]
    own += [((2, 2, quarter, n), low_type) for n in columns]
    own += [((2, quarter, n), low_type) for n in columns]
    own += [((2, quarter, n), low_type) for n in columns]
    own += [((2 * quarter, n), low_type) for n in columns]
    own += [((cut.row_size - 1, cut.part, n), low_type) for n in columns]
    z = cut.row_size - 1
    semaphores = [dma(count), dma(count, z), dma(count, z), dma(count, 2), dma(count, 2), dma(count, 4), dma(count, 4)]
    semaphores += [dma(2), dma(blocks // 2 + blocks)]
    semaphores += [dma(count, 4), dma(count, 4), dma(count, 2), dma(count, 2), dma(count, z), dma(count, z)]
    pair_swaps = 3 + 7 * (blocks // 2) + blocks
    semaphores += [dma(pair_swaps), dma(pair_swaps), dma(2 + z), dma(2 + z)]
    return pl.pallas_call(
        partial(layer_kernel, cut),
        out_shape=like(outs),
        in_specs=[any_spec()] * 2 + [vmem_spec()] * (len(args) - 6) + [smem_spec()] * 4,
        out_specs=[any_spec()] * 2 + [vmem_spec()] * (len(outs) - 2),
        scratch_shapes=scratch(own) + semaphores,
        compiler_params=pltpu.CompilerParams(collective_id=0, has_side_effects=True, vmem_limit_bytes=vmem_most),
        name="whole_layer",
    )(*args)


def fused_device(
    cut,
    tokens, cotangent, qkv_weight, out_weight, up_weight, down_weight, query_bias, value_bias, out_bias, up_bias,
    down_bias, first_gain, first_shift, second_gain, second_shift, head_gate, hidden_gate, intermediate_gate,
    attention_gate, feedforward_gate, prefix_length,
):
    half, width, units, part = cut.part_width, cut.width, cut.units, cut.part
    rows = [
        query_bias, value_bias, out_bias, up_bias, down_bias, first_gain, first_shift, second_gain, second_shift,
        hidden_gate, intermediate_gate,
    ]
    scalars = [head_gate, attention_gate, feedforward_gate, prefix_length]
    weights = [qkv_weight, out_weight.T, up_weight, down_weight.T]
    layer_out, grad_tokens, *made = run_layer(cut, tokens, cotangent, *weights, *rows, *scalars)
    seq_total = lax.axis_size(("dp", "row"))
    lanes = [half, half, width, units, width, width, width, width, width, cut.heads, width, units, seq_total, seq_total]
    shapes = [(3, part, half), (part, half), (part, units), (part, units)] + [(n,) for n in lanes]
    outs = pl.pallas_call(
        partial(place_kernel, cut),
        out_shape=like([(shape, wide) for shape in shapes]),
        in_specs=[vmem_spec()] * len(made),
        out_specs=[vmem_spec()] * len(shapes),
        name="place_results",
    )(*made)
    return (layer_out, grad_tokens, outs[0], outs[1].T, outs[2], outs[3].T, *outs[4:])


def cut_of(args):
    tokens, qkv_weight, up_weight, head_gate, prefix_length = args[0], args[2], args[4], args[15], args[20]
    length, part_width = tokens.shape
    part, width = qkv_weight.shape[1], args[11].shape[0]
    heads = head_gate.shape[0]
    row_size, dp_size = lax.axis_size("row"), lax.axis_size("dp")
    fits = (
        prefix_length.shape[0] == 1
        and lax.axis_size("col") == 2
        and dp_size == 4
        and row_size % 2 == 0
        and part % 16 == 0
        and heads % 2 == 0
        and part_width == qkv_weight.shape[2]
        and part_width == 3 * (2 * part_width // heads)
        and (2 * part_width // heads) % 128 == 0
        and width % 256 == 0
        and length % 512 == 0
        and up_weight.shape[1] == 2 * width
    )
    if not fits:
        return None
    return Cut(
        length, width, part_width, heads, part_width // heads, up_weight.shape[1], part, row_size, 256, 128, length // 2
    )


def any_device(*args):
    cut = cut_of(args)
    return per_device(*args) if cut is None else fused_device(cut, *args)


def solution(mesh):
    placed = (
        P(("dp", "row"), "col"),
        P(("dp", "row"), "col"),
        P(None, ("dp", "row"), "col"),
        P("col", ("dp", "row")),
        P(("dp", "row"), "col"),
        P("col", ("dp", "row")),
        P("col"),
        P("col"),
        P(),
        P("col"),
        P(),
        P(),
        P(),
        P(),
        P(),
        P("col"),
        P(),
        P("col"),
        P(("dp", "row")),
        P(("dp", "row")),
        P(("dp", "row")),
    )
    return jax.shard_map(
        any_device,
        mesh=mesh,
        in_specs=placed,
        out_specs=(
            P(("dp", "row"), "col"),
            P(("dp", "row"), "col"),
            P(None, ("dp", "row"), "col"),
            P("col", ("dp", "row")),
            P(("dp", "row"), "col"),
            P("col", ("dp", "row")),
            P("col"),
            P("col"),
            P(),
            P("col"),
            P(),
            P(),
            P(),
            P(),
            P(),
            P("col"),
            P(),
            P("col"),
            P(),
            P(),
        ),
        check_vma=False,
    )
```

```python
from functools import partial
import math
from typing import NamedTuple

import jax
import jax.numpy as jnp
from jax import lax
from jax.experimental import pallas as pl
from jax.experimental.pallas import tpu as pltpu
from jax.sharding import PartitionSpec as P

masked_value = -1e30
norm_eps = 1e-05


def norm_forward(values, scale_gain, shift_term):
    centre = jnp.mean(values, axis=1, keepdims=True)
    centred = values - centre
    spread = jnp.mean(centred * centred, axis=1, keepdims=True)
    inverse = lax.rsqrt(spread + norm_eps)
    normed = centred * inverse
    return (normed * scale_gain + shift_term, normed, inverse)


def norm_backward(gradient, normed, inverse, scale_gain):
    scaled = gradient * scale_gain
    first_mean = jnp.mean(scaled, axis=1, keepdims=True)
    second_mean = jnp.mean(scaled * normed, axis=1, keepdims=True)
    return inverse * (scaled - first_mean - normed * second_mean)


def block_mask(start_row, block_rows, length, prefix_value):
    key_index = jnp.arange(length, dtype=jnp.int32)
    query_index = start_row + jnp.arange(block_rows, dtype=jnp.int32)
    return (key_index[None, :] < prefix_value) | (key_index[None, :] <= query_index[:, None])


def block_scores(query_block, key_seq, start_row, prefix_value, scale_factor):
    block_rows = query_block.shape[0]
    length = key_seq.shape[0]
    allowed = block_mask(start_row, block_rows, length, prefix_value)
    scores = (
        jnp.einsum("qhd,khd->hqk", query_block, key_seq, preferred_element_type=jnp.float32)
        * scale_factor
    )
    return jnp.where(allowed[None], scores, masked_value)


def attend_sequence(query_seq, key_seq, value_seq, prefix_value, block_rows, scale_factor):
    length = key_seq.shape[0]
    block_count = length // block_rows
    query_blocks = query_seq.reshape(
        block_count, block_rows, query_seq.shape[1], query_seq.shape[2]
    )
    starts = jnp.arange(block_count, dtype=jnp.int32) * block_rows

    def one_block(element):
        query_block, start_row = element
        scores = block_scores(query_block, key_seq, start_row, prefix_value, scale_factor)
        row_peak = jnp.max(scores, axis=2, keepdims=True)
        exponent = jnp.exp(scores - row_peak)
        row_total = jnp.sum(exponent, axis=2, keepdims=True)
        weights_low = (exponent / row_total).astype(jnp.bfloat16)
        context = jnp.einsum(
            "hqk,khd->qhd", weights_low, value_seq, preferred_element_type=jnp.float32
        )
        return (context, row_peak[..., 0] + jnp.log(row_total[..., 0]))

    contexts, log_totals = lax.map(one_block, (query_blocks, starts))
    return (contexts.reshape(length, query_seq.shape[1], query_seq.shape[2]), log_totals)


def attend_back(
    query_seq, key_seq, value_seq, grad_seq, log_seq, prefix_value, block_rows, scale_factor
):
    length = key_seq.shape[0]
    block_count = length // block_rows
    head_count = query_seq.shape[1]
    head_size = query_seq.shape[2]
    query_blocks = query_seq.reshape(block_count, block_rows, head_count, head_size)
    grad_blocks = grad_seq.reshape(block_count, block_rows, head_count, head_size)
    starts = jnp.arange(block_count, dtype=jnp.int32) * block_rows

    def one_block(running, element):
        grad_keys, grad_values = running
        query_block, grad_block, log_block, start_row = element
        scores = block_scores(query_block, key_seq, start_row, prefix_value, scale_factor)
        probs = jnp.exp(scores - log_block[..., None])
        grad_probs = jnp.einsum(
            "qhd,khd->hqk", grad_block, value_seq, preferred_element_type=jnp.float32
        )
        row_inner = jnp.sum(probs * grad_probs, axis=2, keepdims=True)
        grad_scores = (probs * (grad_probs - row_inner)).astype(jnp.bfloat16)
        grad_query = (
            jnp.einsum("hqk,khd->qhd", grad_scores, key_seq, preferred_element_type=jnp.float32)
            * scale_factor
        )
        grad_keys = (
            grad_keys
            + jnp.einsum(
                "hqk,qhd->khd", grad_scores, query_block, preferred_element_type=jnp.float32
            )
            * scale_factor
        )
        grad_values = grad_values + jnp.einsum(
            "hqk,qhd->khd",
            probs.astype(jnp.bfloat16),
            grad_block,
            preferred_element_type=jnp.float32,
        )
        return ((grad_keys, grad_values), grad_query)

    zeros_kv = jnp.zeros((length, head_count, head_size), jnp.float32)
    (grad_keys, grad_values), grad_query = lax.scan(
        one_block, (zeros_kv, zeros_kv), (query_blocks, grad_blocks, log_seq, starts)
    )
    return (grad_query.reshape(length, head_count, head_size), grad_keys, grad_values)


def per_device(
    tokens,
    cotangent,
    qkv_weight,
    out_weight,
    up_weight,
    down_weight,
    query_bias,
    value_bias,
    out_bias,
    up_bias,
    down_bias,
    first_gain,
    first_shift,
    second_gain,
    second_shift,
    head_gate,
    hidden_gate,
    intermediate_gate,
    attention_gate,
    feedforward_gate,
    prefix_length,
):
    row_count = tokens.shape[0]
    seq_count = prefix_length.shape[0]
    length = row_count // seq_count
    local_heads = head_gate.shape[0]
    head_width = qkv_weight.shape[2]
    head_size = head_width // local_heads
    model_width = first_gain.shape[0]
    part_width = model_width // lax.axis_size("col")
    block_rows = min(512, length)
    scale_factor = head_size ** (-0.5)
    col_index = lax.axis_index("col")
    qkv_low, out_low = (
        lax.all_gather(qkv_weight.astype(jnp.bfloat16), ("dp", "row"), axis=1, tiled=True),
        lax.all_gather(out_weight.astype(jnp.bfloat16), ("dp", "row"), axis=1, tiled=True),
    )
    up_low, down_low = (
        lax.all_gather(up_weight.astype(jnp.bfloat16), ("dp", "row"), axis=0, tiled=True),
        lax.all_gather(down_weight.astype(jnp.bfloat16), ("dp", "row"), axis=1, tiled=True),
    )
    token_full = lax.all_gather(tokens, "col", axis=1, tiled=True)
    projected = jnp.einsum("td,kdf->ktf", token_full, qkv_low, preferred_element_type=jnp.float32)
    query_low = (projected[0] + query_bias).astype(jnp.bfloat16)
    key_low = projected[1].astype(jnp.bfloat16)
    value_low = (projected[2] + value_bias).astype(jnp.bfloat16)

    def split_heads(array):
        return array.reshape(seq_count, length, local_heads, head_size)

    def forward_seq(element):
        query_seq, key_seq, value_seq, prefix_value = element
        return attend_sequence(
            query_seq, key_seq, value_seq, prefix_value, block_rows, scale_factor
        )

    contexts, log_totals = lax.map(
        forward_seq,
        (split_heads(query_low), split_heads(key_low), split_heads(value_low), prefix_length),
    )
    context = contexts.reshape(row_count, head_width)
    gate_columns = jnp.repeat(head_gate.astype(jnp.float32), head_size)
    gated_low = (context * gate_columns).astype(jnp.bfloat16)
    attn_terms = jnp.dot(gated_low, out_low, preferred_element_type=jnp.float32)
    attn_out = lax.psum(attn_terms, "col") + out_bias
    hidden_mask = hidden_gate.astype(jnp.float32)
    attn_rows = jnp.repeat(attention_gate.astype(jnp.float32), length)[:, None]
    dense_rows = jnp.repeat(feedforward_gate.astype(jnp.float32), length)[:, None]
    first_sum = token_full.astype(jnp.float32) + attn_rows * hidden_mask * attn_out
    normed_one, first_normed, first_inverse = norm_forward(first_sum, first_gain, first_shift)
    normed_low = normed_one.astype(jnp.bfloat16)
    pre_act = jnp.dot(normed_low, up_low, preferred_element_type=jnp.float32) + up_bias
    activated, gelu_pull = jax.vjp(partial(jax.nn.gelu, approximate=False), pre_act)
    unit_mask = intermediate_gate.astype(jnp.float32)
    inner_low = (activated * unit_mask).astype(jnp.bfloat16)
    dense_terms = jnp.dot(inner_low, down_low, preferred_element_type=jnp.float32)
    dense_out = lax.psum(dense_terms, "col") + down_bias
    second_sum = normed_one + dense_rows * hidden_mask * dense_out
    layer_full, second_normed, second_inverse = norm_forward(second_sum, second_gain, second_shift)
    layer_out = lax.dynamic_slice_in_dim(layer_full, col_index * part_width, part_width, 1)
    grad_full = lax.all_gather(cotangent, "col", axis=1, tiled=True).astype(jnp.float32)
    grad_gain_two = jnp.sum(grad_full * second_normed, axis=0)
    grad_shift_two = jnp.sum(grad_full, axis=0)
    grad_second = norm_backward(grad_full, second_normed, second_inverse, second_gain)
    grad_dense_low = (dense_rows * hidden_mask * grad_second).astype(jnp.bfloat16)
    dense_product = dense_out * grad_second
    grad_dense_gate = jnp.sum(
        dense_product.reshape(seq_count, length, model_width) * hidden_mask, axis=(1, 2)
    )
    hidden_from_dense = jnp.sum(dense_rows * dense_product, axis=0)
    grad_down_bias = jnp.sum(grad_dense_low.astype(jnp.float32), axis=0)
    up_low, down_low = (
        lax.all_gather(up_weight.astype(jnp.bfloat16), ("dp", "row"), axis=0, tiled=True),
        lax.all_gather(down_weight.astype(jnp.bfloat16), ("dp", "row"), axis=1, tiled=True),
    )
    grad_down = jnp.einsum(
        "tf,td->fd", inner_low, grad_dense_low, preferred_element_type=jnp.float32
    )
    grad_inner_low = jnp.einsum(
        "td,fd->tf", grad_dense_low, down_low, preferred_element_type=jnp.float32
    ).astype(jnp.bfloat16)
    grad_inner = grad_inner_low.astype(jnp.float32)
    grad_unit_gate = jnp.sum(activated * grad_inner, axis=0)
    (grad_pre,) = gelu_pull(unit_mask * grad_inner)
    grad_pre_low = grad_pre.astype(jnp.bfloat16)
    grad_up_bias = jnp.sum(grad_pre_low.astype(jnp.float32), axis=0)
    grad_up = jnp.einsum("td,tf->df", normed_low, grad_pre_low, preferred_element_type=jnp.float32)
    dense_parts = (
        lax.psum_scatter(grad_up, ("dp", "row"), scatter_dimension=0, tiled=True),
        lax.psum_scatter(grad_down, ("dp", "row"), scatter_dimension=1, tiled=True),
    )
    hidden_terms = jnp.einsum("tf,df->td", grad_pre_low, up_low, preferred_element_type=jnp.float32)
    grad_normed = grad_second + lax.psum(hidden_terms, "col")
    grad_gain_one = jnp.sum(grad_normed * first_normed, axis=0)
    grad_shift_one = jnp.sum(grad_normed, axis=0)
    grad_first = norm_backward(grad_normed, first_normed, first_inverse, first_gain)
    grad_attn_low = (attn_rows * hidden_mask * grad_first).astype(jnp.bfloat16)
    attn_product = attn_out * grad_first
    grad_attn_gate = jnp.sum(
        attn_product.reshape(seq_count, length, model_width) * hidden_mask, axis=(1, 2)
    )
    grad_hidden = hidden_from_dense + jnp.sum(attn_rows * attn_product, axis=0)
    grad_out_bias = jnp.sum(grad_attn_low.astype(jnp.float32), axis=0)
    qkv_low, out_low = (
        lax.all_gather(qkv_weight.astype(jnp.bfloat16), ("dp", "row"), axis=1, tiled=True),
        lax.all_gather(out_weight.astype(jnp.bfloat16), ("dp", "row"), axis=1, tiled=True),
    )
    grad_out = jnp.einsum("tc,td->cd", gated_low, grad_attn_low, preferred_element_type=jnp.float32)
    grad_gated_low = jnp.einsum(
        "td,cd->tc", grad_attn_low, out_low, preferred_element_type=jnp.float32
    ).astype(jnp.bfloat16)
    grad_head_cols = jnp.sum(context * grad_gated_low.astype(jnp.float32), axis=0)
    grad_head = jnp.sum(grad_head_cols.reshape(local_heads, head_size), axis=1)
    grad_context = grad_gated_low * gate_columns.astype(jnp.bfloat16)

    def backward_seq(element):
        query_seq, key_seq, value_seq, grad_seq, log_seq, prefix_value = element
        return attend_back(
            query_seq, key_seq, value_seq, grad_seq, log_seq, prefix_value, block_rows, scale_factor
        )

    grad_query, grad_keys, grad_values = lax.map(
        backward_seq,
        (
            split_heads(query_low),
            split_heads(key_low),
            split_heads(value_low),
            split_heads(grad_context),
            log_totals,
            prefix_length,
        ),
    )
    grad_qkv_low = jnp.stack([grad_query, grad_keys, grad_values]).reshape(3, row_count, head_width)
    grad_qkv_low = grad_qkv_low.astype(jnp.bfloat16)
    grad_query_bias = jnp.sum(grad_qkv_low[0].astype(jnp.float32), axis=0)
    grad_value_bias = jnp.sum(grad_qkv_low[2].astype(jnp.float32), axis=0)
    grad_qkv = jnp.einsum(
        "td,ktf->kdf", token_full, grad_qkv_low, preferred_element_type=jnp.float32
    )
    input_terms = jnp.einsum(
        "ktf,kdf->td", grad_qkv_low, qkv_low, preferred_element_type=jnp.float32
    )
    grad_tokens = lax.psum_scatter(
        input_terms.astype(jnp.bfloat16), "col", scatter_dimension=1, tiled=True
    ).astype(jnp.float32)
    grad_tokens = grad_tokens + lax.dynamic_slice_in_dim(
        grad_first, col_index * part_width, part_width, 1
    )
    grad_up_part, grad_down_part = dense_parts
    grad_qkv_part, grad_out_part = (
        lax.psum_scatter(grad_qkv, ("dp", "row"), scatter_dimension=1, tiled=True),
        lax.psum_scatter(grad_out, ("dp", "row"), scatter_dimension=1, tiled=True),
    )
    seq_total = seq_count * lax.axis_size(("dp", "row"))
    seq_start = lax.axis_index(("dp", "row")) * seq_count
    seq_stack = lax.dynamic_update_slice_in_dim(
        jnp.zeros((2, seq_total), jnp.float32),
        jnp.stack([grad_attn_gate, grad_dense_gate]),
        seq_start,
        1,
    )
    full_stack = jnp.stack(
        [
            grad_out_bias,
            grad_down_bias,
            grad_gain_one,
            grad_shift_one,
            grad_gain_two,
            grad_shift_two,
            grad_hidden,
        ]
    )
    half_stack = jnp.stack([grad_query_bias, grad_value_bias])
    unit_stack = jnp.stack([grad_up_bias, grad_unit_gate])
    full_sum, half_sum, unit_sum, head_sum, seq_sum = lax.psum(
        (full_stack, half_stack, unit_stack, grad_head, seq_stack), ("dp", "row")
    )
    return (
        layer_out,
        grad_tokens,
        grad_qkv_part,
        grad_out_part,
        grad_up_part,
        grad_down_part,
        half_sum[0],
        half_sum[1],
        full_sum[0],
        unit_sum[0],
        full_sum[1],
        full_sum[2],
        full_sum[3],
        full_sum[4],
        full_sum[5],
        head_sum,
        full_sum[6],
        unit_sum[1],
        seq_sum[0],
        seq_sum[1],
    )


low_type = jnp.bfloat16
wide = jnp.float32
mesh_ids = pl.DeviceIdType.MESH


def dot_nn(left, right):
    return jnp.dot(left, right, preferred_element_type=wide)


def dot_nt(left, right):
    return lax.dot_general(left, right, (((1,), (1,)), ((), ())), preferred_element_type=wide)


def rows_at(index, count):
    return pl.ds(pl.multiple_of(index * count, count), count)


def fold_rows(values):
    return jnp.sum(values.reshape(values.shape[0] // 8, 8, values.shape[1]), axis=0)


def norm_parts(values):
    centre = jnp.mean(values, axis=1, keepdims=True)
    centred = values - centre
    spread = jnp.mean(centred * centred, axis=1, keepdims=True)
    inverse = lax.rsqrt(spread + norm_eps)
    return centred * inverse, inverse


class Place:
    def __init__(self, row_size):
        self.dp, self.row, self.col = (lax.axis_index(name) for name in ("dp", "row", "col"))
        self.row_size = row_size
        self.x, self.y = lax.rem(self.dp, 2), self.dp // 2
        self.x_dp = self.y * 2 + (1 - self.x)
        self.y_dp = (1 - self.y) * 2 + self.x

    def x_mate(self):
        return {"dp": self.x_dp}

    def y_mate(self):
        return {"dp": self.y_dp}

    def row_mate(self, step):
        return {"row": lax.rem(self.row + step, self.row_size)}

    def col_mate(self):
        return {"col": 1 - self.col}

    def barrier(self):
        semaphore = pltpu.get_barrier_semaphore()
        mates = [self.x_mate(), self.y_mate(), self.col_mate()]
        mates += [self.row_mate(step) for step in range(1, self.row_size)]
        for mate in mates:
            pl.semaphore_signal(semaphore, inc=1, device_id=mate, device_id_type=mesh_ids)
        pl.semaphore_wait(semaphore, len(mates))


def send(source, target, semaphores, index, mate):
    sent, received = semaphores
    return pltpu.make_async_remote_copy(
        src_ref=source,
        dst_ref=target,
        send_sem=sent.at[index],
        recv_sem=received.at[index],
        device_id=mate,
        device_id_type=mesh_ids,
    )


class Gather:
    def __init__(self, place, shards, chunks, turned, order, own_sem, z_sems, two_sems, three_sems, turned_sems):
        self.place, self.shards, self.chunks, self.turned = place, shards, chunks, turned
        self.own_sem, self.z_sems, self.two_sems, self.three_sems = own_sem, z_sems, two_sems, three_sems
        self.turned_sems = turned_sems
        self.part = shards[0].shape[0]
        self.block = self.part * place.row_size
        self.half = self.block // 2
        self.steps, self.done = order, 0

    def block_rows(self, dp):
        return pl.ds(pl.multiple_of(dp * self.block, 16), self.block)

    def half_rows(self, dp, half):
        return pl.ds(pl.multiple_of(dp * self.block + half * self.half, 16), self.half)

    def part_rows(self, dp):
        return pl.ds(pl.multiple_of(dp * self.block + self.place.row * self.part, 16), self.part)

    def half_cols(self, c, half):
        count = self.chunks[c].shape[1] // 2
        return pl.ds(half * count, count)

    def own(self, c):
        rows = self.part_rows(self.place.dp)
        return pltpu.make_async_copy(self.shards[c], self.chunks[c].at[rows], self.own_sem.at[c])

    def along_z(self, c):
        place, rows = self.place, self.part_rows(self.place.dp)
        return [
            send(self.shards[c], self.chunks[c].at[rows], self.z_sems, (c, step - 1), place.row_mate(step))
            for step in range(1, place.row_size)
        ]

    def turned_z(self, c):
        place, found = self.place, []
        for step in range(1, place.row_size):
            for half, dp in ((0, place.x_dp), (1, place.y_dp)):
                at = self.chunks[c].at[self.part_rows(dp), self.half_cols(c, half)]
                found.append(send(at, at, self.turned_sems, (c, 2 * step - 2 + half), place.row_mate(step)))
        return found

    def second(self, c):
        place, chunk, found = self.place, self.chunks[c], []
        for half, mate in ((0, place.x_mate()), (1, place.y_mate())):
            if c in self.turned:
                cols = self.half_cols(c, half)
                source, target = self.shards[c].at[:, cols], chunk.at[self.part_rows(place.dp), cols]
            else:
                source = target = chunk.at[self.half_rows(place.dp, half)]
            found.append(send(source, target, self.two_sems, (c, half), mate))
        return found

    def third(self, c):
        place, chunk, found = self.place, self.chunks[c], []
        for index, (dp, half, mate) in enumerate(
            (
                (place.dp, 0, place.y_mate()),
                (place.dp, 1, place.x_mate()),
                (place.x_dp, 0, place.y_mate()),
                (place.y_dp, 1, place.x_mate()),
            )
        ):
            if c in self.turned:
                at = chunk.at[self.block_rows(dp), self.half_cols(c, half)]
            else:
                at = chunk.at[self.half_rows(dp, half)]
            found.append(send(at, at, self.three_sems, (c, index), mate))
        return found

    def step(self):
        stage, c = self.steps[self.done]
        self.done += 1
        if stage < 0:
            self.own(c).start()
            for copy in self.along_z(c) + (self.second(c) if c in self.turned else []):
                copy.start()
        elif stage == 0 and c in self.turned:
            for copy in self.second(c):
                copy.wait_recv()
            for copy in self.turned_z(c):
                copy.start()
        elif stage == 0:
            self.own(c).wait()
            for copy in self.along_z(c):
                copy.wait_recv()
            for copy in self.second(c):
                copy.start()
        elif stage == 1:
            if c in self.turned:
                self.own(c).wait()
                waits = self.along_z(c) + self.turned_z(c)
            else:
                waits = self.second(c)
            for copy in waits:
                copy.wait_recv()
            for copy in self.third(c):
                copy.start()
        else:
            for copy in self.third(c):
                copy.wait_recv()

    def begin(self):
        while self.steps[self.done][0] < 0:
            self.step()

    def advance(self, count):
        for _ in range(count):
            if self.done < len(self.steps):
                self.step()

    def need(self, c):
        while self.done <= self.steps.index((2, c)):
            self.step()

    def finish(self):
        self.advance(len(self.steps))
        for c in range(len(self.chunks)):
            for copy in self.along_z(c) + self.second(c) + self.third(c):
                copy.wait_send()
            for copy in self.turned_z(c) if c in self.turned else []:
                copy.wait_send()


class Scatter:
    def __init__(
        self, place, chunks, outs, turned, order, first, mid_send, mid, last_send, last, one_sems, two_sems, z_sems
    ):
        self.place, self.chunks, self.outs, self.turned = place, chunks, outs, turned
        self.first, self.mid_send, self.mid, self.last_send, self.last = first, mid_send, mid, last_send, last
        self.one_sems, self.two_sems, self.z_sems = one_sems, two_sems, z_sems
        self.part = outs[0].shape[0]
        self.block = self.part * place.row_size
        self.half = self.block // 2
        self.count = len(chunks)
        self.steps, self.done, self.begun = order, 0, []

    def block_rows(self, dp):
        return pl.ds(pl.multiple_of(dp * self.block, 16), self.block)

    def half_rows(self, dp, half):
        return pl.ds(pl.multiple_of(dp * self.block + half * self.half, 16), self.half)

    def z_rows(self, z):
        return pl.ds(pl.multiple_of(z * self.part, 16), self.part)

    def half_cols(self, c, half):
        count = self.chunks[c].shape[1] // 2
        return pl.ds(half * count, count)

    def one(self, c):
        place, chunk, first = self.place, self.chunks[c], self.first[c]
        found = []
        for i in range(2):
            for half, dp, mate in (
                (0, (1 - place.y) * 2 + i, place.y_mate()),
                (1, i * 2 + (1 - place.x), place.x_mate()),
            ):
                if c in self.turned:
                    at = chunk.at[self.block_rows(dp), self.half_cols(c, half)]
                else:
                    at = chunk.at[self.half_rows(dp, half)]
                found.append(send(at, first.at[half, i], self.one_sems, (c, 2 * half + i), mate))
        return found

    def two(self, c):
        place = self.place
        source, target = (self.last_send[c], self.last[c]) if c in self.turned else (self.mid_send[c], self.mid[c])
        return [
            send(source.at[0], target.at[0], self.two_sems, (c, 0), place.x_mate()),
            send(source.at[1], target.at[1], self.two_sems, (c, 1), place.y_mate()),
        ]

    def along_z(self, c):
        place, found = self.place, []
        for step in range(1, place.row_size):
            rows = self.z_rows(lax.rem(place.row + step, place.row_size))
            if c in self.turned:
                source, target = self.mid_send[c].at[:, rows], self.mid[c].at[step - 1]
            else:
                source, target = self.last_send[c].at[rows], self.last[c].at[step - 1]
            found.append(send(source, target, self.z_sems, (c, step - 1), place.row_mate(step)))
        return found

    def begin(self, c):
        self.begun.append(c)
        for copy in self.one(c):
            copy.start()

    def step(self):
        stage, c = self.steps[self.done]
        self.done += 1
        if c in self.turned:
            self.turned_step(stage, c)
            return
        place, chunk = self.place, self.chunks[c]
        first, mid_send, mid = self.first[c], self.mid_send[c], self.mid[c]
        last_send, last = self.last_send[c], self.last[c]
        if stage == 0:
            for copy in self.one(c):
                copy.wait_recv()
            mid_send[0] = (
                chunk[self.half_rows(place.x_dp, 0), :].astype(wide) + first[0, 1 - place.x].astype(wide)
            ).astype(low_type)
            mid_send[1] = (
                chunk[self.half_rows(place.y_dp, 1), :].astype(wide) + first[1, 1 - place.y].astype(wide)
            ).astype(low_type)
            for copy in self.two(c):
                copy.start()
        elif stage == 1:
            for copy in self.two(c):
                copy.wait_recv()
            for half, slot in ((0, place.x), (1, place.y)):
                last_send[pl.ds(half * self.half, self.half), :] = (
                    chunk[self.half_rows(place.dp, half), :].astype(wide)
                    + first[half, slot].astype(wide)
                    + mid[half].astype(wide)
                ).astype(low_type)
            for copy in self.along_z(c):
                copy.start()
        else:
            total = last_send[self.z_rows(place.row), :].astype(wide)
            for step, copy in enumerate(self.along_z(c)):
                copy.wait_recv()
                total = total + last[step].astype(wide)
            self.outs[c][...] = total

    def turned_step(self, stage, c):
        place, chunk, out = self.place, self.chunks[c], self.outs[c]
        first, mid_send, mid = self.first[c], self.mid_send[c], self.mid[c]
        last_send, last = self.last_send[c], self.last[c]
        if stage == 0:
            for copy in self.one(c):
                copy.wait_recv()
            for half in range(2):
                for i in range(2):
                    dp = place.y * 2 + i if half == 0 else i * 2 + place.x
                    mine = chunk[self.block_rows(dp), self.half_cols(c, half)].astype(wide)
                    mid_send[2 * half + i] = (mine + first[half, i].astype(wide)).astype(low_type)
            for copy in self.along_z(c):
                copy.start()
        elif stage == 1:
            for copy in self.along_z(c):
                copy.wait_recv()
            for half, slot in ((0, place.x), (1, place.y)):
                for index, keep in ((slot, True), (1 - slot, False)):
                    total = mid_send[2 * half + index, self.z_rows(place.row), :].astype(wide)
                    for step in range(place.row_size - 1):
                        total = total + mid[step, 2 * half + index].astype(wide)
                    if keep:
                        out[:, self.half_cols(c, half)] = total
                    else:
                        last_send[half] = total.astype(low_type)
            for copy in self.two(c):
                copy.start()
        else:
            for half, copy in enumerate(self.two(c)):
                copy.wait_recv()
                out[:, self.half_cols(c, half)] += last[half].astype(wide)

    def advance(self, count):
        for _ in range(count):
            if self.done < len(self.steps) and self.steps[self.done][1] in self.begun:
                self.step()

    def finish(self):
        self.advance(len(self.steps))
        for c in range(self.count):
            for copy in self.one(c) + self.two(c) + self.along_z(c):
                copy.wait_send()


def masked_tile(tile, query_start, key_start, prefix):
    key_index = key_start + lax.broadcasted_iota(jnp.int32, tile.shape, 0)
    query_index = query_start + lax.broadcasted_iota(jnp.int32, tile.shape, 1)
    return jnp.where((key_index < prefix) | (key_index <= query_index), tile, masked_value)


def key_tiles(block, rows, prefix_most):
    count = max((block + 1) * rows, prefix_most) // rows
    return [(tile, tile >= block) for tile in range(count)]


def flat_row(ref):
    return ref[...].reshape(1, ref.shape[0])


def gate_row(gates, heads, size):
    head = lax.broadcasted_iota(jnp.int32, (1, heads * size), 1) // size
    row = jnp.zeros((1, heads * size), wide)
    for h in range(heads):
        row = jnp.where(head == h, gates[h].astype(wide), row)
    return row


def layer_kernel(
    cut,
    token_part, cot_part, qkv_w, out_w, up_w, down_w, query_bias, value_bias, out_bias, up_bias, down_bias,
    first_gain, first_shift, second_gain, second_shift, hidden_gate, unit_gate,
    head_gate, attention_gate, feedforward_gate, prefix_length,
    layer_out, token_out, small_out, *rest,
):
    length, width, heads, size = cut.length, cut.width, cut.heads, cut.size
    part, rows, fine = cut.part_width, cut.rows, cut.fine
    blocks = length // rows
    own_count = blocks // 2
    pair = 2 * size
    pairs = heads // 2
    count = pairs + 5
    rest = list(rest)

    def take(number):
        taken = rest[:number]
        del rest[:number]
        return taken

    grads = take(count)
    (wa, wm, token, token_t, qkv, lse, ctx, attn_out, normed_t, gelu, slope, second, low, dense_t, sums) = take(15)
    (cot, total, arrive_a, arrive_b, stage, token_recv, ctx_grad, key_grad, value_grad) = take(9)
    (pair_wide, pair_low, key_t, shards_a, shards_m) = take(5)
    (small, small_c, small_x, small_y, small_z, unit_sums, head_sums) = take(7)
    buffers, first, mid_send, mid, last_send, last = (take(count) for _ in range(6))
    (own_sem, gz_s, gz_r, g2_s, g2_r, g3_s, g3_r, gt_s, gt_r, half_sem, out_sem) = take(11)
    (s1_s, s1_r, s2_s, s2_r, sz_s, sz_r) = take(6)
    (col_s, col_r, small_s, small_r) = take(4)
    group = wm.shape[2]
    place = Place(cut.row_size)
    for p in range(pairs):
        for k in range(3):
            shards_a[p, :, k * pair : (k + 1) * pair] = qkv_w[k, :, p * pair : (p + 1) * pair].astype(low_type)
    shards_a[pairs] = out_w[...].astype(low_type)
    for j in range(2):
        shards_m[2 * j] = up_w[:, j * group : (j + 1) * group].astype(low_type)
        shards_m[2 * j + 1] = down_w[:, j * group : (j + 1) * group].astype(low_type)
    place.barrier()
    prefix = prefix_length[0]
    attn_gate, dense_gate = attention_gate[0].astype(wide), feedforward_gate[0].astype(wide)
    hidden, unit_row = flat_row(hidden_gate).astype(wide), flat_row(unit_gate).astype(wide)
    query_bias, value_bias, up_bias, out_bias, down_bias, first_gain, first_shift, second_gain, second_shift = (
        flat_row(ref)
        for ref in (
            query_bias, value_bias, up_bias, out_bias, down_bias, first_gain, first_shift, second_gain, second_shift
        )
    )
    chunks = [wa.at[i] for i in range(pairs + 1)] + [wm.at[i] for i in range(4)]
    shards = [shards_a.at[i] for i in range(pairs + 1)] + [shards_m.at[i] for i in range(4)]
    gather = Gather(
        place, shards, chunks, gather_turned, gather_order, own_sem, (gz_s, gz_r), (g2_s, g2_r), (g3_s, g3_r),
        (gt_s, gt_r),
    )
    scatter = Scatter(
        place, buffers, grads, scatter_turned, scatter_order, first, mid_send, mid, last_send, last,
        (s1_s, s1_r), (s2_s, s2_r), (sz_s, sz_r),
    )

    def to_mate(source, target, index):
        return send(source, target, (col_s, col_r), index, place.col_mate())

    def own_block(i):
        return rows_at(place.col * own_count + i, rows)

    def mate_block(i):
        return rows_at((1 - place.col) * own_count + i, rows)

    def near(i):
        return pl.ds(i * rows, rows) if isinstance(i, int) else rows_at(i, rows)

    def mate_first(t):
        return lax.rem((1 - place.col) * own_count + t, blocks)

    own_cols = pl.ds(pl.multiple_of(place.col * part, 128), part)
    own_half = pl.ds(pl.multiple_of(place.col * (length // 2), rows), length // 2)
    mate_half = pl.ds(pl.multiple_of((1 - place.col) * (length // 2), rows), length // 2)
    token_own = pltpu.make_async_copy(token_part, token.at[:, own_cols], half_sem.at[0])
    token_sent = to_mate(token_part, token.at[:, own_cols], 0)
    cot_own = pltpu.make_async_copy(cot_part.at[own_half], cot.at[:, own_cols], half_sem.at[1])
    cot_sent = to_mate(cot_part.at[mate_half], cot.at[:, own_cols], 1)

    def attn_swap(i):
        return to_mate(total.at[mate_block(i)], arrive_a.at[near(i)], 2 + i)

    def normed_swap(i):
        return to_mate(low.at[own_block(i)], low.at[own_block(i)], 2 + own_count + i)

    def dense_swap(i):
        return to_mate(total.at[mate_block(i)], arrive_b.at[near(i)], 2 + 2 * own_count + i)

    def grad_swap(i):
        return to_mate(low.at[own_block(i)], low.at[own_block(i)], 2 + 3 * own_count + i)

    def hidden_swap(i):
        return to_mate(total.at[mate_block(i)], arrive_a.at[near(i)], 2 + 4 * own_count + i)

    def attn_grad_swap(i):
        return to_mate(low.at[own_block(i)], low.at[own_block(i)], 2 + 5 * own_count + i)

    def layer_swap(i):
        return to_mate(stage.at[1, near(i)], layer_out.at[own_block(i)], 2 + 6 * own_count + i)

    def token_swap(b):
        return to_mate(total.at[near(b), pl.ds(0, part)], token_recv.at[near(b)], 2 + 7 * own_count + b)

    small_swap = 2 + 7 * own_count + blocks

    def layer_put(i):
        return pltpu.make_async_copy(stage.at[0, near(i)], layer_out.at[own_block(i)], out_sem.at[i])

    gather.begin()
    for copy in (token_own, token_sent, cot_own, cot_sent):
        copy.start()
    sums[...] = jnp.zeros_like(sums)
    unit_sums[...] = jnp.zeros_like(unit_sums)
    head_sums[...] = jnp.zeros_like(head_sums)
    token_own.wait()
    token_sent.wait_recv()

    @pl.loop(0, blocks)
    def _(b):
        at = rows_at(b, rows)
        token_t[:, at] = token[at, :].T

    value_t, ctx_t = pair_low, pair_wide
    lane_head = lax.broadcasted_iota(jnp.int32, (1, pair), 1) // size
    for p in range(pairs):
        gather.need(p)
        query_row = query_bias[:, p * pair : (p + 1) * pair]
        bias = jnp.concatenate(
            [query_row, jnp.zeros_like(query_row), value_bias[:, p * pair : (p + 1) * pair]], axis=1
        )

        @pl.loop(0, blocks)
        def _(b, p=p, bias=bias):
            at = rows_at(b, rows)
            made = dot_nn(token[at, :], wa[p]) + bias
            qkv[p, at, :] = made.astype(low_type)
            value_t[:, at] = made[:, 2 * pair :].T.astype(low_type)
            key_t[p, :, at] = made[:, pair : 2 * pair].T.astype(low_type)

        pace = gather_pace[min(p, len(gather_pace) - 2)]
        gather.advance(pace[0])

        @pl.loop(0, 2)
        def _(h, p=p, pace=pace):
            own = jnp.where(lane_head == h, size ** (-0.5), 0.0).astype(low_type)
            head_rows = rows_at(h, size)
            for b in range(blocks):
                query = qkv[p, b * rows : (b + 1) * rows, :pair] * own
                tiles, masked = [], key_tiles(b, rows, cut.prefix_most)
                for tile, needs in masked:
                    score = dot_nt(qkv[p, tile * rows : (tile + 1) * rows, pair : 2 * pair], query)
                    tiles.append(masked_tile(score, b * rows, tile * rows, prefix) if needs else score)
                peak = tiles[0].max(axis=0, keepdims=True)
                for score in tiles[1:]:
                    peak = jnp.maximum(peak, score.max(axis=0, keepdims=True))
                row_total = jnp.zeros_like(peak)
                weights = []
                for score in tiles:
                    weights.append(jnp.exp(score - peak))
                    row_total = row_total + weights[-1].sum(axis=0, keepdims=True)
                share = 1.0 / row_total
                found = jnp.zeros((size, rows), wide)
                for (tile, _), weight in zip(masked, weights):
                    found = found + dot_nn(
                        value_t[head_rows, tile * rows : (tile + 1) * rows], (weight * share).astype(low_type)
                    )
                ctx_t[head_rows, b * rows : (b + 1) * rows] = found
                lse[2 * p + h, :, b * rows : (b + 1) * rows] = peak + jnp.log(row_total)
                for now in range(2):
                    if b % 2 and pace[1 + 2 * now + b // 2]:

                        @pl.when(h == now)
                        def _():
                            gather.advance(pace[1 + 2 * now + b // 2])

        @pl.loop(0, blocks)
        def _(b, p=p):
            at = rows_at(b, rows)
            ctx[at, p * pair : (p + 1) * pair] = ctx_t[:, at].T.astype(low_type)

    gather.need(pairs)
    gate_columns = gate_row(head_gate, heads, size)
    gate_low = gate_columns.astype(low_type)

    @pl.loop(0, blocks)
    def _(t):
        at = rows_at(mate_first(t), rows)
        total[at, :] = dot_nt(ctx[at, :] * gate_low, wa[pairs])

        @pl.when(t < own_count)
        def _():
            attn_swap(t).start()

    gather.advance(gather_pace[-1][0])
    gate_cols = attn_gate * hidden
    for i in range(own_count):
        attn_swap(i).wait_recv()

        @pl.loop(i * rows // fine, (i + 1) * rows // fine)
        def _(k):
            here = rows_at(k, fine)
            at = pl.ds(pl.multiple_of(place.col * (length // 2) + k * fine, fine), fine)
            attn = total[at, :] + arrive_a[here, :] + out_bias
            attn_out[here, :] = attn
            normed, _ = norm_parts(token[at, :].astype(wide) + gate_cols * attn)
            out = normed * first_gain + first_shift
            second[here, :] = out
            low[at, :] = out.astype(low_type)

        normed_swap(i).start()
    gather.advance(gather_pace[-1][1])

    masks = [unit_row[:, j * group : (j + 1) * group] for j in range(2)]
    for j in range(2):
        gather.need(pairs + 1 + 2 * j)
        bias_row = up_bias[:, j * group : (j + 1) * group]

        @pl.loop(0, blocks)
        def _(t, j=j, bias_row=bias_row):
            at = rows_at(lax.rem(place.col * own_count + t, blocks), rows)
            if j == 0:

                @pl.when(t == own_count)
                def _():
                    for i in range(own_count):
                        normed_swap(i).wait_recv()

            pre = dot_nn(low[at, :], wm[2 * j]) + bias_row
            share = 0.5 * (1.0 + lax.erf(pre * (2.0 ** -0.5)))
            gelu[j, at, :] = (pre * share).astype(low_type)
            density = jnp.exp(-0.5 * pre * pre) * ((2.0 * math.pi) ** -0.5)
            slope[j, at, :] = (share + pre * density).astype(low_type)
            if j == 0:
                normed_t[:, at] = low[at, :].T

        if j == 0:
            for i in range(own_count):
                attn_swap(i).wait_send()
                normed_swap(i).wait_send()
        gather.need(pairs + 2 + 2 * j)

        @pl.loop(0, blocks)
        def _(t, j=j):
            at = rows_at(mate_first(t), rows)
            made = dot_nt(gelu[j, at, :] * masks[j].astype(low_type), wm[2 * j + 1])
            if j == 0:
                total[at, :] = made
            else:
                total[at, :] += made

                @pl.when(t < own_count)
                def _():
                    dense_swap(t).start()

    cot_own.wait()
    cot_sent.wait_recv()
    for i in range(own_count):
        dense_swap(i).wait_recv()

        @pl.loop(i * rows // fine, (i + 1) * rows // fine)
        def _(k):
            here = rows_at(k, fine)
            at = pl.ds(pl.multiple_of(place.col * (length // 2) + k * fine, fine), fine)
            dense = total[at, :] + arrive_b[here, :] + down_bias
            normed, inverse = norm_parts(second[here, :] + dense_gate * hidden * dense)
            full = normed * second_gain + second_shift
            stage[0, here, :] = jnp.where(place.col == 0, full[:, :part], full[:, part:])
            stage[1, here, :] = jnp.where(place.col == 0, full[:, part:], full[:, :part])
            grad = cot[here, :].astype(wide)
            scaled = grad * second_gain
            one = jnp.mean(scaled, axis=1, keepdims=True)
            two = jnp.mean(scaled * normed, axis=1, keepdims=True)
            made = inverse * (scaled - one - normed * two)
            second[here, :] = made
            gated = (dense_gate * hidden * made).astype(low_type)
            low[at, :] = gated
            sums[0] += fold_rows(grad * normed)
            sums[1] += fold_rows(grad)
            sums[2] += fold_rows(gated.astype(wide))
            sums[3] += fold_rows(dense * made)

        grad_swap(i).start()
        dense_t[:, own_block(i)] = low[own_block(i), :].T
    for i in range(own_count):
        layer_swap(i).start()
        layer_put(i).start()
        grad_swap(i).wait_recv()
        dense_t[:, mate_block(i)] = low[mate_block(i), :].T

    def product(target, left, right, mask=None):
        @pl.loop(0, width // rows)
        def _(i):
            at = rows_at(i, rows)
            made = dot_nn(left[at, :], right[...])
            target[at, :] = (made if mask is None else made * mask).astype(low_type)

    for j in range(2):
        product(buffers[j], dense_t, gelu.at[j], masks[j])
        scatter.begin(j)
    for i in range(own_count):
        dense_swap(i).wait_send()
    for j in range(2):

        @pl.loop(0, blocks)
        def _(t, j=j):
            at = rows_at(mate_first(t), rows)
            inner = dot_nn(low[at, :], wm[2 * j + 1]).astype(low_type).astype(wide)
            unit_sums[2 + j] += fold_rows(gelu[j, at, :].astype(wide) * inner)
            pre = (masks[j] * inner * slope[j, at, :].astype(wide)).astype(low_type)
            slope[j, at, :] = pre
            unit_sums[j] += fold_rows(pre.astype(wide))
            made = dot_nt(pre, wm[2 * j])
            if j == 0:
                total[at, :] = made
            else:
                total[at, :] += made

                @pl.when(t < own_count)
                def _():
                    hidden_swap(t).start()

        scatter.advance(scatter_pace[0][j])
        product(buffers[2 + j], normed_t, slope.at[j])
        scatter.begin(2 + j)

    for i in range(own_count):
        grad_swap(i).wait_send()
    for i in range(own_count):
        hidden_swap(i).wait_recv()

        @pl.loop(i * rows // fine, (i + 1) * rows // fine)
        def _(k):
            here = rows_at(k, fine)
            at = pl.ds(pl.multiple_of(place.col * (length // 2) + k * fine, fine), fine)
            attn = attn_out[here, :]
            normed, inverse = norm_parts(token[at, :].astype(wide) + gate_cols * attn)
            grad = second[here, :] + (total[at, :] + arrive_a[here, :])
            scaled = grad * first_gain
            one = jnp.mean(scaled, axis=1, keepdims=True)
            two = jnp.mean(scaled * normed, axis=1, keepdims=True)
            made = inverse * (scaled - one - normed * two)
            second[here, :] = made
            gated = (gate_cols * made).astype(low_type)
            low[at, :] = gated
            sums[4] += fold_rows(grad * normed)
            sums[5] += fold_rows(grad)
            sums[6] += fold_rows(gated.astype(wide))
            sums[7] += fold_rows(attn * made)

        attn_grad_swap(i).start()
        dense_t[:, own_block(i)] = low[own_block(i), :].T
        scatter.advance(scatter_pace[1][i])
    for i in range(own_count):
        attn_grad_swap(i).wait_recv()
        dense_t[:, mate_block(i)] = low[mate_block(i), :].T

    @pl.loop(0, blocks)
    def _(b):
        at = rows_at(b, rows)
        gated = dot_nn(low[at, :], wa[pairs]).astype(low_type).astype(wide)
        seen = ctx[at, :].astype(wide)
        head_sums[...] += fold_rows(seen * gated)
        ctx_grad[at, :] = (gated * gate_columns).astype(low_type)
        ctx[at, :] = (seen * gate_columns).astype(low_type)

    product(buffers[4], dense_t, ctx)
    scatter.begin(4)
    scatter.advance(scatter_pace[2][0])
    for i in range(own_count):
        hidden_swap(i).wait_send()
        layer_put(i).wait()
        layer_swap(i).wait()
    query_t = pair_wide
    bias_sums = []
    for p in range(pairs):

        key_grad[...] = jnp.zeros_like(key_grad)
        value_grad[...] = jnp.zeros_like(value_grad)
        pace = scatter_pace[3 + min(p, len(scatter_pace) - 4)]

        @pl.loop(0, 2)
        def _(h, p=p, pace=pace):
            own = jnp.where(lane_head == h, size ** (-0.5), 0.0).astype(low_type)
            one_head = jnp.where(lane_head == h, 1.0, 0.0).astype(low_type)
            head_rows = rows_at(h, size)
            for b in range(blocks):
                query = qkv[p, b * rows : (b + 1) * rows, :pair] * own
                context = ctx_grad[b * rows : (b + 1) * rows, p * pair : (p + 1) * pair] * one_head
                logs = lse[2 * p + h, :, b * rows : (b + 1) * rows]
                inner = jnp.zeros_like(logs)
                kept, masked = [], key_tiles(b, rows, cut.prefix_most)
                for tile, needs in masked:
                    score = dot_nt(qkv[p, tile * rows : (tile + 1) * rows, pair : 2 * pair], query)
                    score = masked_tile(score, b * rows, tile * rows, prefix) if needs else score
                    prob = jnp.exp(score - logs)
                    grad_prob = dot_nt(qkv[p, tile * rows : (tile + 1) * rows, 2 * pair :], context)
                    inner = inner + (prob * grad_prob).sum(axis=0, keepdims=True)
                    kept.append((prob, grad_prob))
                found = jnp.zeros((size, rows), wide)
                for (tile, _), (prob, grad_prob) in zip(masked, kept):
                    at = slice(tile * rows, (tile + 1) * rows)
                    grad_score = (prob * (grad_prob - inner)).astype(low_type)
                    value_grad[at, :] += dot_nn(prob.astype(low_type), context)
                    key_grad[at, :] += dot_nn(grad_score, query)
                    found = found + dot_nn(key_t[p, head_rows, at], grad_score)
                query_t[head_rows, b * rows : (b + 1) * rows] = found * size ** (-0.5)
                for now in range(2):
                    if b % 2 and pace[2 * now + b // 2]:

                        @pl.when(h == now)
                        def _():
                            scatter.advance(pace[2 * now + b // 2])

        query_sum = jnp.zeros((8, pair), wide)
        value_sum = jnp.zeros((8, pair), wide)
        for b in range(blocks):
            at = pl.ds(b * rows, rows)
            query_low = query_t[:, at].T.astype(low_type)
            value_low = value_grad[at, :].astype(low_type)
            qkv[p, at, :pair] = query_low
            qkv[p, at, pair : 2 * pair] = key_grad[at, :].astype(low_type)
            qkv[p, at, 2 * pair :] = value_low
            query_sum += fold_rows(query_low.astype(wide))
            value_sum += fold_rows(value_low.astype(wide))
        bias_sums.append((query_sum, value_sum))
        product(buffers[5 + p], token_t, qkv.at[p])
        scatter.begin(5 + p)
        scatter.advance(pace[4])

    @pl.loop(0, blocks)
    def _(t):
        b = mate_first(t)
        at = rows_at(b, rows)
        made = dot_nt(qkv[0, at, :], wa[0])
        for p in range(1, pairs):
            made = made + dot_nt(qkv[p, at, :], wa[p])
        kept = second[rows_at(lax.rem(t, own_count), rows), :]
        made = made + jnp.where(t >= own_count, kept, 0.0)
        total[at, :part] = jnp.where(place.col == 0, made[:, part:], made[:, :part])
        total[at, part:] = jnp.where(place.col == 0, made[:, :part], made[:, part:])
        token_swap(b).start()

    def whole(values):
        return jnp.sum(values, axis=0, keepdims=True)

    dense_col, attn_col = whole(sums[3]), whole(sums[7])
    seq_lane = lax.broadcasted_iota(jnp.int32, (1, width), 1)
    here = place.dp * place.row_size + place.row
    dense_all = jnp.sum(dense_col * hidden, axis=1, keepdims=True)
    attn_all = jnp.sum(attn_col * hidden, axis=1, keepdims=True)
    seq_row = jnp.where(seq_lane == here, attn_all, 0.0) + jnp.where(seq_lane == here + width // 2, dense_all, 0.0)
    small[0:1, :] = whole(sums[6])
    small[1:2, :] = whole(sums[2])
    small[2:3, :] = whole(sums[4])
    small[3:4, :] = whole(sums[5])
    small[4:5, :] = whole(sums[0])
    small[5:6, :] = whole(sums[1])
    small[6:7, :] = dense_gate * dense_col + attn_gate * attn_col
    small[7:8, :] = seq_row
    for j in range(4):
        small[8 + j : 9 + j, :] = whole(unit_sums[j])
    for p in range(pairs):
        small[12:13, p * pair : (p + 1) * pair] = whole(bias_sums[p][0])
        small[12:13, part + p * pair : part + (p + 1) * pair] = whole(bias_sums[p][1])
    small[13:14, :part] = whole(head_sums[...])
    small[13:14, part:] = jnp.zeros((1, part), wide)
    small[14:16, :] = jnp.zeros((2, width), wide)
    copy_c = to_mate(small.at[pl.ds(0, 8)], small_c.at[0, pl.ds(0, 8)], small_swap)
    copy_c.start()
    copy_c.wait_recv()
    small_c[1, 0:8, :] = small[0:8, :] + small_c[0, 0:8, :]
    small_c[1, 8:16, :] = small[8:16, :]
    copy_x = send(small_c.at[1], small_x.at[0], (small_s, small_r), 0, place.x_mate())
    copy_x.start()
    scatter.advance(1)
    copy_x.wait_recv()
    small_x[1] = small_c[1] + small_x[0]
    copy_y = send(small_x.at[1], small_y.at[0], (small_s, small_r), 1, place.y_mate())
    copy_y.start()
    scatter.advance(1)
    copy_y.wait_recv()
    mine = small_x[1] + small_y[0]
    small_y[1] = mine
    small_z[place.row] = mine
    copies = [
        send(small_y.at[1], small_z.at[place.row], (small_s, small_r), 1 + step, place.row_mate(step))
        for step in range(1, cut.row_size)
    ]
    for copy in copies:
        copy.start()
    for b in range(blocks):
        token_swap(b).wait_recv()
        found = total[near(b), part:] + token_recv[near(b), :]
        stage[b // own_count, near(b % own_count), :] = found
        pltpu.make_async_copy(
            stage.at[b // own_count, near(b % own_count)], token_out.at[near(b)], out_sem.at[own_count + b]
        ).start()
    scatter.finish()
    for copy in copies:
        copy.wait_recv()
    result = small_z[0]
    for z in range(1, cut.row_size):
        result = result + small_z[z]
    small_out[...] = result
    gather.finish()
    for copy in [token_sent, cot_sent, copy_c, copy_x, copy_y] + copies:
        copy.wait_send()
    for i in range(own_count):
        attn_grad_swap(i).wait_send()
    for b in range(blocks):
        token_swap(b).wait_send()
        pltpu.make_async_copy(
            stage.at[b // own_count, near(b % own_count)], token_out.at[near(b)], out_sem.at[own_count + b]
        ).wait()


def place_kernel(cut, layer_in, token_in, small, down_0, down_1, up_0, up_1, grad_out_t, *rest):
    pairs, pair, part, width = cut.heads // 2, 2 * cut.size, cut.part_width, cut.width
    pieces, rest = rest[:pairs], rest[pairs:]
    (
        layer_out, token_out, grad_qkv, grad_out, grad_up, grad_down, query_bias, value_bias, out_bias, up_bias,
        down_bias, first_gain, first_shift, second_gain, second_shift, head, hidden, unit, attention, feedforward,
        held, in_sem, out_sem,
    ) = rest
    count = held.shape[1]
    step = layer_in.shape[0] // count
    moves = []
    for a, (source, target) in enumerate(((layer_in, layer_out), (token_in, token_out))):
        for i in range(count):
            at = pl.ds(i * step, step)
            into = pltpu.make_async_copy(source.at[at], held.at[a, i], in_sem.at[a, i])
            into.start()
            moves.append((into, pltpu.make_async_copy(held.at[a, i], target.at[at], out_sem.at[a, i])))
    for into, out in moves:
        into.wait()
        out.start()
    group = cut.units // 2
    for p, piece in enumerate(pieces):
        for k in range(3):
            grad_qkv[k, :, p * pair : (p + 1) * pair] = piece[:, k * pair : (k + 1) * pair]
    grad_out[...] = grad_out_t[...]
    for j, (up, down) in enumerate(((up_0, down_0), (up_1, down_1))):
        grad_up[:, j * group : (j + 1) * group] = up[...]
        grad_down[:, j * group : (j + 1) * group] = down[...]

    def flat(target, values):
        target[...] = values.reshape(target.shape)

    flat(up_bias, jnp.concatenate([small[8:9, :], small[9:10, :]], axis=1))
    flat(unit, jnp.concatenate([small[10:11, :], small[11:12, :]], axis=1))
    flat(query_bias, small[12:13, :part])
    flat(value_bias, small[12:13, part:])
    for row, target in enumerate((out_bias, down_bias, first_gain, first_shift, second_gain, second_shift, hidden)):
        flat(target, small[row : row + 1, :])
    lane = lax.broadcasted_iota(jnp.int32, (1, part), 1) // cut.size
    slot = lax.broadcasted_iota(jnp.int32, (1, cut.heads), 1)
    found = jnp.zeros((1, cut.heads), wide)
    for h in range(cut.heads):
        one = jnp.sum(jnp.where(lane == h, small[13:14, :part], 0.0), axis=1, keepdims=True)
        found = jnp.where(slot == h, one, found)
    flat(head, found)
    seq_total = attention.shape[0]
    flat(attention, small[7:8, :seq_total])
    flat(feedforward, small[7:8, width // 2 : width // 2 + seq_total])
    for _, out in moves:
        out.wait()


gather_turned = (5, 7)
scatter_turned = (0,)
gather_order = ((-1, 0), (-1, 1), (0, 0), (-1, 2), (0, 1), (-1, 3), (1, 0), (0, 2), (-1, 4), (1, 1), (2, 0), (0, 3), (-1, 5), (1, 2), (2, 1), (0, 4), (-1, 6), (1, 3), (2, 2), (0, 5), (-1, 7), (1, 4), (2, 3), (0, 6), (1, 5), (2, 4), (0, 7), (1, 6), (2, 5), (1, 7), (2, 6), (2, 7))
scatter_order = ((0, 0), (0, 1), (0, 2), (1, 0), (1, 1), (0, 3), (0, 4), (1, 2), (2, 0), (0, 5), (1, 3), (1, 4), (0, 6), (1, 5), (0, 7), (1, 6), (2, 1), (1, 7), (2, 3), (2, 4), (2, 6), (2, 5), (2, 2), (2, 7))
gather_pace = ((3, 0, 0, 0, 3), (1, 3, 0, 0, 1), (0, 0, 1, 3, 2), (0, 2))
scatter_pace = ((0, 1), (0, 1), (0,), (1, 0, 0, 1, 1), (1, 1, 1, 1, 0), (1, 1, 1, 2, 0))


class Cut(NamedTuple):
    length: int
    width: int
    part_width: int
    heads: int
    size: int
    units: int
    part: int
    row_size: int
    rows: int
    fine: int
    prefix_most: int


def any_spec():
    return pl.BlockSpec(memory_space=pl.ANY)


def vmem_spec():
    return pl.BlockSpec(memory_space=pltpu.VMEM)


def smem_spec():
    return pl.BlockSpec(memory_space=pltpu.SMEM)


def like(items):
    return [jax.ShapeDtypeStruct(shape, kind) for shape, kind in items]


def scratch(items):
    return [pltpu.VMEM(shape, kind) for shape, kind in items]


def dma(*shape):
    return pltpu.SemaphoreType.DMA(shape)


vmem_most = 67043328


def run_layer(cut, *args):
    length, width, half = cut.length, cut.width, cut.part_width
    group = cut.units // 2
    pairs = cut.heads // 2
    blocks = length // cut.rows
    columns = [group] * 4 + [half] * (pairs + 1)
    count = len(columns)
    outs = [((length, half), wide), ((length, half), wide), ((16, width), wide)]
    outs += [((cut.part, n), wide) for n in columns]
    own = [
        ((pairs + 1, width, half), low_type),
        ((4, width, group), low_type),
        ((length, width), low_type),
        ((width, length), low_type),
        ((pairs, length, half), low_type),
        ((cut.heads, 1, length), wide),
        ((length, half), low_type),
        ((length // 2, width), wide),
        ((width, length), low_type),
        ((2, length, group), low_type),
        ((2, length, group), low_type),
        ((length // 2, width), wide),
        ((length, width), low_type),
        ((width, length), low_type),
        ((8, 8, width), wide),
        ((length // 2, width), low_type),
        ((length, width), wide),
        ((length // 2, width), wide),
        ((length // 2, width), wide),
        ((2, length // 2, half), wide),
        ((length, half), wide),
        ((length, half), low_type),
        ((length, 2 * cut.size), wide),
        ((length, 2 * cut.size), wide),
        ((2 * cut.size, length), wide),
        ((2 * cut.size, length), low_type),
        ((pairs, 2 * cut.size, length), low_type),
        ((pairs + 1, cut.part, half), low_type),
        ((4, cut.part, group), low_type),
        ((16, width), wide),
        ((2, 16, width), wide),
        ((2, 16, width), wide),
        ((2, 16, width), wide),
        ((cut.row_size, 16, width), wide),
        ((4, 8, width), wide),
        ((8, half), wide),
    ]
    quarter = cut.part * cut.row_size // 2
    own += [((width, n), low_type) for n in columns]
    z = cut.row_size - 1
    turned = [c in scatter_turned for c in range(count)]
    both = list(zip(columns, turned))
    own += [((2, 2, 2 * quarter, n // 2) if turn else (2, 2, quarter, n), low_type) for n, turn in both]
    own += [((4, 2 * quarter, n // 2) if turn else (2, quarter, n), low_type) for n, turn in both]
    own += [((z, 4, cut.part, n // 2) if turn else (2, quarter, n), low_type) for n, turn in both]
    own += [((2, cut.part, n // 2) if turn else (2 * quarter, n), low_type) for n, turn in both]
    own += [((2, cut.part, n // 2) if turn else (z, cut.part, n), low_type) for n, turn in both]
    semaphores = [dma(count), dma(count, z), dma(count, z), dma(count, 2), dma(count, 2), dma(count, 4), dma(count, 4)]
    semaphores += [dma(count, 2 * z), dma(count, 2 * z), dma(2), dma(blocks // 2 + blocks)]
    semaphores += [dma(count, 4), dma(count, 4), dma(count, 2), dma(count, 2), dma(count, z), dma(count, z)]
    pair_swaps = 3 + 7 * (blocks // 2) + blocks
    semaphores += [dma(pair_swaps), dma(pair_swaps), dma(2 + z), dma(2 + z)]
    return pl.pallas_call(
        partial(layer_kernel, cut),
        out_shape=like(outs),
        in_specs=[any_spec()] * 2 + [vmem_spec()] * (len(args) - 6) + [smem_spec()] * 4,
        out_specs=[any_spec()] * 2 + [vmem_spec()] * (len(outs) - 2),
        scratch_shapes=scratch(own) + semaphores,
        compiler_params=pltpu.CompilerParams(collective_id=0, has_side_effects=True, vmem_limit_bytes=vmem_most),
        name="whole_layer",
    )(*args)


def fused_device(
    cut,
    tokens, cotangent, qkv_weight, out_weight, up_weight, down_weight, query_bias, value_bias, out_bias, up_bias,
    down_bias, first_gain, first_shift, second_gain, second_shift, head_gate, hidden_gate, intermediate_gate,
    attention_gate, feedforward_gate, prefix_length,
):
    half, width, units, part = cut.part_width, cut.width, cut.units, cut.part
    rows = [
        query_bias, value_bias, out_bias, up_bias, down_bias, first_gain, first_shift, second_gain, second_shift,
        hidden_gate, intermediate_gate,
    ]
    scalars = [head_gate, attention_gate, feedforward_gate, prefix_length]
    weights = [qkv_weight, out_weight.T, up_weight, down_weight.T]
    made = run_layer(cut, tokens, cotangent, *weights, *rows, *scalars)
    seq_total = lax.axis_size(("dp", "row"))
    lanes = [half, half, width, units, width, width, width, width, width, cut.heads, width, units, seq_total, seq_total]
    shapes = [(3, part, half), (part, half), (part, units), (part, units)] + [(n,) for n in lanes]
    whole = (cut.length, half)
    layer_out, grad_tokens, *outs = pl.pallas_call(
        partial(place_kernel, cut),
        out_shape=like([(shape, wide) for shape in [whole, whole] + shapes]),
        in_specs=[any_spec()] * 2 + [vmem_spec()] * (len(made) - 2),
        out_specs=[any_spec()] * 2 + [vmem_spec()] * len(shapes),
        scratch_shapes=[pltpu.VMEM((2, 4, cut.length // 4, half), wide), dma(2, 4), dma(2, 4)],
        name="place_results",
    )(*made)
    return (layer_out, grad_tokens, outs[0], outs[1].T, outs[2], outs[3].T, *outs[4:])


def cut_of(args):
    tokens, qkv_weight, up_weight, head_gate, prefix_length = args[0], args[2], args[4], args[15], args[20]
    length, part_width = tokens.shape
    part, width = qkv_weight.shape[1], args[11].shape[0]
    heads = head_gate.shape[0]
    row_size, dp_size = lax.axis_size("row"), lax.axis_size("dp")
    fits = (
        prefix_length.shape[0] == 1
        and lax.axis_size("col") == 2
        and dp_size == 4
        and row_size % 2 == 0
        and part % 16 == 0
        and heads % 2 == 0
        and part_width == qkv_weight.shape[2]
        and part_width == 3 * (2 * part_width // heads)
        and (2 * part_width // heads) % 128 == 0
        and width % 256 == 0
        and length % 512 == 0
        and up_weight.shape[1] == 2 * width
    )
    if not fits:
        return None
    return Cut(
        length, width, part_width, heads, part_width // heads, up_weight.shape[1], part, row_size, 256, 128, length // 2
    )


def any_device(*args):
    cut = cut_of(args)
    return per_device(*args) if cut is None else fused_device(cut, *args)


def solution(mesh):
    placed = (
        P(("dp", "row"), "col"),
        P(("dp", "row"), "col"),
        P(None, ("dp", "row"), "col"),
        P("col", ("dp", "row")),
        P(("dp", "row"), "col"),
        P("col", ("dp", "row")),
        P("col"),
        P("col"),
        P(),
        P("col"),
        P(),
        P(),
        P(),
        P(),
        P(),
        P("col"),
        P(),
        P("col"),
        P(("dp", "row")),
        P(("dp", "row")),
        P(("dp", "row")),
    )
    return jax.shard_map(
        any_device,
        mesh=mesh,
        in_specs=placed,
        out_specs=(
            P(("dp", "row"), "col"),
            P(("dp", "row"), "col"),
            P(None, ("dp", "row"), "col"),
            P("col", ("dp", "row")),
            P(("dp", "row"), "col"),
            P("col", ("dp", "row")),
            P("col"),
            P("col"),
            P(),
            P("col"),
            P(),
            P(),
            P(),
            P(),
            P(),
            P("col"),
            P(),
            P("col"),
            P(),
            P(),
        ),
        check_vma=False,
    )
```

```python
from functools import partial
import math
from typing import NamedTuple

import jax
import jax.numpy as jnp
from jax import lax
from jax.experimental import pallas as pl
from jax.experimental.pallas import tpu as pltpu
from jax.sharding import PartitionSpec as P

masked_value = -1e30
norm_eps = 1e-05


def norm_forward(values, scale_gain, shift_term):
    centre = jnp.mean(values, axis=1, keepdims=True)
    centred = values - centre
    spread = jnp.mean(centred * centred, axis=1, keepdims=True)
    inverse = lax.rsqrt(spread + norm_eps)
    normed = centred * inverse
    return (normed * scale_gain + shift_term, normed, inverse)


def norm_backward(gradient, normed, inverse, scale_gain):
    scaled = gradient * scale_gain
    first_mean = jnp.mean(scaled, axis=1, keepdims=True)
    second_mean = jnp.mean(scaled * normed, axis=1, keepdims=True)
    return inverse * (scaled - first_mean - normed * second_mean)


def block_mask(start_row, block_rows, length, prefix_value):
    key_index = jnp.arange(length, dtype=jnp.int32)
    query_index = start_row + jnp.arange(block_rows, dtype=jnp.int32)
    return (key_index[None, :] < prefix_value) | (key_index[None, :] <= query_index[:, None])


def block_scores(query_block, key_seq, start_row, prefix_value, scale_factor):
    block_rows = query_block.shape[0]
    length = key_seq.shape[0]
    allowed = block_mask(start_row, block_rows, length, prefix_value)
    scores = (
        jnp.einsum("qhd,khd->hqk", query_block, key_seq, preferred_element_type=jnp.float32)
        * scale_factor
    )
    return jnp.where(allowed[None], scores, masked_value)


def attend_sequence(query_seq, key_seq, value_seq, prefix_value, block_rows, scale_factor):
    length = key_seq.shape[0]
    block_count = length // block_rows
    query_blocks = query_seq.reshape(
        block_count, block_rows, query_seq.shape[1], query_seq.shape[2]
    )
    starts = jnp.arange(block_count, dtype=jnp.int32) * block_rows

    def one_block(element):
        query_block, start_row = element
        scores = block_scores(query_block, key_seq, start_row, prefix_value, scale_factor)
        row_peak = jnp.max(scores, axis=2, keepdims=True)
        exponent = jnp.exp(scores - row_peak)
        row_total = jnp.sum(exponent, axis=2, keepdims=True)
        weights_low = (exponent / row_total).astype(jnp.bfloat16)
        context = jnp.einsum(
            "hqk,khd->qhd", weights_low, value_seq, preferred_element_type=jnp.float32
        )
        return (context, row_peak[..., 0] + jnp.log(row_total[..., 0]))

    contexts, log_totals = lax.map(one_block, (query_blocks, starts))
    return (contexts.reshape(length, query_seq.shape[1], query_seq.shape[2]), log_totals)


def attend_back(
    query_seq, key_seq, value_seq, grad_seq, log_seq, prefix_value, block_rows, scale_factor
):
    length = key_seq.shape[0]
    block_count = length // block_rows
    head_count = query_seq.shape[1]
    head_size = query_seq.shape[2]
    query_blocks = query_seq.reshape(block_count, block_rows, head_count, head_size)
    grad_blocks = grad_seq.reshape(block_count, block_rows, head_count, head_size)
    starts = jnp.arange(block_count, dtype=jnp.int32) * block_rows

    def one_block(running, element):
        grad_keys, grad_values = running
        query_block, grad_block, log_block, start_row = element
        scores = block_scores(query_block, key_seq, start_row, prefix_value, scale_factor)
        probs = jnp.exp(scores - log_block[..., None])
        grad_probs = jnp.einsum(
            "qhd,khd->hqk", grad_block, value_seq, preferred_element_type=jnp.float32
        )
        row_inner = jnp.sum(probs * grad_probs, axis=2, keepdims=True)
        grad_scores = (probs * (grad_probs - row_inner)).astype(jnp.bfloat16)
        grad_query = (
            jnp.einsum("hqk,khd->qhd", grad_scores, key_seq, preferred_element_type=jnp.float32)
            * scale_factor
        )
        grad_keys = (
            grad_keys
            + jnp.einsum(
                "hqk,qhd->khd", grad_scores, query_block, preferred_element_type=jnp.float32
            )
            * scale_factor
        )
        grad_values = grad_values + jnp.einsum(
            "hqk,qhd->khd",
            probs.astype(jnp.bfloat16),
            grad_block,
            preferred_element_type=jnp.float32,
        )
        return ((grad_keys, grad_values), grad_query)

    zeros_kv = jnp.zeros((length, head_count, head_size), jnp.float32)
    (grad_keys, grad_values), grad_query = lax.scan(
        one_block, (zeros_kv, zeros_kv), (query_blocks, grad_blocks, log_seq, starts)
    )
    return (grad_query.reshape(length, head_count, head_size), grad_keys, grad_values)


def per_device(
    tokens,
    cotangent,
    qkv_weight,
    out_weight,
    up_weight,
    down_weight,
    query_bias,
    value_bias,
    out_bias,
    up_bias,
    down_bias,
    first_gain,
    first_shift,
    second_gain,
    second_shift,
    head_gate,
    hidden_gate,
    intermediate_gate,
    attention_gate,
    feedforward_gate,
    prefix_length,
):
    row_count = tokens.shape[0]
    seq_count = prefix_length.shape[0]
    length = row_count // seq_count
    local_heads = head_gate.shape[0]
    head_width = qkv_weight.shape[2]
    head_size = head_width // local_heads
    model_width = first_gain.shape[0]
    part_width = model_width // lax.axis_size("col")
    block_rows = min(512, length)
    scale_factor = head_size ** (-0.5)
    col_index = lax.axis_index("col")
    qkv_low, out_low = (
        lax.all_gather(qkv_weight.astype(jnp.bfloat16), ("dp", "row"), axis=1, tiled=True),
        lax.all_gather(out_weight.astype(jnp.bfloat16), ("dp", "row"), axis=1, tiled=True),
    )
    up_low, down_low = (
        lax.all_gather(up_weight.astype(jnp.bfloat16), ("dp", "row"), axis=0, tiled=True),
        lax.all_gather(down_weight.astype(jnp.bfloat16), ("dp", "row"), axis=1, tiled=True),
    )
    token_full = lax.all_gather(tokens, "col", axis=1, tiled=True)
    projected = jnp.einsum("td,kdf->ktf", token_full, qkv_low, preferred_element_type=jnp.float32)
    query_low = (projected[0] + query_bias).astype(jnp.bfloat16)
    key_low = projected[1].astype(jnp.bfloat16)
    value_low = (projected[2] + value_bias).astype(jnp.bfloat16)

    def split_heads(array):
        return array.reshape(seq_count, length, local_heads, head_size)

    def forward_seq(element):
        query_seq, key_seq, value_seq, prefix_value = element
        return attend_sequence(
            query_seq, key_seq, value_seq, prefix_value, block_rows, scale_factor
        )

    contexts, log_totals = lax.map(
        forward_seq,
        (split_heads(query_low), split_heads(key_low), split_heads(value_low), prefix_length),
    )
    context = contexts.reshape(row_count, head_width)
    gate_columns = jnp.repeat(head_gate.astype(jnp.float32), head_size)
    gated_low = (context * gate_columns).astype(jnp.bfloat16)
    attn_terms = jnp.dot(gated_low, out_low, preferred_element_type=jnp.float32)
    attn_out = lax.psum(attn_terms, "col") + out_bias
    hidden_mask = hidden_gate.astype(jnp.float32)
    attn_rows = jnp.repeat(attention_gate.astype(jnp.float32), length)[:, None]
    dense_rows = jnp.repeat(feedforward_gate.astype(jnp.float32), length)[:, None]
    first_sum = token_full.astype(jnp.float32) + attn_rows * hidden_mask * attn_out
    normed_one, first_normed, first_inverse = norm_forward(first_sum, first_gain, first_shift)
    normed_low = normed_one.astype(jnp.bfloat16)
    pre_act = jnp.dot(normed_low, up_low, preferred_element_type=jnp.float32) + up_bias
    activated, gelu_pull = jax.vjp(partial(jax.nn.gelu, approximate=False), pre_act)
    unit_mask = intermediate_gate.astype(jnp.float32)
    inner_low = (activated * unit_mask).astype(jnp.bfloat16)
    dense_terms = jnp.dot(inner_low, down_low, preferred_element_type=jnp.float32)
    dense_out = lax.psum(dense_terms, "col") + down_bias
    second_sum = normed_one + dense_rows * hidden_mask * dense_out
    layer_full, second_normed, second_inverse = norm_forward(second_sum, second_gain, second_shift)
    layer_out = lax.dynamic_slice_in_dim(layer_full, col_index * part_width, part_width, 1)
    grad_full = lax.all_gather(cotangent, "col", axis=1, tiled=True).astype(jnp.float32)
    grad_gain_two = jnp.sum(grad_full * second_normed, axis=0)
    grad_shift_two = jnp.sum(grad_full, axis=0)
    grad_second = norm_backward(grad_full, second_normed, second_inverse, second_gain)
    grad_dense_low = (dense_rows * hidden_mask * grad_second).astype(jnp.bfloat16)
    dense_product = dense_out * grad_second
    grad_dense_gate = jnp.sum(
        dense_product.reshape(seq_count, length, model_width) * hidden_mask, axis=(1, 2)
    )
    hidden_from_dense = jnp.sum(dense_rows * dense_product, axis=0)
    grad_down_bias = jnp.sum(grad_dense_low.astype(jnp.float32), axis=0)
    up_low, down_low = (
        lax.all_gather(up_weight.astype(jnp.bfloat16), ("dp", "row"), axis=0, tiled=True),
        lax.all_gather(down_weight.astype(jnp.bfloat16), ("dp", "row"), axis=1, tiled=True),
    )
    grad_down = jnp.einsum(
        "tf,td->fd", inner_low, grad_dense_low, preferred_element_type=jnp.float32
    )
    grad_inner_low = jnp.einsum(
        "td,fd->tf", grad_dense_low, down_low, preferred_element_type=jnp.float32
    ).astype(jnp.bfloat16)
    grad_inner = grad_inner_low.astype(jnp.float32)
    grad_unit_gate = jnp.sum(activated * grad_inner, axis=0)
    (grad_pre,) = gelu_pull(unit_mask * grad_inner)
    grad_pre_low = grad_pre.astype(jnp.bfloat16)
    grad_up_bias = jnp.sum(grad_pre_low.astype(jnp.float32), axis=0)
    grad_up = jnp.einsum("td,tf->df", normed_low, grad_pre_low, preferred_element_type=jnp.float32)
    dense_parts = (
        lax.psum_scatter(grad_up, ("dp", "row"), scatter_dimension=0, tiled=True),
        lax.psum_scatter(grad_down, ("dp", "row"), scatter_dimension=1, tiled=True),
    )
    hidden_terms = jnp.einsum("tf,df->td", grad_pre_low, up_low, preferred_element_type=jnp.float32)
    grad_normed = grad_second + lax.psum(hidden_terms, "col")
    grad_gain_one = jnp.sum(grad_normed * first_normed, axis=0)
    grad_shift_one = jnp.sum(grad_normed, axis=0)
    grad_first = norm_backward(grad_normed, first_normed, first_inverse, first_gain)
    grad_attn_low = (attn_rows * hidden_mask * grad_first).astype(jnp.bfloat16)
    attn_product = attn_out * grad_first
    grad_attn_gate = jnp.sum(
        attn_product.reshape(seq_count, length, model_width) * hidden_mask, axis=(1, 2)
    )
    grad_hidden = hidden_from_dense + jnp.sum(attn_rows * attn_product, axis=0)
    grad_out_bias = jnp.sum(grad_attn_low.astype(jnp.float32), axis=0)
    qkv_low, out_low = (
        lax.all_gather(qkv_weight.astype(jnp.bfloat16), ("dp", "row"), axis=1, tiled=True),
        lax.all_gather(out_weight.astype(jnp.bfloat16), ("dp", "row"), axis=1, tiled=True),
    )
    grad_out = jnp.einsum("tc,td->cd", gated_low, grad_attn_low, preferred_element_type=jnp.float32)
    grad_gated_low = jnp.einsum(
        "td,cd->tc", grad_attn_low, out_low, preferred_element_type=jnp.float32
    ).astype(jnp.bfloat16)
    grad_head_cols = jnp.sum(context * grad_gated_low.astype(jnp.float32), axis=0)
    grad_head = jnp.sum(grad_head_cols.reshape(local_heads, head_size), axis=1)
    grad_context = grad_gated_low * gate_columns.astype(jnp.bfloat16)

    def backward_seq(element):
        query_seq, key_seq, value_seq, grad_seq, log_seq, prefix_value = element
        return attend_back(
            query_seq, key_seq, value_seq, grad_seq, log_seq, prefix_value, block_rows, scale_factor
        )

    grad_query, grad_keys, grad_values = lax.map(
        backward_seq,
        (
            split_heads(query_low),
            split_heads(key_low),
            split_heads(value_low),
            split_heads(grad_context),
            log_totals,
            prefix_length,
        ),
    )
    grad_qkv_low = jnp.stack([grad_query, grad_keys, grad_values]).reshape(3, row_count, head_width)
    grad_qkv_low = grad_qkv_low.astype(jnp.bfloat16)
    grad_query_bias = jnp.sum(grad_qkv_low[0].astype(jnp.float32), axis=0)
    grad_value_bias = jnp.sum(grad_qkv_low[2].astype(jnp.float32), axis=0)
    grad_qkv = jnp.einsum(
        "td,ktf->kdf", token_full, grad_qkv_low, preferred_element_type=jnp.float32
    )
    input_terms = jnp.einsum(
        "ktf,kdf->td", grad_qkv_low, qkv_low, preferred_element_type=jnp.float32
    )
    grad_tokens = lax.psum_scatter(
        input_terms.astype(jnp.bfloat16), "col", scatter_dimension=1, tiled=True
    ).astype(jnp.float32)
    grad_tokens = grad_tokens + lax.dynamic_slice_in_dim(
        grad_first, col_index * part_width, part_width, 1
    )
    grad_up_part, grad_down_part = dense_parts
    grad_qkv_part, grad_out_part = (
        lax.psum_scatter(grad_qkv, ("dp", "row"), scatter_dimension=1, tiled=True),
        lax.psum_scatter(grad_out, ("dp", "row"), scatter_dimension=1, tiled=True),
    )
    seq_total = seq_count * lax.axis_size(("dp", "row"))
    seq_start = lax.axis_index(("dp", "row")) * seq_count
    seq_stack = lax.dynamic_update_slice_in_dim(
        jnp.zeros((2, seq_total), jnp.float32),
        jnp.stack([grad_attn_gate, grad_dense_gate]),
        seq_start,
        1,
    )
    full_stack = jnp.stack(
        [
            grad_out_bias,
            grad_down_bias,
            grad_gain_one,
            grad_shift_one,
            grad_gain_two,
            grad_shift_two,
            grad_hidden,
        ]
    )
    half_stack = jnp.stack([grad_query_bias, grad_value_bias])
    unit_stack = jnp.stack([grad_up_bias, grad_unit_gate])
    full_sum, half_sum, unit_sum, head_sum, seq_sum = lax.psum(
        (full_stack, half_stack, unit_stack, grad_head, seq_stack), ("dp", "row")
    )
    return (
        layer_out,
        grad_tokens,
        grad_qkv_part,
        grad_out_part,
        grad_up_part,
        grad_down_part,
        half_sum[0],
        half_sum[1],
        full_sum[0],
        unit_sum[0],
        full_sum[1],
        full_sum[2],
        full_sum[3],
        full_sum[4],
        full_sum[5],
        head_sum,
        full_sum[6],
        unit_sum[1],
        seq_sum[0],
        seq_sum[1],
    )


low_type = jnp.bfloat16
wide = jnp.float32
mesh_ids = pl.DeviceIdType.MESH


def dot_nn(left, right):
    return jnp.dot(left, right, preferred_element_type=wide)


def dot_nt(left, right):
    return lax.dot_general(left, right, (((1,), (1,)), ((), ())), preferred_element_type=wide)


def rows_at(index, count):
    return pl.ds(pl.multiple_of(index * count, count), count)


def fold_rows(values):
    return jnp.sum(values.reshape(values.shape[0] // 8, 8, values.shape[1]), axis=0)


def norm_parts(values):
    centre = jnp.mean(values, axis=1, keepdims=True)
    centred = values - centre
    spread = jnp.mean(centred * centred, axis=1, keepdims=True)
    inverse = lax.rsqrt(spread + norm_eps)
    return centred * inverse, inverse


class Place:
    def __init__(self, row_size):
        self.dp, self.row, self.col = (lax.axis_index(name) for name in ("dp", "row", "col"))
        self.row_size = row_size
        self.x, self.y = lax.rem(self.dp, 2), self.dp // 2
        self.x_dp = self.y * 2 + (1 - self.x)
        self.y_dp = (1 - self.y) * 2 + self.x

    def x_mate(self):
        return {"dp": self.x_dp}

    def y_mate(self):
        return {"dp": self.y_dp}

    def row_mate(self, step):
        return {"row": lax.rem(self.row + step, self.row_size)}

    def col_mate(self):
        return {"col": 1 - self.col}

    def barrier(self):
        semaphore = pltpu.get_barrier_semaphore()
        mates = [self.x_mate(), self.y_mate(), self.col_mate()]
        mates += [self.row_mate(step) for step in range(1, self.row_size)]
        for mate in mates:
            pl.semaphore_signal(semaphore, inc=1, device_id=mate, device_id_type=mesh_ids)
        pl.semaphore_wait(semaphore, len(mates))


def send(source, target, semaphores, index, mate):
    sent, received = semaphores
    return pltpu.make_async_remote_copy(
        src_ref=source,
        dst_ref=target,
        send_sem=sent.at[index],
        recv_sem=received.at[index],
        device_id=mate,
        device_id_type=mesh_ids,
    )


class Gather:
    def __init__(self, place, shards, chunks, turned, order, own_sem, z_sems, two_sems, three_sems, turned_sems):
        self.place, self.shards, self.chunks, self.turned = place, shards, chunks, turned
        self.own_sem, self.z_sems, self.two_sems, self.three_sems = own_sem, z_sems, two_sems, three_sems
        self.turned_sems = turned_sems
        self.part = shards[0].shape[0]
        self.block = self.part * place.row_size
        self.half = self.block // 2
        self.steps, self.done = order, 0

    def block_rows(self, dp):
        return pl.ds(pl.multiple_of(dp * self.block, 16), self.block)

    def half_rows(self, dp, half):
        return pl.ds(pl.multiple_of(dp * self.block + half * self.half, 16), self.half)

    def part_rows(self, dp):
        return pl.ds(pl.multiple_of(dp * self.block + self.place.row * self.part, 16), self.part)

    def half_cols(self, c, half):
        count = self.chunks[c].shape[1] // 2
        return pl.ds(half * count, count)

    def own(self, c):
        rows = self.part_rows(self.place.dp)
        return pltpu.make_async_copy(self.shards[c], self.chunks[c].at[rows], self.own_sem.at[c])

    def along_z(self, c):
        place, rows = self.place, self.part_rows(self.place.dp)
        return [
            send(self.shards[c], self.chunks[c].at[rows], self.z_sems, (c, step - 1), place.row_mate(step))
            for step in range(1, place.row_size)
        ]

    def turned_z(self, c):
        place, found = self.place, []
        for step in range(1, place.row_size):
            for half, dp in ((0, place.x_dp), (1, place.y_dp)):
                at = self.chunks[c].at[self.part_rows(dp), self.half_cols(c, half)]
                found.append(send(at, at, self.turned_sems, (c, 2 * step - 2 + half), place.row_mate(step)))
        return found

    def second(self, c):
        place, chunk, found = self.place, self.chunks[c], []
        for half, mate in ((0, place.x_mate()), (1, place.y_mate())):
            if c in self.turned:
                cols = self.half_cols(c, half)
                source, target = self.shards[c].at[:, cols], chunk.at[self.part_rows(place.dp), cols]
            else:
                source = target = chunk.at[self.half_rows(place.dp, half)]
            found.append(send(source, target, self.two_sems, (c, half), mate))
        return found

    def third(self, c):
        place, chunk, found = self.place, self.chunks[c], []
        for index, (dp, half, mate) in enumerate(
            (
                (place.dp, 0, place.y_mate()),
                (place.dp, 1, place.x_mate()),
                (place.x_dp, 0, place.y_mate()),
                (place.y_dp, 1, place.x_mate()),
            )
        ):
            if c in self.turned:
                at = chunk.at[self.block_rows(dp), self.half_cols(c, half)]
            else:
                at = chunk.at[self.half_rows(dp, half)]
            found.append(send(at, at, self.three_sems, (c, index), mate))
        return found

    def step(self):
        stage, c = self.steps[self.done]
        self.done += 1
        if stage < 0:
            self.own(c).start()
            for copy in self.along_z(c) + (self.second(c) if c in self.turned else []):
                copy.start()
        elif stage == 0 and c in self.turned:
            for copy in self.second(c):
                copy.wait_recv()
            for copy in self.turned_z(c):
                copy.start()
        elif stage == 0:
            self.own(c).wait()
            for copy in self.along_z(c):
                copy.wait_recv()
            for copy in self.second(c):
                copy.start()
        elif stage == 1:
            if c in self.turned:
                self.own(c).wait()
                waits = self.along_z(c) + self.turned_z(c)
            else:
                waits = self.second(c)
            for copy in waits:
                copy.wait_recv()
            for copy in self.third(c):
                copy.start()
        else:
            for copy in self.third(c):
                copy.wait_recv()

    def begin(self):
        while self.steps[self.done][0] < 0:
            self.step()

    def advance(self, count):
        for _ in range(count):
            if self.done < len(self.steps):
                self.step()

    def need(self, c):
        while self.done <= self.steps.index((2, c)):
            self.step()

    def finish(self):
        self.advance(len(self.steps))
        for c in range(len(self.chunks)):
            for copy in self.along_z(c) + self.second(c) + self.third(c):
                copy.wait_send()
            for copy in self.turned_z(c) if c in self.turned else []:
                copy.wait_send()


class Scatter:
    def __init__(
        self, place, chunks, outs, turned, order, first, mid_send, mid, last_send, last, one_sems, two_sems, z_sems
    ):
        self.place, self.chunks, self.outs, self.turned = place, chunks, outs, turned
        self.first, self.mid_send, self.mid, self.last_send, self.last = first, mid_send, mid, last_send, last
        self.one_sems, self.two_sems, self.z_sems = one_sems, two_sems, z_sems
        self.part = outs[0].shape[0]
        self.block = self.part * place.row_size
        self.half = self.block // 2
        self.count = len(chunks)
        self.steps, self.done, self.begun = order, 0, []

    def block_rows(self, dp):
        return pl.ds(pl.multiple_of(dp * self.block, 16), self.block)

    def half_rows(self, dp, half):
        return pl.ds(pl.multiple_of(dp * self.block + half * self.half, 16), self.half)

    def z_rows(self, z):
        return pl.ds(pl.multiple_of(z * self.part, 16), self.part)

    def half_cols(self, c, half):
        count = self.chunks[c].shape[1] // 2
        return pl.ds(half * count, count)

    def one(self, c):
        place, chunk, first = self.place, self.chunks[c], self.first[c]
        found = []
        for i in range(2):
            for half, dp, mate in (
                (0, (1 - place.y) * 2 + i, place.y_mate()),
                (1, i * 2 + (1 - place.x), place.x_mate()),
            ):
                if c in self.turned:
                    at = chunk.at[self.block_rows(dp), self.half_cols(c, half)]
                else:
                    at = chunk.at[self.half_rows(dp, half)]
                found.append(send(at, first.at[half, i], self.one_sems, (c, 2 * half + i), mate))
        return found

    def two(self, c):
        place = self.place
        source, target = (self.last_send[c], self.last[c]) if c in self.turned else (self.mid_send[c], self.mid[c])
        return [
            send(source.at[0], target.at[0], self.two_sems, (c, 0), place.x_mate()),
            send(source.at[1], target.at[1], self.two_sems, (c, 1), place.y_mate()),
        ]

    def along_z(self, c):
        place, found = self.place, []
        for step in range(1, place.row_size):
            rows = self.z_rows(lax.rem(place.row + step, place.row_size))
            if c in self.turned:
                source, target = self.mid_send[c].at[:, rows], self.mid[c].at[step - 1]
            else:
                source, target = self.last_send[c].at[rows], self.last[c].at[step - 1]
            found.append(send(source, target, self.z_sems, (c, step - 1), place.row_mate(step)))
        return found

    def begin(self, c):
        self.begun.append(c)
        for copy in self.one(c):
            copy.start()

    def step(self):
        stage, c = self.steps[self.done]
        self.done += 1
        if c in self.turned:
            self.turned_step(stage, c)
            return
        place, chunk = self.place, self.chunks[c]
        first, mid_send, mid = self.first[c], self.mid_send[c], self.mid[c]
        last_send, last = self.last_send[c], self.last[c]
        if stage == 0:
            for copy in self.one(c):
                copy.wait_recv()
            mid_send[0] = (
                chunk[self.half_rows(place.x_dp, 0), :].astype(wide) + first[0, 1 - place.x].astype(wide)
            ).astype(low_type)
            mid_send[1] = (
                chunk[self.half_rows(place.y_dp, 1), :].astype(wide) + first[1, 1 - place.y].astype(wide)
            ).astype(low_type)
            for copy in self.two(c):
                copy.start()
        elif stage == 1:
            for copy in self.two(c):
                copy.wait_recv()
            for half, slot in ((0, place.x), (1, place.y)):
                last_send[pl.ds(half * self.half, self.half), :] = (
                    chunk[self.half_rows(place.dp, half), :].astype(wide)
                    + first[half, slot].astype(wide)
                    + mid[half].astype(wide)
                ).astype(low_type)
            for copy in self.along_z(c):
                copy.start()
        else:
            total = last_send[self.z_rows(place.row), :].astype(wide)
            for step, copy in enumerate(self.along_z(c)):
                copy.wait_recv()
                total = total + last[step].astype(wide)
            self.outs[c][...] = total

    def turned_step(self, stage, c):
        place, chunk, out = self.place, self.chunks[c], self.outs[c]
        first, mid_send, mid = self.first[c], self.mid_send[c], self.mid[c]
        last_send, last = self.last_send[c], self.last[c]
        if stage == 0:
            for copy in self.one(c):
                copy.wait_recv()
            for half in range(2):
                for i in range(2):
                    dp = place.y * 2 + i if half == 0 else i * 2 + place.x
                    mine = chunk[self.block_rows(dp), self.half_cols(c, half)].astype(wide)
                    mid_send[2 * half + i] = (mine + first[half, i].astype(wide)).astype(low_type)
            for copy in self.along_z(c):
                copy.start()
        elif stage == 1:
            for copy in self.along_z(c):
                copy.wait_recv()
            for half, slot in ((0, place.x), (1, place.y)):
                for index, keep in ((slot, True), (1 - slot, False)):
                    total = mid_send[2 * half + index, self.z_rows(place.row), :].astype(wide)
                    for step in range(place.row_size - 1):
                        total = total + mid[step, 2 * half + index].astype(wide)
                    if keep:
                        out[:, self.half_cols(c, half)] = total
                    else:
                        last_send[half] = total.astype(low_type)
            for copy in self.two(c):
                copy.start()
        else:
            for half, copy in enumerate(self.two(c)):
                copy.wait_recv()
                out[:, self.half_cols(c, half)] += last[half].astype(wide)

    def advance(self, count):
        for _ in range(count):
            if self.done < len(self.steps) and self.steps[self.done][1] in self.begun:
                self.step()

    def finish(self):
        self.advance(len(self.steps))
        for c in range(self.count):
            for copy in self.one(c) + self.two(c) + self.along_z(c):
                copy.wait_send()


def masked_tile(tile, query_start, key_start, prefix):
    key_index = key_start + lax.broadcasted_iota(jnp.int32, tile.shape, 0)
    query_index = query_start + lax.broadcasted_iota(jnp.int32, tile.shape, 1)
    return jnp.where((key_index < prefix) | (key_index <= query_index), tile, masked_value)


def key_tiles(block, rows, prefix_most):
    count = max((block + 1) * rows, prefix_most) // rows
    return [(tile, tile >= block) for tile in range(count)]


def flat_row(ref):
    return ref[...].reshape(1, ref.shape[0])


def gate_row(gates, heads, size):
    head = lax.broadcasted_iota(jnp.int32, (1, heads * size), 1) // size
    row = jnp.zeros((1, heads * size), wide)
    for h in range(heads):
        row = jnp.where(head == h, gates[h].astype(wide), row)
    return row


def layer_kernel(
    cut,
    token_part, cot_part, qkv_w, out_w, up_w, down_w, query_bias, value_bias, out_bias, up_bias, down_bias,
    first_gain, first_shift, second_gain, second_shift, hidden_gate, unit_gate,
    head_gate, attention_gate, feedforward_gate, prefix_length,
    layer_out, token_out, small_out, *rest,
):
    length, width, heads, size = cut.length, cut.width, cut.heads, cut.size
    part, rows, fine = cut.part_width, cut.rows, cut.fine
    blocks = length // rows
    own_count = blocks // 2
    pair = 2 * size
    pairs = heads // 2
    count = pairs + 5
    rest = list(rest)

    def take(number):
        taken = rest[:number]
        del rest[:number]
        return taken

    grads = take(count)
    (wa, wm, token, token_t, qkv, lse, ctx, attn_out, normed_t, gelu, slope, second, low, dense_t, sums) = take(15)
    (cot, total, arrive_a, arrive_b, stage, token_recv, ctx_grad, key_grad, value_grad) = take(9)
    (pair_wide, pair_low, key_t, shards_a, shards_m) = take(5)
    (small, small_c, small_x, small_y, small_z, unit_sums, head_sums) = take(7)
    buffers, first, mid_send, mid, last_send, last = (take(count) for _ in range(6))
    (own_sem, gz_s, gz_r, g2_s, g2_r, g3_s, g3_r, gt_s, gt_r, half_sem, out_sem) = take(11)
    (s1_s, s1_r, s2_s, s2_r, sz_s, sz_r) = take(6)
    (col_s, col_r, small_s, small_r) = take(4)
    group = wm.shape[2]
    place = Place(cut.row_size)
    for p in range(pairs):
        for k in range(3):
            shards_a[p, :, k * pair : (k + 1) * pair] = qkv_w[k, :, p * pair : (p + 1) * pair].astype(low_type)
    shards_a[pairs] = out_w[...].astype(low_type)
    for j in range(2):
        shards_m[2 * j] = up_w[:, j * group : (j + 1) * group].astype(low_type)
        shards_m[2 * j + 1] = down_w[:, j * group : (j + 1) * group].astype(low_type)
    place.barrier()
    prefix = prefix_length[0]
    attn_gate, dense_gate = attention_gate[0].astype(wide), feedforward_gate[0].astype(wide)
    hidden, unit_row = flat_row(hidden_gate).astype(wide), flat_row(unit_gate).astype(wide)
    query_bias, value_bias, up_bias, out_bias, down_bias, first_gain, first_shift, second_gain, second_shift = (
        flat_row(ref)
        for ref in (
            query_bias, value_bias, up_bias, out_bias, down_bias, first_gain, first_shift, second_gain, second_shift
        )
    )
    chunks = [wa.at[i] for i in range(pairs + 1)] + [wm.at[i] for i in range(4)]
    shards = [shards_a.at[i] for i in range(pairs + 1)] + [shards_m.at[i] for i in range(4)]
    gather = Gather(
        place, shards, chunks, gather_turned, gather_order, own_sem, (gz_s, gz_r), (g2_s, g2_r), (g3_s, g3_r),
        (gt_s, gt_r),
    )
    scatter = Scatter(
        place, buffers, grads, scatter_turned, scatter_order, first, mid_send, mid, last_send, last,
        (s1_s, s1_r), (s2_s, s2_r), (sz_s, sz_r),
    )

    def to_mate(source, target, index):
        return send(source, target, (col_s, col_r), index, place.col_mate())

    def own_block(i):
        return rows_at(place.col * own_count + i, rows)

    def mate_block(i):
        return rows_at((1 - place.col) * own_count + i, rows)

    def near(i):
        return pl.ds(i * rows, rows) if isinstance(i, int) else rows_at(i, rows)

    def mate_first(t):
        return lax.rem((1 - place.col) * own_count + t, blocks)

    own_cols = pl.ds(pl.multiple_of(place.col * part, 128), part)
    own_half = pl.ds(pl.multiple_of(place.col * (length // 2), rows), length // 2)
    mate_half = pl.ds(pl.multiple_of((1 - place.col) * (length // 2), rows), length // 2)
    token_own = pltpu.make_async_copy(token_part, token.at[:, own_cols], half_sem.at[0])
    token_sent = to_mate(token_part, token.at[:, own_cols], 0)
    cot_own = pltpu.make_async_copy(cot_part.at[own_half], cot.at[:, own_cols], half_sem.at[1])
    cot_sent = to_mate(cot_part.at[mate_half], cot.at[:, own_cols], 1)

    def attn_swap(i):
        return to_mate(total.at[mate_block(i)], arrive_a.at[near(i)], 2 + i)

    def normed_swap(i):
        return to_mate(low.at[own_block(i)], low.at[own_block(i)], 2 + own_count + i)

    def dense_swap(i):
        return to_mate(total.at[mate_block(i)], arrive_b.at[near(i)], 2 + 2 * own_count + i)

    def grad_swap(i):
        return to_mate(low.at[own_block(i)], low.at[own_block(i)], 2 + 3 * own_count + i)

    def hidden_swap(i):
        return to_mate(total.at[mate_block(i)], arrive_a.at[near(i)], 2 + 4 * own_count + i)

    def attn_grad_swap(i):
        return to_mate(low.at[own_block(i)], low.at[own_block(i)], 2 + 5 * own_count + i)

    def layer_swap(i):
        return to_mate(stage.at[1, near(i)], layer_out.at[own_block(i)], 2 + 6 * own_count + i)

    def token_swap(b):
        return to_mate(total.at[near(b), pl.ds(0, part)], token_recv.at[near(b)], 2 + 7 * own_count + b)

    small_swap = 2 + 7 * own_count + blocks

    def layer_put(i):
        return pltpu.make_async_copy(stage.at[0, near(i)], layer_out.at[own_block(i)], out_sem.at[i])

    gather.begin()
    for copy in (token_own, token_sent, cot_own, cot_sent):
        copy.start()
    sums[...] = jnp.zeros_like(sums)
    unit_sums[...] = jnp.zeros_like(unit_sums)
    head_sums[...] = jnp.zeros_like(head_sums)
    token_own.wait()
    token_sent.wait_recv()

    @pl.loop(0, blocks)
    def _(b):
        at = rows_at(b, rows)
        token_t[:, at] = token[at, :].T

    value_t, ctx_t = pair_low, pair_wide
    lane_head = lax.broadcasted_iota(jnp.int32, (1, pair), 1) // size
    for p in range(pairs):
        gather.need(p)
        query_row = query_bias[:, p * pair : (p + 1) * pair]
        bias = jnp.concatenate(
            [query_row, jnp.zeros_like(query_row), value_bias[:, p * pair : (p + 1) * pair]], axis=1
        )

        @pl.loop(0, blocks)
        def _(b, p=p, bias=bias):
            at = rows_at(b, rows)
            made = dot_nn(token[at, :], wa[p]) + bias
            qkv[p, at, :] = made.astype(low_type)
            value_t[:, at] = made[:, 2 * pair :].T.astype(low_type)
            key_t[p, :, at] = made[:, pair : 2 * pair].T.astype(low_type)

        pace = gather_pace[min(p, len(gather_pace) - 2)]
        gather.advance(pace[0])

        @pl.loop(0, 2)
        def _(h, p=p, pace=pace):
            own = jnp.where(lane_head == h, size ** (-0.5), 0.0).astype(low_type)
            head_rows = rows_at(h, size)
            for b in range(blocks):
                query = qkv[p, b * rows : (b + 1) * rows, :pair] * own
                tiles, masked = [], key_tiles(b, rows, cut.prefix_most)
                for tile, needs in masked:
                    score = dot_nt(qkv[p, tile * rows : (tile + 1) * rows, pair : 2 * pair], query)
                    tiles.append(masked_tile(score, b * rows, tile * rows, prefix) if needs else score)
                peak = tiles[0].max(axis=0, keepdims=True)
                for score in tiles[1:]:
                    peak = jnp.maximum(peak, score.max(axis=0, keepdims=True))
                row_total = jnp.zeros_like(peak)
                weights = []
                for score in tiles:
                    weights.append(jnp.exp(score - peak))
                    row_total = row_total + weights[-1].sum(axis=0, keepdims=True)
                share = 1.0 / row_total
                found = jnp.zeros((size, rows), wide)
                for (tile, _), weight in zip(masked, weights):
                    found = found + dot_nn(
                        value_t[head_rows, tile * rows : (tile + 1) * rows], (weight * share).astype(low_type)
                    )
                ctx_t[head_rows, b * rows : (b + 1) * rows] = found
                lse[2 * p + h, :, b * rows : (b + 1) * rows] = peak + jnp.log(row_total)
                for now in range(2):
                    if b % 2 and pace[1 + 2 * now + b // 2]:

                        @pl.when(h == now)
                        def _():
                            gather.advance(pace[1 + 2 * now + b // 2])

        @pl.loop(0, blocks)
        def _(b, p=p):
            at = rows_at(b, rows)
            ctx[at, p * pair : (p + 1) * pair] = ctx_t[:, at].T.astype(low_type)

    gather.need(pairs)
    gate_columns = gate_row(head_gate, heads, size)
    gate_low = gate_columns.astype(low_type)

    @pl.loop(0, blocks)
    def _(t):
        at = rows_at(mate_first(t), rows)
        total[at, :] = dot_nt(ctx[at, :] * gate_low, wa[pairs])

        @pl.when(t < own_count)
        def _():
            attn_swap(t).start()

    gather.advance(gather_pace[-1][0])
    gate_cols = attn_gate * hidden
    for i in range(own_count):
        attn_swap(i).wait_recv()

        @pl.loop(i * rows // fine, (i + 1) * rows // fine)
        def _(k):
            here = rows_at(k, fine)
            at = pl.ds(pl.multiple_of(place.col * (length // 2) + k * fine, fine), fine)
            attn = total[at, :] + arrive_a[here, :] + out_bias
            attn_out[here, :] = attn
            normed, _ = norm_parts(token[at, :].astype(wide) + gate_cols * attn)
            out = normed * first_gain + first_shift
            second[here, :] = out
            low[at, :] = out.astype(low_type)

        normed_swap(i).start()
    gather.advance(gather_pace[-1][1])

    masks = [unit_row[:, j * group : (j + 1) * group] for j in range(2)]
    for j in range(2):
        gather.need(pairs + 1 + 2 * j)
        bias_row = up_bias[:, j * group : (j + 1) * group]

        @pl.loop(0, blocks)
        def _(t, j=j, bias_row=bias_row):
            at = rows_at(lax.rem(place.col * own_count + t, blocks), rows)
            if j == 0:

                @pl.when(t == own_count)
                def _():
                    for i in range(own_count):
                        normed_swap(i).wait_recv()

            pre = dot_nn(low[at, :], wm[2 * j]) + bias_row
            share = 0.5 * (1.0 + lax.erf(pre * (2.0 ** -0.5)))
            gelu[j, at, :] = (pre * share).astype(low_type)
            density = jnp.exp(-0.5 * pre * pre) * ((2.0 * math.pi) ** -0.5)
            slope[j, at, :] = (share + pre * density).astype(low_type)
            if j == 0:
                normed_t[:, at] = low[at, :].T

        if j == 0:
            for i in range(own_count):
                attn_swap(i).wait_send()
                normed_swap(i).wait_send()
        gather.need(pairs + 2 + 2 * j)

        @pl.loop(0, blocks)
        def _(t, j=j):
            at = rows_at(mate_first(t), rows)
            made = dot_nt(gelu[j, at, :] * masks[j].astype(low_type), wm[2 * j + 1])
            if j == 0:
                total[at, :] = made
            else:
                total[at, :] += made

                @pl.when(t < own_count)
                def _():
                    dense_swap(t).start()

    cot_own.wait()
    cot_sent.wait_recv()
    for i in range(own_count):
        dense_swap(i).wait_recv()

        @pl.loop(i * rows // fine, (i + 1) * rows // fine)
        def _(k):
            here = rows_at(k, fine)
            at = pl.ds(pl.multiple_of(place.col * (length // 2) + k * fine, fine), fine)
            dense = total[at, :] + arrive_b[here, :] + down_bias
            normed, inverse = norm_parts(second[here, :] + dense_gate * hidden * dense)
            full = normed * second_gain + second_shift
            stage[0, here, :] = jnp.where(place.col == 0, full[:, :part], full[:, part:])
            stage[1, here, :] = jnp.where(place.col == 0, full[:, part:], full[:, :part])
            grad = cot[here, :].astype(wide)
            scaled = grad * second_gain
            one = jnp.mean(scaled, axis=1, keepdims=True)
            two = jnp.mean(scaled * normed, axis=1, keepdims=True)
            made = inverse * (scaled - one - normed * two)
            second[here, :] = made
            gated = (dense_gate * hidden * made).astype(low_type)
            low[at, :] = gated
            sums[0] += fold_rows(grad * normed)
            sums[1] += fold_rows(grad)
            sums[2] += fold_rows(gated.astype(wide))
            sums[3] += fold_rows(dense * made)

        grad_swap(i).start()
        dense_t[:, own_block(i)] = low[own_block(i), :].T
    for i in range(own_count):
        layer_swap(i).start()
        layer_put(i).start()
        grad_swap(i).wait_recv()
        dense_t[:, mate_block(i)] = low[mate_block(i), :].T

    def product(target, left, right, mask=None):
        @pl.loop(0, width // rows)
        def _(i):
            at = rows_at(i, rows)
            made = dot_nn(left[at, :], right[...])
            target[at, :] = (made if mask is None else made * mask).astype(low_type)

    for j in range(2):
        product(buffers[j], dense_t, gelu.at[j], masks[j])
        scatter.begin(j)
    for i in range(own_count):
        dense_swap(i).wait_send()
    for j in range(2):

        @pl.loop(0, blocks)
        def _(t, j=j):
            at = rows_at(mate_first(t), rows)
            inner = dot_nn(low[at, :], wm[2 * j + 1]).astype(low_type).astype(wide)
            unit_sums[2 + j] += fold_rows(gelu[j, at, :].astype(wide) * inner)
            pre = (masks[j] * inner * slope[j, at, :].astype(wide)).astype(low_type)
            slope[j, at, :] = pre
            unit_sums[j] += fold_rows(pre.astype(wide))
            made = dot_nt(pre, wm[2 * j])
            if j == 0:
                total[at, :] = made
            else:
                total[at, :] += made

                @pl.when(t < own_count)
                def _():
                    hidden_swap(t).start()

        scatter.advance(scatter_pace[0][j])
        product(buffers[2 + j], normed_t, slope.at[j])
        scatter.begin(2 + j)

    for i in range(own_count):
        grad_swap(i).wait_send()
    for i in range(own_count):
        hidden_swap(i).wait_recv()

        @pl.loop(i * rows // fine, (i + 1) * rows // fine)
        def _(k):
            here = rows_at(k, fine)
            at = pl.ds(pl.multiple_of(place.col * (length // 2) + k * fine, fine), fine)
            attn = attn_out[here, :]
            normed, inverse = norm_parts(token[at, :].astype(wide) + gate_cols * attn)
            grad = second[here, :] + (total[at, :] + arrive_a[here, :])
            scaled = grad * first_gain
            one = jnp.mean(scaled, axis=1, keepdims=True)
            two = jnp.mean(scaled * normed, axis=1, keepdims=True)
            made = inverse * (scaled - one - normed * two)
            second[here, :] = made
            gated = (gate_cols * made).astype(low_type)
            low[at, :] = gated
            sums[4] += fold_rows(grad * normed)
            sums[5] += fold_rows(grad)
            sums[6] += fold_rows(gated.astype(wide))
            sums[7] += fold_rows(attn * made)

        attn_grad_swap(i).start()
        dense_t[:, own_block(i)] = low[own_block(i), :].T
        scatter.advance(scatter_pace[1][i])
    for i in range(own_count):
        attn_grad_swap(i).wait_recv()
        dense_t[:, mate_block(i)] = low[mate_block(i), :].T

    @pl.loop(0, blocks)
    def _(b):
        at = rows_at(b, rows)
        gated = dot_nn(low[at, :], wa[pairs]).astype(low_type).astype(wide)
        seen = ctx[at, :].astype(wide)
        head_sums[...] += fold_rows(seen * gated)
        ctx_grad[at, :] = (gated * gate_columns).astype(low_type)
        ctx[at, :] = (seen * gate_columns).astype(low_type)

    product(buffers[4], dense_t, ctx)
    scatter.begin(4)
    scatter.advance(scatter_pace[2][0])
    for i in range(own_count):
        hidden_swap(i).wait_send()
        layer_put(i).wait()
        layer_swap(i).wait()
    query_t = pair_wide
    bias_sums = []
    for p in range(pairs):

        key_grad[...] = jnp.zeros_like(key_grad)
        value_grad[...] = jnp.zeros_like(value_grad)
        pace = scatter_pace[3 + min(p, len(scatter_pace) - 4)]

        @pl.loop(0, 2)
        def _(h, p=p, pace=pace):
            own = jnp.where(lane_head == h, size ** (-0.5), 0.0).astype(low_type)
            one_head = jnp.where(lane_head == h, 1.0, 0.0).astype(low_type)
            head_rows = rows_at(h, size)
            for b in range(blocks):
                query = qkv[p, b * rows : (b + 1) * rows, :pair] * own
                context = ctx_grad[b * rows : (b + 1) * rows, p * pair : (p + 1) * pair] * one_head
                logs = lse[2 * p + h, :, b * rows : (b + 1) * rows]
                inner = jnp.zeros_like(logs)
                kept, masked = [], key_tiles(b, rows, cut.prefix_most)
                for tile, needs in masked:
                    score = dot_nt(qkv[p, tile * rows : (tile + 1) * rows, pair : 2 * pair], query)
                    score = masked_tile(score, b * rows, tile * rows, prefix) if needs else score
                    prob = jnp.exp(score - logs)
                    grad_prob = dot_nt(qkv[p, tile * rows : (tile + 1) * rows, 2 * pair :], context)
                    inner = inner + (prob * grad_prob).sum(axis=0, keepdims=True)
                    kept.append((prob, grad_prob))
                found = jnp.zeros((size, rows), wide)
                for (tile, _), (prob, grad_prob) in zip(masked, kept):
                    at = slice(tile * rows, (tile + 1) * rows)
                    grad_score = (prob * (grad_prob - inner)).astype(low_type)
                    value_grad[at, :] += dot_nn(prob.astype(low_type), context)
                    key_grad[at, :] += dot_nn(grad_score, query)
                    found = found + dot_nn(key_t[p, head_rows, at], grad_score)
                query_t[head_rows, b * rows : (b + 1) * rows] = found * size ** (-0.5)
                for now in range(2):
                    if b % 2 and pace[2 * now + b // 2]:

                        @pl.when(h == now)
                        def _():
                            scatter.advance(pace[2 * now + b // 2])

        query_sum = jnp.zeros((8, pair), wide)
        value_sum = jnp.zeros((8, pair), wide)
        for b in range(blocks):
            at = pl.ds(b * rows, rows)
            query_low = query_t[:, at].T.astype(low_type)
            value_low = value_grad[at, :].astype(low_type)
            qkv[p, at, :pair] = query_low
            qkv[p, at, pair : 2 * pair] = key_grad[at, :].astype(low_type)
            qkv[p, at, 2 * pair :] = value_low
            query_sum += fold_rows(query_low.astype(wide))
            value_sum += fold_rows(value_low.astype(wide))
        bias_sums.append((query_sum, value_sum))
        product(buffers[5 + p], token_t, qkv.at[p])
        scatter.begin(5 + p)
        scatter.advance(pace[4])

    @pl.loop(0, blocks)
    def _(t):
        b = mate_first(t)
        at = rows_at(b, rows)
        made = dot_nt(qkv[0, at, :], wa[0])
        for p in range(1, pairs):
            made = made + dot_nt(qkv[p, at, :], wa[p])
        kept = second[rows_at(lax.rem(t, own_count), rows), :]
        made = made + jnp.where(t >= own_count, kept, 0.0)
        total[at, :part] = jnp.where(place.col == 0, made[:, part:], made[:, :part])
        total[at, part:] = jnp.where(place.col == 0, made[:, :part], made[:, part:])
        token_swap(b).start()

    def whole(values):
        return jnp.sum(values, axis=0, keepdims=True)

    dense_col, attn_col = whole(sums[3]), whole(sums[7])
    seq_lane = lax.broadcasted_iota(jnp.int32, (1, width), 1)
    here = place.dp * place.row_size + place.row
    dense_all = jnp.sum(dense_col * hidden, axis=1, keepdims=True)
    attn_all = jnp.sum(attn_col * hidden, axis=1, keepdims=True)
    seq_row = jnp.where(seq_lane == here, attn_all, 0.0) + jnp.where(seq_lane == here + width // 2, dense_all, 0.0)
    small[0:1, :] = whole(sums[6])
    small[1:2, :] = whole(sums[2])
    small[2:3, :] = whole(sums[4])
    small[3:4, :] = whole(sums[5])
    small[4:5, :] = whole(sums[0])
    small[5:6, :] = whole(sums[1])
    small[6:7, :] = dense_gate * dense_col + attn_gate * attn_col
    small[7:8, :] = seq_row
    for j in range(4):
        small[8 + j : 9 + j, :] = whole(unit_sums[j])
    for p in range(pairs):
        small[12:13, p * pair : (p + 1) * pair] = whole(bias_sums[p][0])
        small[12:13, part + p * pair : part + (p + 1) * pair] = whole(bias_sums[p][1])
    small[13:14, :part] = whole(head_sums[...])
    small[13:14, part:] = jnp.zeros((1, part), wide)
    small[14:16, :] = jnp.zeros((2, width), wide)
    copy_c = to_mate(small.at[pl.ds(0, 8)], small_c.at[0, pl.ds(0, 8)], small_swap)
    copy_c.start()
    copy_c.wait_recv()
    small_c[1, 0:8, :] = small[0:8, :] + small_c[0, 0:8, :]
    small_c[1, 8:16, :] = small[8:16, :]
    copy_x = send(small_c.at[1], small_x.at[0], (small_s, small_r), 0, place.x_mate())
    copy_x.start()
    scatter.advance(1)
    copy_x.wait_recv()
    small_x[1] = small_c[1] + small_x[0]
    copy_y = send(small_x.at[1], small_y.at[0], (small_s, small_r), 1, place.y_mate())
    copy_y.start()
    scatter.advance(1)
    copy_y.wait_recv()
    mine = small_x[1] + small_y[0]
    small_y[1] = mine
    small_z[place.row] = mine
    copies = [
        send(small_y.at[1], small_z.at[place.row], (small_s, small_r), 1 + step, place.row_mate(step))
        for step in range(1, cut.row_size)
    ]
    for copy in copies:
        copy.start()
    for b in range(blocks):
        token_swap(b).wait_recv()
        found = total[near(b), part:] + token_recv[near(b), :]
        stage[b // own_count, near(b % own_count), :] = found
        pltpu.make_async_copy(
            stage.at[b // own_count, near(b % own_count)], token_out.at[near(b)], out_sem.at[own_count + b]
        ).start()
    scatter.finish()
    for copy in copies:
        copy.wait_recv()
    result = small_z[0]
    for z in range(1, cut.row_size):
        result = result + small_z[z]
    small_out[...] = result
    gather.finish()
    for copy in [token_sent, cot_sent, copy_c, copy_x, copy_y] + copies:
        copy.wait_send()
    for i in range(own_count):
        attn_grad_swap(i).wait_send()
    for b in range(blocks):
        token_swap(b).wait_send()
        pltpu.make_async_copy(
            stage.at[b // own_count, near(b % own_count)], token_out.at[near(b)], out_sem.at[own_count + b]
        ).wait()


def place_kernel(cut, count, layer_in, token_in, *rest):
    pairs, pair, part, width = cut.heads // 2, 2 * cut.size, cut.part_width, cut.width
    sources, rest = rest[:count], rest[count:]
    (
        layer_out, token_out, grad_qkv, grad_out, grad_up, grad_down, query_bias, value_bias, out_bias, up_bias,
        down_bias, first_gain, first_shift, second_gain, second_shift, head, hidden, unit, attention, feedforward,
    ) = rest[:20]
    held, targets, (in_sem, out_sem, source_sem) = rest[20], rest[21 : 21 + count], rest[21 + count :]
    parts = held.shape[1]
    step = layer_in.shape[0] // parts
    moves = []
    for a, (source, target) in enumerate(((layer_in, layer_out), (token_in, token_out))):
        for i in range(parts):
            at = pl.ds(i * step, step)
            into = pltpu.make_async_copy(source.at[at], held.at[a, i], in_sem.at[a, i])
            into.start()
            moves.append((into, pltpu.make_async_copy(held.at[a, i], target.at[at], out_sem.at[a, i])))
    loads = [pltpu.make_async_copy(a, b, source_sem.at[i]) for i, (a, b) in enumerate(zip(sources, targets))]
    for copy in loads:
        copy.start()
    for into, out in moves:
        into.wait()
        out.start()
    for copy in loads:
        copy.wait()
    small, down_0, down_1, up_0, up_1, grad_out_t, *pieces = targets
    group = cut.units // 2
    for p in range(pairs):
        for k in range(3):
            grad_qkv[k, :, p * pair : (p + 1) * pair] = pieces[p][:, k * pair : (k + 1) * pair]
    grad_out[...] = grad_out_t[...]
    for j, (up, down) in enumerate(((up_0, down_0), (up_1, down_1))):
        grad_up[:, j * group : (j + 1) * group] = up[...]
        grad_down[:, j * group : (j + 1) * group] = down[...]

    def flat(target, values):
        target[...] = values.reshape(target.shape)

    flat(up_bias, jnp.concatenate([small[8:9, :], small[9:10, :]], axis=1))
    flat(unit, jnp.concatenate([small[10:11, :], small[11:12, :]], axis=1))
    flat(query_bias, small[12:13, :part])
    flat(value_bias, small[12:13, part:])
    for row, target in enumerate((out_bias, down_bias, first_gain, first_shift, second_gain, second_shift, hidden)):
        flat(target, small[row : row + 1, :])
    lane = lax.broadcasted_iota(jnp.int32, (1, part), 1) // cut.size
    slot = lax.broadcasted_iota(jnp.int32, (1, cut.heads), 1)
    found = jnp.zeros((1, cut.heads), wide)
    for h in range(cut.heads):
        one = jnp.sum(jnp.where(lane == h, small[13:14, :part], 0.0), axis=1, keepdims=True)
        found = jnp.where(slot == h, one, found)
    flat(head, found)
    seq_total = attention.shape[0]
    flat(attention, small[7:8, :seq_total])
    flat(feedforward, small[7:8, width // 2 : width // 2 + seq_total])
    for _, out in moves:
        out.wait()


gather_turned = (5, 7)
scatter_turned = (0,)
gather_order = ((-1, 0), (-1, 1), (0, 0), (-1, 2), (0, 1), (-1, 3), (1, 0), (0, 2), (-1, 4), (1, 1), (2, 0), (0, 3), (-1, 5), (1, 2), (2, 1), (0, 4), (-1, 6), (1, 3), (2, 2), (0, 5), (-1, 7), (1, 4), (2, 3), (0, 6), (1, 5), (2, 4), (0, 7), (1, 6), (2, 5), (1, 7), (2, 6), (2, 7))
scatter_order = ((0, 0), (0, 1), (0, 2), (1, 0), (1, 1), (0, 3), (0, 4), (1, 2), (0, 5), (2, 0), (1, 3), (1, 4), (0, 6), (1, 5), (0, 7), (1, 6), (2, 1), (1, 7), (2, 3), (2, 4), (2, 6), (2, 5), (2, 2), (2, 7))
gather_pace = ((3, 0, 0, 0, 3), (1, 3, 0, 0, 1), (0, 0, 1, 3, 2), (0, 2))
scatter_pace = ((0, 1), (0, 1), (0,), (1, 0, 0, 1, 1), (1, 1, 1, 1, 0), (1, 1, 1, 2, 0))


class Cut(NamedTuple):
    length: int
    width: int
    part_width: int
    heads: int
    size: int
    units: int
    part: int
    row_size: int
    rows: int
    fine: int
    prefix_most: int


def any_spec():
    return pl.BlockSpec(memory_space=pl.ANY)


def vmem_spec():
    return pl.BlockSpec(memory_space=pltpu.VMEM)


def smem_spec():
    return pl.BlockSpec(memory_space=pltpu.SMEM)


def like(items):
    return [jax.ShapeDtypeStruct(shape, kind) for shape, kind in items]


def scratch(items):
    return [pltpu.VMEM(shape, kind) for shape, kind in items]


def dma(*shape):
    return pltpu.SemaphoreType.DMA(shape)


vmem_most = 67043328


def run_layer(cut, *args):
    length, width, half = cut.length, cut.width, cut.part_width
    group = cut.units // 2
    pairs = cut.heads // 2
    blocks = length // cut.rows
    columns = [group] * 4 + [half] * (pairs + 1)
    count = len(columns)
    outs = [((length, half), wide), ((length, half), wide), ((16, width), wide)]
    outs += [((cut.part, n), wide) for n in columns]
    own = [
        ((pairs + 1, width, half), low_type),
        ((4, width, group), low_type),
        ((length, width), low_type),
        ((width, length), low_type),
        ((pairs, length, half), low_type),
        ((cut.heads, 1, length), wide),
        ((length, half), low_type),
        ((length // 2, width), wide),
        ((width, length), low_type),
        ((2, length, group), low_type),
        ((2, length, group), low_type),
        ((length // 2, width), wide),
        ((length, width), low_type),
        ((width, length), low_type),
        ((8, 8, width), wide),
        ((length // 2, width), low_type),
        ((length, width), wide),
        ((length // 2, width), wide),
        ((length // 2, width), wide),
        ((2, length // 2, half), wide),
        ((length, half), wide),
        ((length, half), low_type),
        ((length, 2 * cut.size), wide),
        ((length, 2 * cut.size), wide),
        ((2 * cut.size, length), wide),
        ((2 * cut.size, length), low_type),
        ((pairs, 2 * cut.size, length), low_type),
        ((pairs + 1, cut.part, half), low_type),
        ((4, cut.part, group), low_type),
        ((16, width), wide),
        ((2, 16, width), wide),
        ((2, 16, width), wide),
        ((2, 16, width), wide),
        ((cut.row_size, 16, width), wide),
        ((4, 8, width), wide),
        ((8, half), wide),
    ]
    quarter = cut.part * cut.row_size // 2
    own += [((width, n), low_type) for n in columns]
    z = cut.row_size - 1
    turned = [c in scatter_turned for c in range(count)]
    both = list(zip(columns, turned))
    own += [((2, 2, 2 * quarter, n // 2) if turn else (2, 2, quarter, n), low_type) for n, turn in both]
    own += [((4, 2 * quarter, n // 2) if turn else (2, quarter, n), low_type) for n, turn in both]
    own += [((z, 4, cut.part, n // 2) if turn else (2, quarter, n), low_type) for n, turn in both]
    own += [((2, cut.part, n // 2) if turn else (2 * quarter, n), low_type) for n, turn in both]
    own += [((2, cut.part, n // 2) if turn else (z, cut.part, n), low_type) for n, turn in both]
    semaphores = [dma(count), dma(count, z), dma(count, z), dma(count, 2), dma(count, 2), dma(count, 4), dma(count, 4)]
    semaphores += [dma(count, 2 * z), dma(count, 2 * z), dma(2), dma(blocks // 2 + blocks)]
    semaphores += [dma(count, 4), dma(count, 4), dma(count, 2), dma(count, 2), dma(count, z), dma(count, z)]
    pair_swaps = 3 + 7 * (blocks // 2) + blocks
    semaphores += [dma(pair_swaps), dma(pair_swaps), dma(2 + z), dma(2 + z)]
    return pl.pallas_call(
        partial(layer_kernel, cut),
        out_shape=like(outs),
        in_specs=[any_spec()] * 2 + [vmem_spec()] * (len(args) - 6) + [smem_spec()] * 4,
        out_specs=[any_spec()] * 2 + [vmem_spec()] * (len(outs) - 2),
        scratch_shapes=scratch(own) + semaphores,
        compiler_params=pltpu.CompilerParams(collective_id=0, has_side_effects=True, vmem_limit_bytes=vmem_most),
        name="whole_layer",
    )(*args)


def fused_device(
    cut,
    tokens, cotangent, qkv_weight, out_weight, up_weight, down_weight, query_bias, value_bias, out_bias, up_bias,
    down_bias, first_gain, first_shift, second_gain, second_shift, head_gate, hidden_gate, intermediate_gate,
    attention_gate, feedforward_gate, prefix_length,
):
    half, width, units, part = cut.part_width, cut.width, cut.units, cut.part
    rows = [
        query_bias, value_bias, out_bias, up_bias, down_bias, first_gain, first_shift, second_gain, second_shift,
        hidden_gate, intermediate_gate,
    ]
    scalars = [head_gate, attention_gate, feedforward_gate, prefix_length]
    weights = [qkv_weight, out_weight.T, up_weight, down_weight.T]
    made = run_layer(cut, tokens, cotangent, *weights, *rows, *scalars)
    seq_total = lax.axis_size(("dp", "row"))
    lanes = [half, half, width, units, width, width, width, width, width, cut.heads, width, units, seq_total, seq_total]
    shapes = [(3, part, half), (part, half), (part, units), (part, units)] + [(n,) for n in lanes]
    whole = (cut.length, half)
    held = [((2, 4, cut.length // 4, half), wide)] + [(piece.shape, piece.dtype) for piece in made[2:]]
    count = len(made) - 2
    layer_out, grad_tokens, *outs = pl.pallas_call(
        partial(place_kernel, cut, count),
        out_shape=like([(shape, wide) for shape in [whole, whole] + shapes]),
        in_specs=[any_spec()] * len(made),
        out_specs=[any_spec()] * 2 + [vmem_spec()] * len(shapes),
        scratch_shapes=scratch(held) + [dma(2, 4), dma(2, 4), dma(count)],
        name="place_results",
    )(*made)
    return (layer_out, grad_tokens, outs[0], outs[1].T, outs[2], outs[3].T, *outs[4:])


def cut_of(args):
    tokens, qkv_weight, up_weight, head_gate, prefix_length = args[0], args[2], args[4], args[15], args[20]
    length, part_width = tokens.shape
    part, width = qkv_weight.shape[1], args[11].shape[0]
    heads = head_gate.shape[0]
    row_size, dp_size = lax.axis_size("row"), lax.axis_size("dp")
    fits = (
        prefix_length.shape[0] == 1
        and lax.axis_size("col") == 2
        and dp_size == 4
        and row_size % 2 == 0
        and part % 16 == 0
        and heads % 2 == 0
        and part_width == qkv_weight.shape[2]
        and part_width == 3 * (2 * part_width // heads)
        and (2 * part_width // heads) % 128 == 0
        and width % 256 == 0
        and length % 512 == 0
        and up_weight.shape[1] == 2 * width
    )
    if not fits:
        return None
    return Cut(
        length, width, part_width, heads, part_width // heads, up_weight.shape[1], part, row_size, 256, 128, length // 2
    )


def any_device(*args):
    cut = cut_of(args)
    return per_device(*args) if cut is None else fused_device(cut, *args)


def solution(mesh):
    placed = (
        P(("dp", "row"), "col"),
        P(("dp", "row"), "col"),
        P(None, ("dp", "row"), "col"),
        P("col", ("dp", "row")),
        P(("dp", "row"), "col"),
        P("col", ("dp", "row")),
        P("col"),
        P("col"),
        P(),
        P("col"),
        P(),
        P(),
        P(),
        P(),
        P(),
        P("col"),
        P(),
        P("col"),
        P(("dp", "row")),
        P(("dp", "row")),
        P(("dp", "row")),
    )
    return jax.shard_map(
        any_device,
        mesh=mesh,
        in_specs=placed,
        out_specs=(
            P(("dp", "row"), "col"),
            P(("dp", "row"), "col"),
            P(None, ("dp", "row"), "col"),
            P("col", ("dp", "row")),
            P(("dp", "row"), "col"),
            P("col", ("dp", "row")),
            P("col"),
            P("col"),
            P(),
            P("col"),
            P(),
            P(),
            P(),
            P(),
            P(),
            P("col"),
            P(),
            P("col"),
            P(),
            P(),
        ),
        check_vma=False,
    )
```

```python
from functools import partial
import math
from typing import NamedTuple

import jax
import jax.numpy as jnp
from jax import lax
from jax.experimental import pallas as pl
from jax.experimental.pallas import tpu as pltpu
from jax.sharding import PartitionSpec as P

masked_value = -1e30
norm_eps = 1e-05


def norm_forward(values, scale_gain, shift_term):
    centre = jnp.mean(values, axis=1, keepdims=True)
    centred = values - centre
    spread = jnp.mean(centred * centred, axis=1, keepdims=True)
    inverse = lax.rsqrt(spread + norm_eps)
    normed = centred * inverse
    return (normed * scale_gain + shift_term, normed, inverse)


def norm_backward(gradient, normed, inverse, scale_gain):
    scaled = gradient * scale_gain
    first_mean = jnp.mean(scaled, axis=1, keepdims=True)
    second_mean = jnp.mean(scaled * normed, axis=1, keepdims=True)
    return inverse * (scaled - first_mean - normed * second_mean)


def block_mask(start_row, block_rows, length, prefix_value):
    key_index = jnp.arange(length, dtype=jnp.int32)
    query_index = start_row + jnp.arange(block_rows, dtype=jnp.int32)
    return (key_index[None, :] < prefix_value) | (key_index[None, :] <= query_index[:, None])


def block_scores(query_block, key_seq, start_row, prefix_value, scale_factor):
    block_rows = query_block.shape[0]
    length = key_seq.shape[0]
    allowed = block_mask(start_row, block_rows, length, prefix_value)
    scores = (
        jnp.einsum("qhd,khd->hqk", query_block, key_seq, preferred_element_type=jnp.float32)
        * scale_factor
    )
    return jnp.where(allowed[None], scores, masked_value)


def attend_sequence(query_seq, key_seq, value_seq, prefix_value, block_rows, scale_factor):
    length = key_seq.shape[0]
    block_count = length // block_rows
    query_blocks = query_seq.reshape(
        block_count, block_rows, query_seq.shape[1], query_seq.shape[2]
    )
    starts = jnp.arange(block_count, dtype=jnp.int32) * block_rows

    def one_block(element):
        query_block, start_row = element
        scores = block_scores(query_block, key_seq, start_row, prefix_value, scale_factor)
        row_peak = jnp.max(scores, axis=2, keepdims=True)
        exponent = jnp.exp(scores - row_peak)
        row_total = jnp.sum(exponent, axis=2, keepdims=True)
        weights_low = (exponent / row_total).astype(jnp.bfloat16)
        context = jnp.einsum(
            "hqk,khd->qhd", weights_low, value_seq, preferred_element_type=jnp.float32
        )
        return (context, row_peak[..., 0] + jnp.log(row_total[..., 0]))

    contexts, log_totals = lax.map(one_block, (query_blocks, starts))
    return (contexts.reshape(length, query_seq.shape[1], query_seq.shape[2]), log_totals)


def attend_back(
    query_seq, key_seq, value_seq, grad_seq, log_seq, prefix_value, block_rows, scale_factor
):
    length = key_seq.shape[0]
    block_count = length // block_rows
    head_count = query_seq.shape[1]
    head_size = query_seq.shape[2]
    query_blocks = query_seq.reshape(block_count, block_rows, head_count, head_size)
    grad_blocks = grad_seq.reshape(block_count, block_rows, head_count, head_size)
    starts = jnp.arange(block_count, dtype=jnp.int32) * block_rows

    def one_block(running, element):
        grad_keys, grad_values = running
        query_block, grad_block, log_block, start_row = element
        scores = block_scores(query_block, key_seq, start_row, prefix_value, scale_factor)
        probs = jnp.exp(scores - log_block[..., None])
        grad_probs = jnp.einsum(
            "qhd,khd->hqk", grad_block, value_seq, preferred_element_type=jnp.float32
        )
        row_inner = jnp.sum(probs * grad_probs, axis=2, keepdims=True)
        grad_scores = (probs * (grad_probs - row_inner)).astype(jnp.bfloat16)
        grad_query = (
            jnp.einsum("hqk,khd->qhd", grad_scores, key_seq, preferred_element_type=jnp.float32)
            * scale_factor
        )
        grad_keys = (
            grad_keys
            + jnp.einsum(
                "hqk,qhd->khd", grad_scores, query_block, preferred_element_type=jnp.float32
            )
            * scale_factor
        )
        grad_values = grad_values + jnp.einsum(
            "hqk,qhd->khd",
            probs.astype(jnp.bfloat16),
            grad_block,
            preferred_element_type=jnp.float32,
        )
        return ((grad_keys, grad_values), grad_query)

    zeros_kv = jnp.zeros((length, head_count, head_size), jnp.float32)
    (grad_keys, grad_values), grad_query = lax.scan(
        one_block, (zeros_kv, zeros_kv), (query_blocks, grad_blocks, log_seq, starts)
    )
    return (grad_query.reshape(length, head_count, head_size), grad_keys, grad_values)


def per_device(
    tokens,
    cotangent,
    qkv_weight,
    out_weight,
    up_weight,
    down_weight,
    query_bias,
    value_bias,
    out_bias,
    up_bias,
    down_bias,
    first_gain,
    first_shift,
    second_gain,
    second_shift,
    head_gate,
    hidden_gate,
    intermediate_gate,
    attention_gate,
    feedforward_gate,
    prefix_length,
):
    row_count = tokens.shape[0]
    seq_count = prefix_length.shape[0]
    length = row_count // seq_count
    local_heads = head_gate.shape[0]
    head_width = qkv_weight.shape[2]
    head_size = head_width // local_heads
    model_width = first_gain.shape[0]
    part_width = model_width // lax.axis_size("col")
    block_rows = min(512, length)
    scale_factor = head_size ** (-0.5)
    col_index = lax.axis_index("col")
    qkv_low, out_low = (
        lax.all_gather(qkv_weight.astype(jnp.bfloat16), ("dp", "row"), axis=1, tiled=True),
        lax.all_gather(out_weight.astype(jnp.bfloat16), ("dp", "row"), axis=1, tiled=True),
    )
    up_low, down_low = (
        lax.all_gather(up_weight.astype(jnp.bfloat16), ("dp", "row"), axis=0, tiled=True),
        lax.all_gather(down_weight.astype(jnp.bfloat16), ("dp", "row"), axis=1, tiled=True),
    )
    token_full = lax.all_gather(tokens, "col", axis=1, tiled=True)
    projected = jnp.einsum("td,kdf->ktf", token_full, qkv_low, preferred_element_type=jnp.float32)
    query_low = (projected[0] + query_bias).astype(jnp.bfloat16)
    key_low = projected[1].astype(jnp.bfloat16)
    value_low = (projected[2] + value_bias).astype(jnp.bfloat16)

    def split_heads(array):
        return array.reshape(seq_count, length, local_heads, head_size)

    def forward_seq(element):
        query_seq, key_seq, value_seq, prefix_value = element
        return attend_sequence(
            query_seq, key_seq, value_seq, prefix_value, block_rows, scale_factor
        )

    contexts, log_totals = lax.map(
        forward_seq,
        (split_heads(query_low), split_heads(key_low), split_heads(value_low), prefix_length),
    )
    context = contexts.reshape(row_count, head_width)
    gate_columns = jnp.repeat(head_gate.astype(jnp.float32), head_size)
    gated_low = (context * gate_columns).astype(jnp.bfloat16)
    attn_terms = jnp.dot(gated_low, out_low, preferred_element_type=jnp.float32)
    attn_out = lax.psum(attn_terms, "col") + out_bias
    hidden_mask = hidden_gate.astype(jnp.float32)
    attn_rows = jnp.repeat(attention_gate.astype(jnp.float32), length)[:, None]
    dense_rows = jnp.repeat(feedforward_gate.astype(jnp.float32), length)[:, None]
    first_sum = token_full.astype(jnp.float32) + attn_rows * hidden_mask * attn_out
    normed_one, first_normed, first_inverse = norm_forward(first_sum, first_gain, first_shift)
    normed_low = normed_one.astype(jnp.bfloat16)
    pre_act = jnp.dot(normed_low, up_low, preferred_element_type=jnp.float32) + up_bias
    activated, gelu_pull = jax.vjp(partial(jax.nn.gelu, approximate=False), pre_act)
    unit_mask = intermediate_gate.astype(jnp.float32)
    inner_low = (activated * unit_mask).astype(jnp.bfloat16)
    dense_terms = jnp.dot(inner_low, down_low, preferred_element_type=jnp.float32)
    dense_out = lax.psum(dense_terms, "col") + down_bias
    second_sum = normed_one + dense_rows * hidden_mask * dense_out
    layer_full, second_normed, second_inverse = norm_forward(second_sum, second_gain, second_shift)
    layer_out = lax.dynamic_slice_in_dim(layer_full, col_index * part_width, part_width, 1)
    grad_full = lax.all_gather(cotangent, "col", axis=1, tiled=True).astype(jnp.float32)
    grad_gain_two = jnp.sum(grad_full * second_normed, axis=0)
    grad_shift_two = jnp.sum(grad_full, axis=0)
    grad_second = norm_backward(grad_full, second_normed, second_inverse, second_gain)
    grad_dense_low = (dense_rows * hidden_mask * grad_second).astype(jnp.bfloat16)
    dense_product = dense_out * grad_second
    grad_dense_gate = jnp.sum(
        dense_product.reshape(seq_count, length, model_width) * hidden_mask, axis=(1, 2)
    )
    hidden_from_dense = jnp.sum(dense_rows * dense_product, axis=0)
    grad_down_bias = jnp.sum(grad_dense_low.astype(jnp.float32), axis=0)
    up_low, down_low = (
        lax.all_gather(up_weight.astype(jnp.bfloat16), ("dp", "row"), axis=0, tiled=True),
        lax.all_gather(down_weight.astype(jnp.bfloat16), ("dp", "row"), axis=1, tiled=True),
    )
    grad_down = jnp.einsum(
        "tf,td->fd", inner_low, grad_dense_low, preferred_element_type=jnp.float32
    )
    grad_inner_low = jnp.einsum(
        "td,fd->tf", grad_dense_low, down_low, preferred_element_type=jnp.float32
    ).astype(jnp.bfloat16)
    grad_inner = grad_inner_low.astype(jnp.float32)
    grad_unit_gate = jnp.sum(activated * grad_inner, axis=0)
    (grad_pre,) = gelu_pull(unit_mask * grad_inner)
    grad_pre_low = grad_pre.astype(jnp.bfloat16)
    grad_up_bias = jnp.sum(grad_pre_low.astype(jnp.float32), axis=0)
    grad_up = jnp.einsum("td,tf->df", normed_low, grad_pre_low, preferred_element_type=jnp.float32)
    dense_parts = (
        lax.psum_scatter(grad_up, ("dp", "row"), scatter_dimension=0, tiled=True),
        lax.psum_scatter(grad_down, ("dp", "row"), scatter_dimension=1, tiled=True),
    )
    hidden_terms = jnp.einsum("tf,df->td", grad_pre_low, up_low, preferred_element_type=jnp.float32)
    grad_normed = grad_second + lax.psum(hidden_terms, "col")
    grad_gain_one = jnp.sum(grad_normed * first_normed, axis=0)
    grad_shift_one = jnp.sum(grad_normed, axis=0)
    grad_first = norm_backward(grad_normed, first_normed, first_inverse, first_gain)
    grad_attn_low = (attn_rows * hidden_mask * grad_first).astype(jnp.bfloat16)
    attn_product = attn_out * grad_first
    grad_attn_gate = jnp.sum(
        attn_product.reshape(seq_count, length, model_width) * hidden_mask, axis=(1, 2)
    )
    grad_hidden = hidden_from_dense + jnp.sum(attn_rows * attn_product, axis=0)
    grad_out_bias = jnp.sum(grad_attn_low.astype(jnp.float32), axis=0)
    qkv_low, out_low = (
        lax.all_gather(qkv_weight.astype(jnp.bfloat16), ("dp", "row"), axis=1, tiled=True),
        lax.all_gather(out_weight.astype(jnp.bfloat16), ("dp", "row"), axis=1, tiled=True),
    )
    grad_out = jnp.einsum("tc,td->cd", gated_low, grad_attn_low, preferred_element_type=jnp.float32)
    grad_gated_low = jnp.einsum(
        "td,cd->tc", grad_attn_low, out_low, preferred_element_type=jnp.float32
    ).astype(jnp.bfloat16)
    grad_head_cols = jnp.sum(context * grad_gated_low.astype(jnp.float32), axis=0)
    grad_head = jnp.sum(grad_head_cols.reshape(local_heads, head_size), axis=1)
    grad_context = grad_gated_low * gate_columns.astype(jnp.bfloat16)

    def backward_seq(element):
        query_seq, key_seq, value_seq, grad_seq, log_seq, prefix_value = element
        return attend_back(
            query_seq, key_seq, value_seq, grad_seq, log_seq, prefix_value, block_rows, scale_factor
        )

    grad_query, grad_keys, grad_values = lax.map(
        backward_seq,
        (
            split_heads(query_low),
            split_heads(key_low),
            split_heads(value_low),
            split_heads(grad_context),
            log_totals,
            prefix_length,
        ),
    )
    grad_qkv_low = jnp.stack([grad_query, grad_keys, grad_values]).reshape(3, row_count, head_width)
    grad_qkv_low = grad_qkv_low.astype(jnp.bfloat16)
    grad_query_bias = jnp.sum(grad_qkv_low[0].astype(jnp.float32), axis=0)
    grad_value_bias = jnp.sum(grad_qkv_low[2].astype(jnp.float32), axis=0)
    grad_qkv = jnp.einsum(
        "td,ktf->kdf", token_full, grad_qkv_low, preferred_element_type=jnp.float32
    )
    input_terms = jnp.einsum(
        "ktf,kdf->td", grad_qkv_low, qkv_low, preferred_element_type=jnp.float32
    )
    grad_tokens = lax.psum_scatter(
        input_terms.astype(jnp.bfloat16), "col", scatter_dimension=1, tiled=True
    ).astype(jnp.float32)
    grad_tokens = grad_tokens + lax.dynamic_slice_in_dim(
        grad_first, col_index * part_width, part_width, 1
    )
    grad_up_part, grad_down_part = dense_parts
    grad_qkv_part, grad_out_part = (
        lax.psum_scatter(grad_qkv, ("dp", "row"), scatter_dimension=1, tiled=True),
        lax.psum_scatter(grad_out, ("dp", "row"), scatter_dimension=1, tiled=True),
    )
    seq_total = seq_count * lax.axis_size(("dp", "row"))
    seq_start = lax.axis_index(("dp", "row")) * seq_count
    seq_stack = lax.dynamic_update_slice_in_dim(
        jnp.zeros((2, seq_total), jnp.float32),
        jnp.stack([grad_attn_gate, grad_dense_gate]),
        seq_start,
        1,
    )
    full_stack = jnp.stack(
        [
            grad_out_bias,
            grad_down_bias,
            grad_gain_one,
            grad_shift_one,
            grad_gain_two,
            grad_shift_two,
            grad_hidden,
        ]
    )
    half_stack = jnp.stack([grad_query_bias, grad_value_bias])
    unit_stack = jnp.stack([grad_up_bias, grad_unit_gate])
    full_sum, half_sum, unit_sum, head_sum, seq_sum = lax.psum(
        (full_stack, half_stack, unit_stack, grad_head, seq_stack), ("dp", "row")
    )
    return (
        layer_out,
        grad_tokens,
        grad_qkv_part,
        grad_out_part,
        grad_up_part,
        grad_down_part,
        half_sum[0],
        half_sum[1],
        full_sum[0],
        unit_sum[0],
        full_sum[1],
        full_sum[2],
        full_sum[3],
        full_sum[4],
        full_sum[5],
        head_sum,
        full_sum[6],
        unit_sum[1],
        seq_sum[0],
        seq_sum[1],
    )


low_type = jnp.bfloat16
wide = jnp.float32
mesh_ids = pl.DeviceIdType.MESH


def dot_nn(left, right):
    return jnp.dot(left, right, preferred_element_type=wide)


def dot_nt(left, right):
    return lax.dot_general(left, right, (((1,), (1,)), ((), ())), preferred_element_type=wide)


def rows_at(index, count):
    return pl.ds(pl.multiple_of(index * count, count), count)


def fold_rows(values):
    return jnp.sum(values.reshape(values.shape[0] // 8, 8, values.shape[1]), axis=0)


def norm_parts(values):
    centre = jnp.mean(values, axis=1, keepdims=True)
    centred = values - centre
    spread = jnp.mean(centred * centred, axis=1, keepdims=True)
    inverse = lax.rsqrt(spread + norm_eps)
    return centred * inverse, inverse


class Place:
    def __init__(self, row_size):
        self.dp, self.row, self.col = (lax.axis_index(name) for name in ("dp", "row", "col"))
        self.row_size = row_size
        self.x, self.y = lax.rem(self.dp, 2), self.dp // 2
        self.x_dp = self.y * 2 + (1 - self.x)
        self.y_dp = (1 - self.y) * 2 + self.x

    def x_mate(self):
        return {"dp": self.x_dp}

    def y_mate(self):
        return {"dp": self.y_dp}

    def row_mate(self, step):
        return {"row": lax.rem(self.row + step, self.row_size)}

    def col_mate(self):
        return {"col": 1 - self.col}

    def barrier(self):
        semaphore = pltpu.get_barrier_semaphore()
        mates = [self.x_mate(), self.y_mate(), self.col_mate()]
        mates += [self.row_mate(step) for step in range(1, self.row_size)]
        for mate in mates:
            pl.semaphore_signal(semaphore, inc=1, device_id=mate, device_id_type=mesh_ids)
        pl.semaphore_wait(semaphore, len(mates))


def send(source, target, semaphores, index, mate):
    sent, received = semaphores
    return pltpu.make_async_remote_copy(
        src_ref=source,
        dst_ref=target,
        send_sem=sent.at[index],
        recv_sem=received.at[index],
        device_id=mate,
        device_id_type=mesh_ids,
    )


class Gather:
    def __init__(self, place, shards, chunks, turned, order, own_sem, z_sems, two_sems, three_sems, turned_sems):
        self.place, self.shards, self.chunks, self.turned = place, shards, chunks, turned
        self.own_sem, self.z_sems, self.two_sems, self.three_sems = own_sem, z_sems, two_sems, three_sems
        self.turned_sems = turned_sems
        self.part = shards[0].shape[0]
        self.block = self.part * place.row_size
        self.half = self.block // 2
        self.steps, self.done = order, 0

    def block_rows(self, dp):
        return pl.ds(pl.multiple_of(dp * self.block, 16), self.block)

    def half_rows(self, dp, half):
        return pl.ds(pl.multiple_of(dp * self.block + half * self.half, 16), self.half)

    def part_rows(self, dp):
        return pl.ds(pl.multiple_of(dp * self.block + self.place.row * self.part, 16), self.part)

    def half_cols(self, c, half):
        count = self.chunks[c].shape[1] // 2
        return pl.ds(half * count, count)

    def own(self, c):
        rows = self.part_rows(self.place.dp)
        return pltpu.make_async_copy(self.shards[c], self.chunks[c].at[rows], self.own_sem.at[c])

    def along_z(self, c):
        place, rows = self.place, self.part_rows(self.place.dp)
        return [
            send(self.shards[c], self.chunks[c].at[rows], self.z_sems, (c, step - 1), place.row_mate(step))
            for step in range(1, place.row_size)
        ]

    def turned_z(self, c):
        place, found = self.place, []
        for step in range(1, place.row_size):
            for half, dp in ((0, place.x_dp), (1, place.y_dp)):
                at = self.chunks[c].at[self.part_rows(dp), self.half_cols(c, half)]
                found.append(send(at, at, self.turned_sems, (c, 2 * step - 2 + half), place.row_mate(step)))
        return found

    def second(self, c):
        place, chunk, found = self.place, self.chunks[c], []
        for half, mate in ((0, place.x_mate()), (1, place.y_mate())):
            if c in self.turned:
                cols = self.half_cols(c, half)
                source, target = self.shards[c].at[:, cols], chunk.at[self.part_rows(place.dp), cols]
            else:
                source = target = chunk.at[self.half_rows(place.dp, half)]
            found.append(send(source, target, self.two_sems, (c, half), mate))
        return found

    def third(self, c):
        place, chunk, found = self.place, self.chunks[c], []
        for index, (dp, half, mate) in enumerate(
            (
                (place.dp, 0, place.y_mate()),
                (place.dp, 1, place.x_mate()),
                (place.x_dp, 0, place.y_mate()),
                (place.y_dp, 1, place.x_mate()),
            )
        ):
            if c in self.turned:
                at = chunk.at[self.block_rows(dp), self.half_cols(c, half)]
            else:
                at = chunk.at[self.half_rows(dp, half)]
            found.append(send(at, at, self.three_sems, (c, index), mate))
        return found

    def step(self):
        stage, c = self.steps[self.done]
        self.done += 1
        if stage < 0:
            self.own(c).start()
            for copy in self.along_z(c) + (self.second(c) if c in self.turned else []):
                copy.start()
        elif stage == 0 and c in self.turned:
            for copy in self.second(c):
                copy.wait_recv()
            for copy in self.turned_z(c):
                copy.start()
        elif stage == 0:
            self.own(c).wait()
            for copy in self.along_z(c):
                copy.wait_recv()
            for copy in self.second(c):
                copy.start()
        elif stage == 1:
            if c in self.turned:
                self.own(c).wait()
                waits = self.along_z(c) + self.turned_z(c)
            else:
                waits = self.second(c)
            for copy in waits:
                copy.wait_recv()
            for copy in self.third(c):
                copy.start()
        else:
            for copy in self.third(c):
                copy.wait_recv()

    def begin(self):
        while self.steps[self.done][0] < 0:
            self.step()

    def advance(self, count):
        for _ in range(count):
            if self.done < len(self.steps):
                self.step()

    def need(self, c):
        while self.done <= self.steps.index((2, c)):
            self.step()

    def finish(self):
        self.advance(len(self.steps))
        for c in range(len(self.chunks)):
            for copy in self.along_z(c) + self.second(c) + self.third(c):
                copy.wait_send()
            for copy in self.turned_z(c) if c in self.turned else []:
                copy.wait_send()


class Scatter:
    def __init__(
        self, place, chunks, outs, turned, order, first, mid_send, mid, last_send, last, one_sems, two_sems, z_sems
    ):
        self.place, self.chunks, self.outs, self.turned = place, chunks, outs, turned
        self.first, self.mid_send, self.mid, self.last_send, self.last = first, mid_send, mid, last_send, last
        self.one_sems, self.two_sems, self.z_sems = one_sems, two_sems, z_sems
        self.part = outs[0].shape[0]
        self.block = self.part * place.row_size
        self.half = self.block // 2
        self.count = len(chunks)
        self.steps, self.done, self.begun = order, 0, []

    def block_rows(self, dp):
        return pl.ds(pl.multiple_of(dp * self.block, 16), self.block)

    def half_rows(self, dp, half):
        return pl.ds(pl.multiple_of(dp * self.block + half * self.half, 16), self.half)

    def z_rows(self, z):
        return pl.ds(pl.multiple_of(z * self.part, 16), self.part)

    def half_cols(self, c, half):
        count = self.chunks[c].shape[1] // 2
        return pl.ds(half * count, count)

    def one(self, c):
        place, chunk, first = self.place, self.chunks[c], self.first[c]
        found = []
        for i in range(2):
            for half, dp, mate in (
                (0, (1 - place.y) * 2 + i, place.y_mate()),
                (1, i * 2 + (1 - place.x), place.x_mate()),
            ):
                if c in self.turned:
                    at = chunk.at[self.block_rows(dp), self.half_cols(c, half)]
                else:
                    at = chunk.at[self.half_rows(dp, half)]
                found.append(send(at, first.at[half, i], self.one_sems, (c, 2 * half + i), mate))
        return found

    def two(self, c):
        place = self.place
        source, target = (self.last_send[c], self.last[c]) if c in self.turned else (self.mid_send[c], self.mid[c])
        return [
            send(source.at[0], target.at[0], self.two_sems, (c, 0), place.x_mate()),
            send(source.at[1], target.at[1], self.two_sems, (c, 1), place.y_mate()),
        ]

    def along_z(self, c):
        place, found = self.place, []
        for step in range(1, place.row_size):
            rows = self.z_rows(lax.rem(place.row + step, place.row_size))
            if c in self.turned:
                source, target = self.mid_send[c].at[:, rows], self.mid[c].at[step - 1]
            else:
                source, target = self.last_send[c].at[rows], self.last[c].at[step - 1]
            found.append(send(source, target, self.z_sems, (c, step - 1), place.row_mate(step)))
        return found

    def begin(self, c):
        self.begun.append(c)
        for copy in self.one(c):
            copy.start()

    def step(self):
        stage, c = self.steps[self.done]
        self.done += 1
        if c in self.turned:
            self.turned_step(stage, c)
        else:
            self.plain_step(stage, c)
        if stage == 2:
            self.put(c).start()

    def put(self, c):
        return pltpu.make_async_copy(self.outs[c], self.results[c], self.put_sem.at[c])

    def plain_step(self, stage, c):
        place, chunk = self.place, self.chunks[c]
        first, mid_send, mid = self.first[c], self.mid_send[c], self.mid[c]
        last_send, last = self.last_send[c], self.last[c]
        if stage == 0:
            for copy in self.one(c):
                copy.wait_recv()
            mid_send[0] = (
                chunk[self.half_rows(place.x_dp, 0), :].astype(wide) + first[0, 1 - place.x].astype(wide)
            ).astype(low_type)
            mid_send[1] = (
                chunk[self.half_rows(place.y_dp, 1), :].astype(wide) + first[1, 1 - place.y].astype(wide)
            ).astype(low_type)
            for copy in self.two(c):
                copy.start()
        elif stage == 1:
            for copy in self.two(c):
                copy.wait_recv()
            for half, slot in ((0, place.x), (1, place.y)):
                last_send[pl.ds(half * self.half, self.half), :] = (
                    chunk[self.half_rows(place.dp, half), :].astype(wide)
                    + first[half, slot].astype(wide)
                    + mid[half].astype(wide)
                ).astype(low_type)
            for copy in self.along_z(c):
                copy.start()
        else:
            total = last_send[self.z_rows(place.row), :].astype(wide)
            for step, copy in enumerate(self.along_z(c)):
                copy.wait_recv()
                total = total + last[step].astype(wide)
            self.outs[c][...] = total

    def turned_step(self, stage, c):
        place, chunk, out = self.place, self.chunks[c], self.outs[c]
        first, mid_send, mid = self.first[c], self.mid_send[c], self.mid[c]
        last_send, last = self.last_send[c], self.last[c]
        if stage == 0:
            for copy in self.one(c):
                copy.wait_recv()
            for half in range(2):
                for i in range(2):
                    dp = place.y * 2 + i if half == 0 else i * 2 + place.x
                    mine = chunk[self.block_rows(dp), self.half_cols(c, half)].astype(wide)
                    mid_send[2 * half + i] = (mine + first[half, i].astype(wide)).astype(low_type)
            for copy in self.along_z(c):
                copy.start()
        elif stage == 1:
            for copy in self.along_z(c):
                copy.wait_recv()
            for half, slot in ((0, place.x), (1, place.y)):
                for index, keep in ((slot, True), (1 - slot, False)):
                    total = mid_send[2 * half + index, self.z_rows(place.row), :].astype(wide)
                    for step in range(place.row_size - 1):
                        total = total + mid[step, 2 * half + index].astype(wide)
                    if keep:
                        out[:, self.half_cols(c, half)] = total
                    else:
                        last_send[half] = total.astype(low_type)
            for copy in self.two(c):
                copy.start()
        else:
            for half, copy in enumerate(self.two(c)):
                copy.wait_recv()
                out[:, self.half_cols(c, half)] += last[half].astype(wide)

    def advance(self, count):
        for _ in range(count):
            if self.done < len(self.steps) and self.steps[self.done][1] in self.begun:
                self.step()

    def finish(self):
        self.advance(len(self.steps))
        for c in range(self.count):
            for copy in self.one(c) + self.two(c) + self.along_z(c):
                copy.wait_send()
            self.put(c).wait()


def masked_tile(tile, query_start, key_start, prefix):
    key_index = key_start + lax.broadcasted_iota(jnp.int32, tile.shape, 0)
    query_index = query_start + lax.broadcasted_iota(jnp.int32, tile.shape, 1)
    return jnp.where((key_index < prefix) | (key_index <= query_index), tile, masked_value)


def key_tiles(block, rows, prefix_most):
    count = max((block + 1) * rows, prefix_most) // rows
    return [(tile, tile >= block) for tile in range(count)]


def flat_row(ref):
    return ref[...].reshape(1, ref.shape[0])


def gate_row(gates, heads, size):
    head = lax.broadcasted_iota(jnp.int32, (1, heads * size), 1) // size
    row = jnp.zeros((1, heads * size), wide)
    for h in range(heads):
        row = jnp.where(head == h, gates[h].astype(wide), row)
    return row


def layer_kernel(
    cut,
    token_part, cot_part, qkv_w, out_w, up_w, down_w, query_bias, value_bias, out_bias, up_bias, down_bias,
    first_gain, first_shift, second_gain, second_shift, hidden_gate, unit_gate,
    head_gate, attention_gate, feedforward_gate, prefix_length,
    layer_out, token_out, small_out, *rest,
):
    length, width, heads, size = cut.length, cut.width, cut.heads, cut.size
    part, rows, fine = cut.part_width, cut.rows, cut.fine
    blocks = length // rows
    own_count = blocks // 2
    pair = 2 * size
    pairs = heads // 2
    count = pairs + 5
    rest = list(rest)

    def take(number):
        taken = rest[:number]
        del rest[:number]
        return taken

    results = take(count)
    (wa, wm, token, token_t, qkv, lse, ctx, attn_out, normed_t, gelu, slope, second, low, dense_t, sums) = take(15)
    (cot, total, arrive_a, arrive_b, stage, token_recv, ctx_grad, key_grad, value_grad) = take(9)
    (pair_wide, pair_low, key_t, shards_a, shards_m) = take(5)
    grads = take(count)
    (small, small_c, small_x, small_y, small_z, unit_sums, head_sums) = take(7)
    buffers, first, mid_send, mid, last_send, last = (take(count) for _ in range(6))
    (own_sem, gz_s, gz_r, g2_s, g2_r, g3_s, g3_r, gt_s, gt_r, half_sem, out_sem) = take(11)
    (s1_s, s1_r, s2_s, s2_r, sz_s, sz_r) = take(6)
    (col_s, col_r, small_s, small_r, put_sem) = take(5)
    group = wm.shape[2]
    place = Place(cut.row_size)
    for p in range(pairs):
        for k in range(3):
            shards_a[p, :, k * pair : (k + 1) * pair] = qkv_w[k, :, p * pair : (p + 1) * pair].astype(low_type)
    shards_a[pairs] = out_w[...].astype(low_type)
    for j in range(2):
        shards_m[2 * j] = up_w[:, j * group : (j + 1) * group].astype(low_type)
        shards_m[2 * j + 1] = down_w[:, j * group : (j + 1) * group].astype(low_type)
    place.barrier()
    prefix = prefix_length[0]
    attn_gate, dense_gate = attention_gate[0].astype(wide), feedforward_gate[0].astype(wide)
    hidden, unit_row = flat_row(hidden_gate).astype(wide), flat_row(unit_gate).astype(wide)
    query_bias, value_bias, up_bias, out_bias, down_bias, first_gain, first_shift, second_gain, second_shift = (
        flat_row(ref)
        for ref in (
            query_bias, value_bias, up_bias, out_bias, down_bias, first_gain, first_shift, second_gain, second_shift
        )
    )
    chunks = [wa.at[i] for i in range(pairs + 1)] + [wm.at[i] for i in range(4)]
    shards = [shards_a.at[i] for i in range(pairs + 1)] + [shards_m.at[i] for i in range(4)]
    gather = Gather(
        place, shards, chunks, gather_turned, gather_order, own_sem, (gz_s, gz_r), (g2_s, g2_r), (g3_s, g3_r),
        (gt_s, gt_r),
    )
    scatter = Scatter(
        place, buffers, grads, scatter_turned, scatter_order, first, mid_send, mid, last_send, last,
        (s1_s, s1_r), (s2_s, s2_r), (sz_s, sz_r),
    )
    scatter.results, scatter.put_sem = results, put_sem

    def to_mate(source, target, index):
        return send(source, target, (col_s, col_r), index, place.col_mate())

    def own_block(i):
        return rows_at(place.col * own_count + i, rows)

    def mate_block(i):
        return rows_at((1 - place.col) * own_count + i, rows)

    def near(i):
        return pl.ds(i * rows, rows) if isinstance(i, int) else rows_at(i, rows)

    def mate_first(t):
        return lax.rem((1 - place.col) * own_count + t, blocks)

    own_cols = pl.ds(pl.multiple_of(place.col * part, 128), part)
    own_half = pl.ds(pl.multiple_of(place.col * (length // 2), rows), length // 2)
    mate_half = pl.ds(pl.multiple_of((1 - place.col) * (length // 2), rows), length // 2)
    token_own = pltpu.make_async_copy(token_part, token.at[:, own_cols], half_sem.at[0])
    token_sent = to_mate(token_part, token.at[:, own_cols], 0)
    cot_own = pltpu.make_async_copy(cot_part.at[own_half], cot.at[:, own_cols], half_sem.at[1])
    cot_sent = to_mate(cot_part.at[mate_half], cot.at[:, own_cols], 1)

    def attn_swap(i):
        return to_mate(total.at[mate_block(i)], arrive_a.at[near(i)], 2 + i)

    def normed_swap(i):
        return to_mate(low.at[own_block(i)], low.at[own_block(i)], 2 + own_count + i)

    def dense_swap(i):
        return to_mate(total.at[mate_block(i)], arrive_b.at[near(i)], 2 + 2 * own_count + i)

    def grad_swap(i):
        return to_mate(low.at[own_block(i)], low.at[own_block(i)], 2 + 3 * own_count + i)

    def hidden_swap(i):
        return to_mate(total.at[mate_block(i)], arrive_a.at[near(i)], 2 + 4 * own_count + i)

    def attn_grad_swap(i):
        return to_mate(low.at[own_block(i)], low.at[own_block(i)], 2 + 5 * own_count + i)

    def layer_swap(i):
        return to_mate(stage.at[1, near(i)], layer_out.at[own_block(i)], 2 + 6 * own_count + i)

    def token_swap(b):
        return to_mate(total.at[near(b), pl.ds(0, part)], token_recv.at[near(b)], 2 + 7 * own_count + b)

    small_swap = 2 + 7 * own_count + blocks

    def layer_put(i):
        return pltpu.make_async_copy(stage.at[0, near(i)], layer_out.at[own_block(i)], out_sem.at[i])

    gather.begin()
    for copy in (token_own, token_sent, cot_own, cot_sent):
        copy.start()
    sums[...] = jnp.zeros_like(sums)
    unit_sums[...] = jnp.zeros_like(unit_sums)
    head_sums[...] = jnp.zeros_like(head_sums)
    token_own.wait()
    token_sent.wait_recv()

    @pl.loop(0, blocks)
    def _(b):
        at = rows_at(b, rows)
        token_t[:, at] = token[at, :].T

    value_t, ctx_t = pair_low, pair_wide
    lane_head = lax.broadcasted_iota(jnp.int32, (1, pair), 1) // size
    for p in range(pairs):
        gather.need(p)
        query_row = query_bias[:, p * pair : (p + 1) * pair]
        bias = jnp.concatenate(
            [query_row, jnp.zeros_like(query_row), value_bias[:, p * pair : (p + 1) * pair]], axis=1
        )

        @pl.loop(0, blocks)
        def _(b, p=p, bias=bias):
            at = rows_at(b, rows)
            made = dot_nn(token[at, :], wa[p]) + bias
            qkv[p, at, :] = made.astype(low_type)
            value_t[:, at] = made[:, 2 * pair :].T.astype(low_type)
            key_t[p, :, at] = made[:, pair : 2 * pair].T.astype(low_type)

        pace = gather_pace[min(p, len(gather_pace) - 2)]
        gather.advance(pace[0])

        @pl.loop(0, 2)
        def _(h, p=p, pace=pace):
            own = jnp.where(lane_head == h, size ** (-0.5), 0.0).astype(low_type)
            head_rows = rows_at(h, size)
            for b in range(blocks):
                query = qkv[p, b * rows : (b + 1) * rows, :pair] * own
                tiles, masked = [], key_tiles(b, rows, cut.prefix_most)
                for tile, needs in masked:
                    score = dot_nt(qkv[p, tile * rows : (tile + 1) * rows, pair : 2 * pair], query)
                    tiles.append(masked_tile(score, b * rows, tile * rows, prefix) if needs else score)
                peak = tiles[0].max(axis=0, keepdims=True)
                for score in tiles[1:]:
                    peak = jnp.maximum(peak, score.max(axis=0, keepdims=True))
                row_total = jnp.zeros_like(peak)
                weights = []
                for score in tiles:
                    weights.append(jnp.exp(score - peak))
                    row_total = row_total + weights[-1].sum(axis=0, keepdims=True)
                share = 1.0 / row_total
                found = jnp.zeros((size, rows), wide)
                for (tile, _), weight in zip(masked, weights):
                    found = found + dot_nn(
                        value_t[head_rows, tile * rows : (tile + 1) * rows], (weight * share).astype(low_type)
                    )
                ctx_t[head_rows, b * rows : (b + 1) * rows] = found
                lse[2 * p + h, :, b * rows : (b + 1) * rows] = peak + jnp.log(row_total)
                for now in range(2):
                    if b % 2 and pace[1 + 2 * now + b // 2]:

                        @pl.when(h == now)
                        def _():
                            gather.advance(pace[1 + 2 * now + b // 2])

        @pl.loop(0, blocks)
        def _(b, p=p):
            at = rows_at(b, rows)
            ctx[at, p * pair : (p + 1) * pair] = ctx_t[:, at].T.astype(low_type)

    gather.need(pairs)
    gate_columns = gate_row(head_gate, heads, size)
    gate_low = gate_columns.astype(low_type)

    @pl.loop(0, blocks)
    def _(t):
        at = rows_at(mate_first(t), rows)
        total[at, :] = dot_nt(ctx[at, :] * gate_low, wa[pairs])

        @pl.when(t < own_count)
        def _():
            attn_swap(t).start()

    gather.advance(gather_pace[-1][0])
    gate_cols = attn_gate * hidden
    for i in range(own_count):
        attn_swap(i).wait_recv()

        @pl.loop(i * rows // fine, (i + 1) * rows // fine)
        def _(k):
            here = rows_at(k, fine)
            at = pl.ds(pl.multiple_of(place.col * (length // 2) + k * fine, fine), fine)
            attn = total[at, :] + arrive_a[here, :] + out_bias
            attn_out[here, :] = attn
            normed, _ = norm_parts(token[at, :].astype(wide) + gate_cols * attn)
            out = normed * first_gain + first_shift
            second[here, :] = out
            low[at, :] = out.astype(low_type)

        normed_swap(i).start()
    gather.advance(gather_pace[-1][1])

    masks = [unit_row[:, j * group : (j + 1) * group] for j in range(2)]
    for j in range(2):
        gather.need(pairs + 1 + 2 * j)
        bias_row = up_bias[:, j * group : (j + 1) * group]

        @pl.loop(0, blocks)
        def _(t, j=j, bias_row=bias_row):
            at = rows_at(lax.rem(place.col * own_count + t, blocks), rows)
            if j == 0:

                @pl.when(t == own_count)
                def _():
                    for i in range(own_count):
                        normed_swap(i).wait_recv()

            pre = dot_nn(low[at, :], wm[2 * j]) + bias_row
            share = 0.5 * (1.0 + lax.erf(pre * (2.0 ** -0.5)))
            gelu[j, at, :] = (pre * share).astype(low_type)
            density = jnp.exp(-0.5 * pre * pre) * ((2.0 * math.pi) ** -0.5)
            slope[j, at, :] = (share + pre * density).astype(low_type)
            if j == 0:
                normed_t[:, at] = low[at, :].T

        if j == 0:
            for i in range(own_count):
                attn_swap(i).wait_send()
                normed_swap(i).wait_send()
        gather.need(pairs + 2 + 2 * j)

        @pl.loop(0, blocks)
        def _(t, j=j):
            at = rows_at(mate_first(t), rows)
            made = dot_nt(gelu[j, at, :] * masks[j].astype(low_type), wm[2 * j + 1])
            if j == 0:
                total[at, :] = made
            else:
                total[at, :] += made

                @pl.when(t < own_count)
                def _():
                    dense_swap(t).start()

    cot_own.wait()
    cot_sent.wait_recv()
    for i in range(own_count):
        dense_swap(i).wait_recv()

        @pl.loop(i * rows // fine, (i + 1) * rows // fine)
        def _(k):
            here = rows_at(k, fine)
            at = pl.ds(pl.multiple_of(place.col * (length // 2) + k * fine, fine), fine)
            dense = total[at, :] + arrive_b[here, :] + down_bias
            normed, inverse = norm_parts(second[here, :] + dense_gate * hidden * dense)
            full = normed * second_gain + second_shift
            stage[0, here, :] = jnp.where(place.col == 0, full[:, :part], full[:, part:])
            stage[1, here, :] = jnp.where(place.col == 0, full[:, part:], full[:, :part])
            grad = cot[here, :].astype(wide)
            scaled = grad * second_gain
            one = jnp.mean(scaled, axis=1, keepdims=True)
            two = jnp.mean(scaled * normed, axis=1, keepdims=True)
            made = inverse * (scaled - one - normed * two)
            second[here, :] = made
            gated = (dense_gate * hidden * made).astype(low_type)
            low[at, :] = gated
            sums[0] += fold_rows(grad * normed)
            sums[1] += fold_rows(grad)
            sums[2] += fold_rows(gated.astype(wide))
            sums[3] += fold_rows(dense * made)

        grad_swap(i).start()
        dense_t[:, own_block(i)] = low[own_block(i), :].T
    for i in range(own_count):
        layer_swap(i).start()
        layer_put(i).start()
        grad_swap(i).wait_recv()
        dense_t[:, mate_block(i)] = low[mate_block(i), :].T

    def product(target, left, right, mask=None):
        @pl.loop(0, width // rows)
        def _(i):
            at = rows_at(i, rows)
            made = dot_nn(left[at, :], right[...])
            target[at, :] = (made if mask is None else made * mask).astype(low_type)

    for j in range(2):
        product(buffers[j], dense_t, gelu.at[j], masks[j])
        scatter.begin(j)
    for i in range(own_count):
        dense_swap(i).wait_send()
    for j in range(2):

        @pl.loop(0, blocks)
        def _(t, j=j):
            at = rows_at(mate_first(t), rows)
            inner = dot_nn(low[at, :], wm[2 * j + 1]).astype(low_type).astype(wide)
            unit_sums[2 + j] += fold_rows(gelu[j, at, :].astype(wide) * inner)
            pre = (masks[j] * inner * slope[j, at, :].astype(wide)).astype(low_type)
            slope[j, at, :] = pre
            unit_sums[j] += fold_rows(pre.astype(wide))
            made = dot_nt(pre, wm[2 * j])
            if j == 0:
                total[at, :] = made
            else:
                total[at, :] += made

                @pl.when(t < own_count)
                def _():
                    hidden_swap(t).start()

        scatter.advance(scatter_pace[0][j])
        product(buffers[2 + j], normed_t, slope.at[j])
        scatter.begin(2 + j)

    for i in range(own_count):
        grad_swap(i).wait_send()
    for i in range(own_count):
        hidden_swap(i).wait_recv()

        @pl.loop(i * rows // fine, (i + 1) * rows // fine)
        def _(k):
            here = rows_at(k, fine)
            at = pl.ds(pl.multiple_of(place.col * (length // 2) + k * fine, fine), fine)
            attn = attn_out[here, :]
            normed, inverse = norm_parts(token[at, :].astype(wide) + gate_cols * attn)
            grad = second[here, :] + (total[at, :] + arrive_a[here, :])
            scaled = grad * first_gain
            one = jnp.mean(scaled, axis=1, keepdims=True)
            two = jnp.mean(scaled * normed, axis=1, keepdims=True)
            made = inverse * (scaled - one - normed * two)
            second[here, :] = made
            gated = (gate_cols * made).astype(low_type)
            low[at, :] = gated
            sums[4] += fold_rows(grad * normed)
            sums[5] += fold_rows(grad)
            sums[6] += fold_rows(gated.astype(wide))
            sums[7] += fold_rows(attn * made)

        attn_grad_swap(i).start()
        dense_t[:, own_block(i)] = low[own_block(i), :].T
        scatter.advance(scatter_pace[1][i])
    for i in range(own_count):
        attn_grad_swap(i).wait_recv()
        dense_t[:, mate_block(i)] = low[mate_block(i), :].T

    @pl.loop(0, blocks)
    def _(b):
        at = rows_at(b, rows)
        gated = dot_nn(low[at, :], wa[pairs]).astype(low_type).astype(wide)
        seen = ctx[at, :].astype(wide)
        head_sums[...] += fold_rows(seen * gated)
        ctx_grad[at, :] = (gated * gate_columns).astype(low_type)
        ctx[at, :] = (seen * gate_columns).astype(low_type)

    product(buffers[4], dense_t, ctx)
    scatter.begin(4)
    scatter.advance(scatter_pace[2][0])
    for i in range(own_count):
        hidden_swap(i).wait_send()
        layer_put(i).wait()
        layer_swap(i).wait()
    query_t = pair_wide
    bias_sums = []
    for p in range(pairs):

        key_grad[...] = jnp.zeros_like(key_grad)
        value_grad[...] = jnp.zeros_like(value_grad)
        pace = scatter_pace[3 + min(p, len(scatter_pace) - 4)]

        @pl.loop(0, 2)
        def _(h, p=p, pace=pace):
            own = jnp.where(lane_head == h, size ** (-0.5), 0.0).astype(low_type)
            one_head = jnp.where(lane_head == h, 1.0, 0.0).astype(low_type)
            head_rows = rows_at(h, size)
            for b in range(blocks):
                query = qkv[p, b * rows : (b + 1) * rows, :pair] * own
                context = ctx_grad[b * rows : (b + 1) * rows, p * pair : (p + 1) * pair] * one_head
                logs = lse[2 * p + h, :, b * rows : (b + 1) * rows]
                inner = jnp.zeros_like(logs)
                kept, masked = [], key_tiles(b, rows, cut.prefix_most)
                for tile, needs in masked:
                    score = dot_nt(qkv[p, tile * rows : (tile + 1) * rows, pair : 2 * pair], query)
                    score = masked_tile(score, b * rows, tile * rows, prefix) if needs else score
                    prob = jnp.exp(score - logs)
                    grad_prob = dot_nt(qkv[p, tile * rows : (tile + 1) * rows, 2 * pair :], context)
                    inner = inner + (prob * grad_prob).sum(axis=0, keepdims=True)
                    kept.append((prob, grad_prob))
                found = jnp.zeros((size, rows), wide)
                for (tile, _), (prob, grad_prob) in zip(masked, kept):
                    at = slice(tile * rows, (tile + 1) * rows)
                    grad_score = (prob * (grad_prob - inner)).astype(low_type)
                    value_grad[at, :] += dot_nn(prob.astype(low_type), context)
                    key_grad[at, :] += dot_nn(grad_score, query)
                    found = found + dot_nn(key_t[p, head_rows, at], grad_score)
                query_t[head_rows, b * rows : (b + 1) * rows] = found * size ** (-0.5)
                for now in range(2):
                    if b % 2 and pace[2 * now + b // 2]:

                        @pl.when(h == now)
                        def _():
                            scatter.advance(pace[2 * now + b // 2])

        query_sum = jnp.zeros((8, pair), wide)
        value_sum = jnp.zeros((8, pair), wide)
        for b in range(blocks):
            at = pl.ds(b * rows, rows)
            query_low = query_t[:, at].T.astype(low_type)
            value_low = value_grad[at, :].astype(low_type)
            qkv[p, at, :pair] = query_low
            qkv[p, at, pair : 2 * pair] = key_grad[at, :].astype(low_type)
            qkv[p, at, 2 * pair :] = value_low
            query_sum += fold_rows(query_low.astype(wide))
            value_sum += fold_rows(value_low.astype(wide))
        bias_sums.append((query_sum, value_sum))
        product(buffers[5 + p], token_t, qkv.at[p])
        scatter.begin(5 + p)
        scatter.advance(pace[4])

    @pl.loop(0, blocks)
    def _(t):
        b = mate_first(t)
        at = rows_at(b, rows)
        made = dot_nt(qkv[0, at, :], wa[0])
        for p in range(1, pairs):
            made = made + dot_nt(qkv[p, at, :], wa[p])
        kept = second[rows_at(lax.rem(t, own_count), rows), :]
        made = made + jnp.where(t >= own_count, kept, 0.0)
        total[at, :part] = jnp.where(place.col == 0, made[:, part:], made[:, :part])
        total[at, part:] = jnp.where(place.col == 0, made[:, :part], made[:, part:])
        token_swap(b).start()

    def whole(values):
        return jnp.sum(values, axis=0, keepdims=True)

    dense_col, attn_col = whole(sums[3]), whole(sums[7])
    seq_lane = lax.broadcasted_iota(jnp.int32, (1, width), 1)
    here = place.dp * place.row_size + place.row
    dense_all = jnp.sum(dense_col * hidden, axis=1, keepdims=True)
    attn_all = jnp.sum(attn_col * hidden, axis=1, keepdims=True)
    seq_row = jnp.where(seq_lane == here, attn_all, 0.0) + jnp.where(seq_lane == here + width // 2, dense_all, 0.0)
    small[0:1, :] = whole(sums[6])
    small[1:2, :] = whole(sums[2])
    small[2:3, :] = whole(sums[4])
    small[3:4, :] = whole(sums[5])
    small[4:5, :] = whole(sums[0])
    small[5:6, :] = whole(sums[1])
    small[6:7, :] = dense_gate * dense_col + attn_gate * attn_col
    small[7:8, :] = seq_row
    for j in range(4):
        small[8 + j : 9 + j, :] = whole(unit_sums[j])
    for p in range(pairs):
        small[12:13, p * pair : (p + 1) * pair] = whole(bias_sums[p][0])
        small[12:13, part + p * pair : part + (p + 1) * pair] = whole(bias_sums[p][1])
    small[13:14, :part] = whole(head_sums[...])
    small[13:14, part:] = jnp.zeros((1, part), wide)
    small[14:16, :] = jnp.zeros((2, width), wide)
    copy_c = to_mate(small.at[pl.ds(0, 8)], small_c.at[0, pl.ds(0, 8)], small_swap)
    copy_c.start()
    copy_c.wait_recv()
    small_c[1, 0:8, :] = small[0:8, :] + small_c[0, 0:8, :]
    small_c[1, 8:16, :] = small[8:16, :]
    copy_x = send(small_c.at[1], small_x.at[0], (small_s, small_r), 0, place.x_mate())
    copy_x.start()
    scatter.advance(1)
    copy_x.wait_recv()
    small_x[1] = small_c[1] + small_x[0]
    copy_y = send(small_x.at[1], small_y.at[0], (small_s, small_r), 1, place.y_mate())
    copy_y.start()
    scatter.advance(1)
    copy_y.wait_recv()
    mine = small_x[1] + small_y[0]
    small_y[1] = mine
    small_z[place.row] = mine
    copies = [
        send(small_y.at[1], small_z.at[place.row], (small_s, small_r), 1 + step, place.row_mate(step))
        for step in range(1, cut.row_size)
    ]
    for copy in copies:
        copy.start()
    for b in range(blocks):
        token_swap(b).wait_recv()
        found = total[near(b), part:] + token_recv[near(b), :]
        stage[b // own_count, near(b % own_count), :] = found
        pltpu.make_async_copy(
            stage.at[b // own_count, near(b % own_count)], token_out.at[near(b)], out_sem.at[own_count + b]
        ).start()
    scatter.finish()
    for copy in copies:
        copy.wait_recv()
    result = small_z[0]
    for z in range(1, cut.row_size):
        result = result + small_z[z]
    small_out[...] = result
    gather.finish()
    for copy in [token_sent, cot_sent, copy_c, copy_x, copy_y] + copies:
        copy.wait_send()
    for i in range(own_count):
        attn_grad_swap(i).wait_send()
    for b in range(blocks):
        token_swap(b).wait_send()
        pltpu.make_async_copy(
            stage.at[b // own_count, near(b % own_count)], token_out.at[near(b)], out_sem.at[own_count + b]
        ).wait()


def place_kernel(cut, count, layer_in, token_in, *rest):
    pairs, pair, part, width = cut.heads // 2, 2 * cut.size, cut.part_width, cut.width
    sources, rest = rest[:count], rest[count:]
    (
        layer_out, token_out, grad_qkv, grad_out, grad_up, grad_down, query_bias, value_bias, out_bias, up_bias,
        down_bias, first_gain, first_shift, second_gain, second_shift, head, hidden, unit, attention, feedforward,
    ) = rest[:20]
    held, targets, (in_sem, out_sem, source_sem) = rest[20], rest[21 : 21 + count], rest[21 + count :]
    parts = held.shape[1]
    step = layer_in.shape[0] // parts
    moves = []
    for a, (source, target) in enumerate(((layer_in, layer_out), (token_in, token_out))):
        for i in range(parts):
            at = pl.ds(i * step, step)
            into = pltpu.make_async_copy(source.at[at], held.at[a, i], in_sem.at[a, i])
            into.start()
            moves.append((into, pltpu.make_async_copy(held.at[a, i], target.at[at], out_sem.at[a, i])))
    loads = [pltpu.make_async_copy(a, b, source_sem.at[i]) for i, (a, b) in enumerate(zip(sources, targets))]
    for copy in loads:
        copy.start()
    for into, out in moves:
        into.wait()
        out.start()
    for copy in loads:
        copy.wait()
    small, down_0, down_1, up_0, up_1, grad_out_t, *pieces = targets
    group = cut.units // 2
    for p in range(pairs):
        for k in range(3):
            grad_qkv[k, :, p * pair : (p + 1) * pair] = pieces[p][:, k * pair : (k + 1) * pair]
    grad_out[...] = grad_out_t[...]
    for j, (up, down) in enumerate(((up_0, down_0), (up_1, down_1))):
        grad_up[:, j * group : (j + 1) * group] = up[...]
        grad_down[:, j * group : (j + 1) * group] = down[...]

    def flat(target, values):
        target[...] = values.reshape(target.shape)

    flat(up_bias, jnp.concatenate([small[8:9, :], small[9:10, :]], axis=1))
    flat(unit, jnp.concatenate([small[10:11, :], small[11:12, :]], axis=1))
    flat(query_bias, small[12:13, :part])
    flat(value_bias, small[12:13, part:])
    for row, target in enumerate((out_bias, down_bias, first_gain, first_shift, second_gain, second_shift, hidden)):
        flat(target, small[row : row + 1, :])
    lane = lax.broadcasted_iota(jnp.int32, (1, part), 1) // cut.size
    slot = lax.broadcasted_iota(jnp.int32, (1, cut.heads), 1)
    found = jnp.zeros((1, cut.heads), wide)
    for h in range(cut.heads):
        one = jnp.sum(jnp.where(lane == h, small[13:14, :part], 0.0), axis=1, keepdims=True)
        found = jnp.where(slot == h, one, found)
    flat(head, found)
    seq_total = attention.shape[0]
    flat(attention, small[7:8, :seq_total])
    flat(feedforward, small[7:8, width // 2 : width // 2 + seq_total])
    for _, out in moves:
        out.wait()


gather_turned = (5, 7)
scatter_turned = (0,)
gather_order = ((-1, 0), (-1, 1), (0, 0), (-1, 2), (0, 1), (-1, 3), (1, 0), (0, 2), (-1, 4), (1, 1), (2, 0), (0, 3), (-1, 5), (1, 2), (2, 1), (0, 4), (-1, 6), (1, 3), (2, 2), (0, 5), (-1, 7), (1, 4), (2, 3), (0, 6), (1, 5), (2, 4), (0, 7), (1, 6), (2, 5), (1, 7), (2, 6), (2, 7))
scatter_order = ((0, 0), (0, 1), (0, 2), (1, 0), (1, 1), (0, 3), (0, 4), (1, 2), (0, 5), (2, 0), (1, 3), (1, 4), (0, 6), (1, 5), (0, 7), (1, 6), (2, 1), (1, 7), (2, 3), (2, 4), (2, 6), (2, 5), (2, 2), (2, 7))
gather_pace = ((3, 0, 0, 0, 3), (1, 3, 0, 0, 1), (0, 0, 1, 3, 2), (0, 2))
scatter_pace = ((0, 1), (0, 1), (0,), (1, 0, 0, 1, 1), (1, 1, 1, 1, 0), (1, 1, 1, 2, 0))


class Cut(NamedTuple):
    length: int
    width: int
    part_width: int
    heads: int
    size: int
    units: int
    part: int
    row_size: int
    rows: int
    fine: int
    prefix_most: int


def any_spec():
    return pl.BlockSpec(memory_space=pl.ANY)


def vmem_spec():
    return pl.BlockSpec(memory_space=pltpu.VMEM)


def smem_spec():
    return pl.BlockSpec(memory_space=pltpu.SMEM)


def like(items):
    return [jax.ShapeDtypeStruct(shape, kind) for shape, kind in items]


def scratch(items):
    return [pltpu.VMEM(shape, kind) for shape, kind in items]


def dma(*shape):
    return pltpu.SemaphoreType.DMA(shape)


vmem_most = 67043328


def run_layer(cut, *args):
    length, width, half = cut.length, cut.width, cut.part_width
    group = cut.units // 2
    pairs = cut.heads // 2
    blocks = length // cut.rows
    columns = [group] * 4 + [half] * (pairs + 1)
    count = len(columns)
    outs = [((length, half), wide), ((length, half), wide), ((16, width), wide)]
    outs += [((cut.part, n), wide) for n in columns]
    own = [
        ((pairs + 1, width, half), low_type),
        ((4, width, group), low_type),
        ((length, width), low_type),
        ((width, length), low_type),
        ((pairs, length, half), low_type),
        ((cut.heads, 1, length), wide),
        ((length, half), low_type),
        ((length // 2, width), wide),
        ((width, length), low_type),
        ((2, length, group), low_type),
        ((2, length, group), low_type),
        ((length // 2, width), wide),
        ((length, width), low_type),
        ((width, length), low_type),
        ((8, 8, width), wide),
        ((length // 2, width), low_type),
        ((length, width), wide),
        ((length // 2, width), wide),
        ((length // 2, width), wide),
        ((2, length // 2, half), wide),
        ((length, half), wide),
        ((length, half), low_type),
        ((length, 2 * cut.size), wide),
        ((length, 2 * cut.size), wide),
        ((2 * cut.size, length), wide),
        ((2 * cut.size, length), low_type),
        ((pairs, 2 * cut.size, length), low_type),
        ((pairs + 1, cut.part, half), low_type),
        ((4, cut.part, group), low_type),
        *[((cut.part, n), wide) for n in columns],
        ((16, width), wide),
        ((2, 16, width), wide),
        ((2, 16, width), wide),
        ((2, 16, width), wide),
        ((cut.row_size, 16, width), wide),
        ((4, 8, width), wide),
        ((8, half), wide),
    ]
    quarter = cut.part * cut.row_size // 2
    own += [((width, n), low_type) for n in columns]
    z = cut.row_size - 1
    turned = [c in scatter_turned for c in range(count)]
    both = list(zip(columns, turned))
    own += [((2, 2, 2 * quarter, n // 2) if turn else (2, 2, quarter, n), low_type) for n, turn in both]
    own += [((4, 2 * quarter, n // 2) if turn else (2, quarter, n), low_type) for n, turn in both]
    own += [((z, 4, cut.part, n // 2) if turn else (2, quarter, n), low_type) for n, turn in both]
    own += [((2, cut.part, n // 2) if turn else (2 * quarter, n), low_type) for n, turn in both]
    own += [((2, cut.part, n // 2) if turn else (z, cut.part, n), low_type) for n, turn in both]
    semaphores = [dma(count), dma(count, z), dma(count, z), dma(count, 2), dma(count, 2), dma(count, 4), dma(count, 4)]
    semaphores += [dma(count, 2 * z), dma(count, 2 * z), dma(2), dma(blocks // 2 + blocks)]
    semaphores += [dma(count, 4), dma(count, 4), dma(count, 2), dma(count, 2), dma(count, z), dma(count, z)]
    pair_swaps = 3 + 7 * (blocks // 2) + blocks
    semaphores += [dma(pair_swaps), dma(pair_swaps), dma(2 + z), dma(2 + z), dma(count)]
    return pl.pallas_call(
        partial(layer_kernel, cut),
        out_shape=like(outs),
        in_specs=[any_spec()] * 2 + [vmem_spec()] * (len(args) - 6) + [smem_spec()] * 4,
        out_specs=[any_spec()] * 2 + [vmem_spec()] + [any_spec()] * count,
        scratch_shapes=scratch(own) + semaphores,
        compiler_params=pltpu.CompilerParams(collective_id=0, has_side_effects=True, vmem_limit_bytes=vmem_most),
        name="whole_layer",
    )(*args)


def fused_device(
    cut,
    tokens, cotangent, qkv_weight, out_weight, up_weight, down_weight, query_bias, value_bias, out_bias, up_bias,
    down_bias, first_gain, first_shift, second_gain, second_shift, head_gate, hidden_gate, intermediate_gate,
    attention_gate, feedforward_gate, prefix_length,
):
    half, width, units, part = cut.part_width, cut.width, cut.units, cut.part
    rows = [
        query_bias, value_bias, out_bias, up_bias, down_bias, first_gain, first_shift, second_gain, second_shift,
        hidden_gate, intermediate_gate,
    ]
    scalars = [head_gate, attention_gate, feedforward_gate, prefix_length]
    weights = [qkv_weight, out_weight.T, up_weight, down_weight.T]
    made = run_layer(cut, tokens, cotangent, *weights, *rows, *scalars)
    seq_total = lax.axis_size(("dp", "row"))
    lanes = [half, half, width, units, width, width, width, width, width, cut.heads, width, units, seq_total, seq_total]
    shapes = [(3, part, half), (part, half), (part, units), (part, units)] + [(n,) for n in lanes]
    whole = (cut.length, half)
    held = [((2, 4, cut.length // 4, half), wide)] + [(piece.shape, piece.dtype) for piece in made[2:]]
    count = len(made) - 2
    layer_out, grad_tokens, *outs = pl.pallas_call(
        partial(place_kernel, cut, count),
        out_shape=like([(shape, wide) for shape in [whole, whole] + shapes]),
        in_specs=[any_spec()] * len(made),
        out_specs=[any_spec()] * 2 + [vmem_spec()] * len(shapes),
        scratch_shapes=scratch(held) + [dma(2, 4), dma(2, 4), dma(count)],
        name="place_results",
    )(*made)
    return (layer_out, grad_tokens, outs[0], outs[1].T, outs[2], outs[3].T, *outs[4:])


def cut_of(args):
    tokens, qkv_weight, up_weight, head_gate, prefix_length = args[0], args[2], args[4], args[15], args[20]
    length, part_width = tokens.shape
    part, width = qkv_weight.shape[1], args[11].shape[0]
    heads = head_gate.shape[0]
    row_size, dp_size = lax.axis_size("row"), lax.axis_size("dp")
    fits = (
        prefix_length.shape[0] == 1
        and lax.axis_size("col") == 2
        and dp_size == 4
        and row_size % 2 == 0
        and part % 16 == 0
        and heads % 2 == 0
        and part_width == qkv_weight.shape[2]
        and part_width == 3 * (2 * part_width // heads)
        and (2 * part_width // heads) % 128 == 0
        and width % 256 == 0
        and length % 512 == 0
        and up_weight.shape[1] == 2 * width
    )
    if not fits:
        return None
    return Cut(
        length, width, part_width, heads, part_width // heads, up_weight.shape[1], part, row_size, 256, 128, length // 2
    )


def any_device(*args):
    cut = cut_of(args)
    return per_device(*args) if cut is None else fused_device(cut, *args)


def solution(mesh):
    placed = (
        P(("dp", "row"), "col"),
        P(("dp", "row"), "col"),
        P(None, ("dp", "row"), "col"),
        P("col", ("dp", "row")),
        P(("dp", "row"), "col"),
        P("col", ("dp", "row")),
        P("col"),
        P("col"),
        P(),
        P("col"),
        P(),
        P(),
        P(),
        P(),
        P(),
        P("col"),
        P(),
        P("col"),
        P(("dp", "row")),
        P(("dp", "row")),
        P(("dp", "row")),
    )
    return jax.shard_map(
        any_device,
        mesh=mesh,
        in_specs=placed,
        out_specs=(
            P(("dp", "row"), "col"),
            P(("dp", "row"), "col"),
            P(None, ("dp", "row"), "col"),
            P("col", ("dp", "row")),
            P(("dp", "row"), "col"),
            P("col", ("dp", "row")),
            P("col"),
            P("col"),
            P(),
            P("col"),
            P(),
            P(),
            P(),
            P(),
            P(),
            P("col"),
            P(),
            P("col"),
            P(),
            P(),
        ),
        check_vma=False,
    )
```
